32 devices in a mesh: dp: 8 (over z, x), tensor: 4 (over y, core).
Axes of the slice: x: 2, y: 2, z: 4, core: 2. Of those that a mesh axis runs over, the one named last changes fastest.
Arguments:
- tokens: bfloat16 [8, 1024, 1024], P('dp'), may hold values from -6 to 6
- prefix: int32 [8], P('dp'), may hold values from 102 to 512, as said below
- norm_gain: float32 [1024], replicated, may hold values from 0.1 to 1.9
- in_weight: bfloat16 [1024, 2, 2048], P(None, None, 'tensor'), may hold values from -0.1875 to 0.1875
- conv_weight: float32 [4, 2048], P(None, 'tensor'), may hold values from -3 to 3
- conv_bias: float32 [2048], P('tensor'), may hold values from -0.5 to 0.5
- xproj_weight: bfloat16 [2048, 96], P('tensor'), may hold values from -0.125 to 0.125
- step_weight: bfloat16 [64, 2048], P(None, 'tensor'), may hold values from -0.75 to 0.75
- step_bias: float32 [2048], P('tensor'), may hold values from -6.5 to -2.5
- decay_log: float32 [16, 2048], P(None, 'tensor'), may hold values from -4 to 1.5
- skip_gain: float32 [2048], P('tensor'), may hold values from 0.5 to 1.5
- out_weight: bfloat16 [2048, 1024], P('tensor'), may hold values from -0.5 to 0.5
- out_cotangent: bfloat16 [8, 1024, 1024], P('dp'), may hold values from -18 to 18
Outputs:
- block_out: bfloat16 [8, 1024, 1024], P('dp')
- grad_tokens: float32 [8, 1024, 1024], P('dp')
- grad_norm_gain: float32 [1024], replicated
- grad_in_weight: float32 [1024, 2, 2048], P(None, None, 'tensor')
- grad_conv_weight: float32 [4, 2048], P(None, 'tensor')
- grad_conv_bias: float32 [2048], P('tensor')
- grad_xproj_weight: float32 [2048, 96], P('tensor')
- grad_step_weight: float32 [64, 2048], P(None, 'tensor')
- grad_step_bias: float32 [2048], P('tensor')
- grad_decay_log: float32 [16, 2048], P(None, 'tensor')
- grad_skip_gain: float32 [2048], P('tensor')
- grad_out_weight: float32 [2048, 1024], P('tensor')
The draws below stay inside these ranges and needn't reach their ends.
Inputs may be any that keep to these rules, and one draw needn't show every extreme that they name: prefix of each sequence; both bounds are reached in every draw.
All inputs are finite; a program needn't handle non-finite values.
Results may differ from the reference program's by a relative error of at most 0.011.
Values may be sent and summed in bfloat16 or wider, within the bound.
No kernel may reach another device: no remote copies, remote signals or barrier semaphores. Data moves between devices by JAX's collectives and lax.ppermute only.
A program may use at most 128 MiB of HBM per device.

```python
import jax
import jax.numpy as jnp
from jax import lax

D = 1024
DI = 2048
N = 16
R = 64
KW = 4
L = 1024
BLOCK = 64
SEQS = 8


def draw_prefix(key, part):
    lengths = jax.random.randint(key, (SEQS,), L // 10, L // 2 + 1, dtype=jnp.int32)
    lengths = lengths.at[0].set(L // 2)
    return lengths.at[SEQS - 1].set(L // 10)


def draw_out_cotangent(key, part):
    seq_scale = 3.0 ** (jnp.arange(SEQS, dtype=jnp.float32) / max(SEQS - 1, 1))
    values = jax.random.normal(key, (SEQS, L, D), jnp.float32) * seq_scale[:, None, None]
    return jnp.clip(values, -18.0, 18.0).astype(jnp.bfloat16)


def levels(rng, dims, cuts, least, top_value):
    loudness = 1.0
    for axis_at, parts in cuts:
        heights = jax.random.uniform(jax.random.fold_in(jax.random.fold_in(rng, 6), axis_at), (parts,), jnp.float32, least / len(cuts), top_value / len(cuts))
        loudness = loudness * jnp.repeat(jnp.exp(heights), dims[axis_at] // parts).reshape((-1,) + (1,) * (len(dims) - 1 - axis_at))
    return loudness


def gaussian(stream_key, shape, width, bound, cuts=(), kind=jnp.bfloat16):
    entries = width * jax.random.normal(stream_key, shape, jnp.float32)
    if cuts:
        entries = entries * levels(stream_key, shape, cuts, -0.22, 0.18)
    return jnp.clip(entries, -bound, bound).astype(kind)


def setup_inputs(seed: int = 0) -> dict:
    splits = jax.random.split(jax.random.key(seed), 14)
    tokens = gaussian(splits[0], (SEQS, L, D), 1.0, 6.0, ((0, 8),))
    prefix = draw_prefix(jax.random.fold_in(splits[13], 71), 0)
    norm_gain = jnp.clip(1.0 + 0.18 * jax.random.normal(splits[2], (D,), jnp.float32), 0.1, 1.9)
    in_weight = gaussian(splits[3], (D, 2, DI), D ** -0.5, 0.1875, ((2, 4),))
    conv_weight = gaussian(splits[4], (KW, DI), KW ** -0.5, 3.0, ((1, 4),), jnp.float32)
    conv_bias = jnp.clip(jax.random.uniform(splits[5], (DI,), jnp.float32, -0.5, 0.5) * levels(splits[5], (DI,), ((0, 4),), -0.4, 0.0), -0.5, 0.5)
    xproj_weight = gaussian(splits[6], (DI, R + 2 * N), DI ** -0.5, 0.125, ((0, 4),))
    step_weight = gaussian(splits[7], (R, DI), R ** -0.5, 0.75, ((1, 4),))
    step_bias = jnp.clip(-6.5 + 4.0 * jax.random.uniform(splits[8], (DI,), jnp.float32) ** levels(splits[8], (DI,), ((0, 4),), -0.2, 0.2), -6.5, -2.5)
    decay_log = jnp.clip(-4.0 + 5.5 * jax.random.uniform(splits[9], (N, DI), jnp.float32) ** levels(splits[9], (N, DI), ((1, 4),), -0.2, 0.2), -4.0, 1.5)
    skip_gain = jnp.clip(0.5 + 1.0 * jax.random.uniform(splits[10], (DI,), jnp.float32) ** levels(splits[10], (DI,), ((0, 4),), -0.2, 0.2), 0.5, 1.5)
    out_weight = gaussian(splits[11], (DI, D), (DI // 16) ** -0.5, 0.5, ((0, 4),))
    out_cotangent = draw_out_cotangent(jax.random.fold_in(splits[13], 71), 0)
    return dict(tokens=tokens, prefix=prefix, norm_gain=norm_gain, in_weight=in_weight, conv_weight=conv_weight, conv_bias=conv_bias, xproj_weight=xproj_weight, step_weight=step_weight, step_bias=step_bias, decay_log=decay_log, skip_gain=skip_gain, out_weight=out_weight, out_cotangent=out_cotangent)


@jax.custom_vjp
def low(v):
    return lax.optimization_barrier(v.astype(jnp.bfloat16)).astype(jnp.float32)

@jax.custom_vjp
def low_back(v):
    return v

def low_keep(v):
    return (low(v), None)

def low_pass(kept, grad):
    return (grad,)

def back_keep(v):
    return (v, None)

def back_low(kept, grad):
    return (low(grad),)
low.defvjp(low_keep, low_pass)
low_back.defvjp(back_keep, back_low)
epsilon = 1e-05

def normalize(values, gain_vec):
    return values * lax.rsqrt(lax.optimization_barrier(jnp.mean(values * values, axis=-1, keepdims=True)) + epsilon) * gain_vec

def convolve(signal, kernel, offset):
    kernel_width = kernel.shape[0]
    length = signal.shape[1]
    padded = jnp.pad(signal, ((0, 0), (kernel_width - 1, 0), (0, 0)))
    summed = jnp.zeros_like(signal) + offset
    for tap_index in range(kernel_width):
        summed = summed + kernel[tap_index] * padded[:, tap_index:tap_index + length]
    return summed

def selective(step_size, drive_in, bmatrix, cmatrix, decay_rate):
    seq_count, length, channels = step_size.shape
    block_count = length // BLOCK

    def blocked(values):
        shaped = values.reshape((seq_count, block_count, BLOCK) + values.shape[2:])
        return jnp.swapaxes(shaped, 0, 1)

    def advance(carry_state, pieces):
        piece_step, piece_drive, piece_bmat, piece_cmat = pieces
        factor = jnp.exp(piece_step[:, :, None, :] * decay_rate)
        source = (piece_step * piece_drive)[:, :, None, :] * piece_bmat[:, :, :, None]
        state = carry_state
        outputs = []
        for position in range(BLOCK):
            state = factor[:, position] * state + source[:, position]
            outputs.append(lax.optimization_barrier(jnp.sum(state * piece_cmat[:, position, :, None], axis=1)))
        return (state, jnp.stack(outputs, axis=1))
    initial = jnp.zeros((seq_count, decay_rate.shape[0], channels), jnp.float32)
    last_state, outputs = lax.scan(jax.checkpoint(advance), initial, (blocked(step_size), blocked(drive_in), blocked(bmatrix), blocked(cmatrix)))
    return jnp.swapaxes(outputs, 0, 1).reshape(seq_count, length, channels)

def mixer_core(pre_act, bmatrix, cmatrix, drive_in, gate_in, step_bias, decay_log, skip_gain, prefix_mask):
    step_size = jax.nn.softplus(pre_act + step_bias)
    decay_rate = -jnp.exp(decay_log)
    ahead_part = selective(step_size, drive_in, bmatrix, cmatrix, decay_rate)
    masked = prefix_mask[:, :, None]
    behind = jnp.flip(selective(jnp.flip(step_size, 1), jnp.flip(drive_in * masked, 1), jnp.flip(bmatrix, 1), jnp.flip(cmatrix, 1), decay_rate), 1)
    combined = ahead_part + behind * masked + skip_gain * drive_in
    return combined * jax.nn.silu(gate_in)

def forward_block(sequence, norm_gain, in_weight, conv_weight, conv_bias, xproj_weight, step_weight, step_bias, decay_log, skip_gain, out_weight, prefix_mask):
    highest = lax.Precision.HIGHEST
    normed = low(normalize(sequence, norm_gain))
    expanded = low_back(jnp.dot(normed, in_weight.reshape(D, 2 * DI), precision=highest))
    conv_input = expanded[:, :DI]
    gate_input = expanded[:, DI:]
    drive_in = low(jax.nn.silu(convolve(conv_input[None], conv_weight, conv_bias)))
    projected = low_back(low(jnp.dot(drive_in[0], xproj_weight, precision=highest)))
    pre_act = low_back(jnp.dot(projected[:, :R], step_weight, precision=highest))
    gated = low(mixer_core(pre_act[None], projected[None, :, R:R + N], projected[None, :, R + N:], drive_in, gate_input[None], step_bias, decay_log, skip_gain, prefix_mask[None]))
    return sequence + jnp.dot(gated[0], out_weight, precision=highest)

def reference(tokens, prefix, norm_gain, in_weight, conv_weight, conv_bias, xproj_weight, step_weight, step_bias, decay_log, skip_gain, out_weight, out_cotangent):
    params = (norm_gain.astype(jnp.float32), in_weight.astype(jnp.float32), conv_weight.astype(jnp.float32), conv_bias.astype(jnp.float32), xproj_weight.astype(jnp.float32), step_weight.astype(jnp.float32), step_bias.astype(jnp.float32), decay_log.astype(jnp.float32), skip_gain.astype(jnp.float32), out_weight.astype(jnp.float32))
    positions = jnp.arange(L, dtype=jnp.int32)

    def one_sequence(gradients, inputs):
        sequence, length_now, cotangent = inputs
        prefix_mask = (positions < length_now).astype(jnp.float32)

        def forward_fn(sequence_in, gain_in, in_w, conv_w, conv_b, xproj_w, step_w, step_b, decay_in, skip_in, out_w):
            return forward_block(sequence_in, gain_in, in_w, conv_w, conv_b, xproj_w, step_w, step_b, decay_in, skip_in, out_w, prefix_mask)
        result, backward = jax.vjp(forward_fn, sequence.astype(jnp.float32), *params)
        cotangents = backward(cotangent.astype(jnp.float32))
        gradients = tuple((total + term for total, term in zip(gradients, cotangents[1:])))
        return (gradients, (result.astype(jnp.bfloat16), cotangents[0]))
    zero_grads = tuple((jnp.zeros_like(value) for value in params))
    gradients, outputs = lax.scan(one_sequence, zero_grads, (tokens, prefix, out_cotangent))
    return (outputs[0], outputs[1], gradients[0], gradients[1], gradients[2], gradients[3], gradients[4], gradients[5], gradients[6], gradients[7], gradients[8], gradients[9])
```

```python
import functools

import jax
import jax.numpy as jnp
from jax import lax
from jax.experimental import pallas as pl
from jax.experimental.pallas import tpu as pltpu
from jax.sharding import PartitionSpec as P

T = 16
LC = 128
LOG2E = 1.4426950408889634
LN2 = 0.6931471805599453
F32 = jnp.float32
BF = jnp.bfloat16
NT = (((1,), (1,)), ((), ()))
STRIDED = True
epsilon = 1e-05


def iota(shape, d):
    return lax.broadcasted_iota(jnp.int32, shape, d)


def mm(a, b):
    return jnp.dot(a, b, preferred_element_type=F32)


def mm_nt(a, b):
    return lax.dot_general(a, b, NT, preferred_element_type=F32)


def row(ref, g, t, n):
    if STRIDED:
        pair = [ref[2 * g + j, pl.ds(t, 8, stride=0), :] for j in (0, 1)]
        wide = jnp.concatenate(pair, axis=1)
        return jnp.concatenate([wide] * (n // 8), axis=0)
    pair = [jnp.broadcast_to(ref[2 * g + j, pl.ds(t, 1), :], (n, 128)) for j in (0, 1)]
    return jnp.concatenate(pair, axis=1)


def spread(base, p, n):
    return (iota((p, T * n), 0) == base + lax.rem(iota((p, T * n), 1), n)).astype(BF)


def pick(base, p, n):
    return (iota((n, p), 1) == base + iota((n, p), 0)).astype(BF)


def fold(base, p, n):
    return (iota((T * n, p), 1) == base + lax.rem(iota((T * n, p), 0), n)).astype(BF)


def blockdiag(rows, n):
    return lax.rem(iota((rows, T * n), 0), T) == lax.div(iota((rows, T * n), 1), n)


def split(ref, value):
    for g in range(value.shape[1] // 128):
        ref[g] = value[:, g * 128 : (g + 1) * 128]


def softplus(x):
    e = jnp.exp2(jnp.abs(x) * -LOG2E)
    small = e * (1.0 - e * (0.5 - e * (1.0 / 3.0 - e * 0.25)))
    return jnp.maximum(x, 0.0) + jnp.where(e < 0.03125, small, jnp.log2(1.0 + e) * LN2)


def one_minus_exp(s):
    small = s * (1.0 - s * (0.5 - s * (1.0 / 6.0 - s * (1.0 / 24.0))))
    return jnp.where(s < 0.0625, small, 1.0 - jnp.exp2(s * -LOG2E))


def front_kernel(ng, prefix_ref, proj_ref, sw_ref, bias_ref, drive_ref, z_ref, dg_ref, dlog_ref, skip_ref,
                 gated_ref, dz_ref, step_ref, dy_ref, hprev_ref, ag_ref, wg_ref, part_ref, gskip_ref,
                 step_s, sd_s, dy_s, sig_s, keep_s, bt_s, ct_s, cbd_s, rc_s, hg_s, g_s, qg_s, st_f, st_h, st_q):
    lc, c = drive_ref.shape
    p = proj_ref.shape[1]
    n = dlog_ref.shape[0]
    r = p - 2 * n
    tn = T * n
    nb = lc // T
    groups = c // 256
    i = pl.program_id(0)
    pfx = prefix_ref[0]
    rate2 = -jnp.exp(dlog_ref[...]) * LOG2E
    lanes = [slice(g * 256, (g + 1) * 256) for g in range(groups)]

    def positions(chunk):
        return iota((lc, 1), 0) + chunk * lc

    def col(ref, t0, k):
        one = jnp.broadcast_to(pltpu.roll(ref[...], lax.rem(lc - t0, lc), 1)[:, k : k + 1], (n, 128))
        return jnp.concatenate([one, one], axis=1)

    @pl.when(i == 0)
    def _():
        st_f[...] = jnp.zeros_like(st_f)
        st_h[...] = jnp.zeros_like(st_h)
        st_q[...] = jnp.zeros_like(st_q)
        gskip_ref[...] = jnp.zeros_like(gskip_ref)

    proj = proj_ref[...]
    bt_s[...] = mm_nt(pick(r, p, n), proj)

    @pl.when(i < ng)
    def _():
        chunk = ng - 1 - i
        step = softplus(mm(proj[:, :r], sw_ref[...]) + bias_ref[...])
        keep_s[chunk] = step

        @pl.when(chunk * lc < pfx)
        def _():
            mask = (positions(chunk) < pfx).astype(F32)
            split(step_s, step)
            split(sd_s, step * drive_ref[...].astype(F32) * mask)
            base = chunk * (lc * n)

            def body(ir, state):
                t0 = pl.multiple_of((nb - 1 - ir) * T, T)
                state = list(state)
                bt = pltpu.roll(bt_s[...], lax.rem(lc - t0, lc), 1)
                for k in range(T - 1, -1, -1):
                    t = t0 + k
                    bb = jnp.broadcast_to(bt[:, k : k + 1], (n, 128))
                    bb = jnp.concatenate([bb, bb], axis=1)
                    at = pl.ds(pl.multiple_of(base + t * n, n), n)
                    for g in range(groups):
                        q = jnp.exp2(row(step_s, g, t, n) * rate2[:, lanes[g]]) * state[g]
                        state[g] = q + bb * row(sd_s, g, t, n)
                        qg_s[at, lanes[g]] = q.astype(BF)
                        g_s[at, lanes[g]] = state[g].astype(BF)
                return tuple(state)

            out = lax.fori_loop(0, nb, body, tuple(st_f[g] for g in range(groups)))
            for g in range(groups):
                st_f[g] = out[g]

    @pl.when(i >= ng)
    def _():
        chunk = i - ng

        @pl.when(chunk < ng)
        def _():
            step_ref[...] = keep_s[jnp.minimum(chunk, ng - 1)]

        @pl.when(chunk >= ng)
        def _():
            step_ref[...] = softplus(mm(proj[:, :r], sw_ref[...]) + bias_ref[...])

        step = step_ref[...]
        drive = drive_ref[...].astype(F32)
        z = z_ref[...]
        sig = 1.0 / (1.0 + jnp.exp2(z * -LOG2E))
        sig_s[...] = sig
        dy = dg_ref[...] * (z * sig)
        dy_ref[...] = dy
        gskip_ref[...] += jnp.sum(dy * drive, axis=0, keepdims=True)
        split(step_s, step)
        split(sd_s, step * drive)
        ct_s[...] = mm_nt(pick(r + n, p, n), proj)
        cbd_s[...] = jnp.where(blockdiag(lc, n), mm(proj, spread(r + n, p, n)), 0.0).astype(BF)
        diag = blockdiag(T, n)

        def mxu(b, buf):
            rows = pl.ds(pl.multiple_of(b * T, T), T)
            kept = {}

            def y_part(g):
                kept[g] = mm(cbd_s[rows, :], hg_s[buf, :, lanes[g]])

            def r_part(g):
                x = mm_nt(dy_ref[rows, lanes[g]].astype(BF), hg_s[buf, :, lanes[g]])
                kept["r"] = x if g == 0 else kept["r"] + x
                if g == groups - 1:
                    rc_s[rows, :] = jnp.where(diag, kept["r"], 0.0).astype(BF)

            def end(g):
                ln = lanes[g]
                y = kept[g] + skip_ref[:, ln] * drive_ref[rows, ln].astype(F32)
                zz = z_ref[rows, ln]
                sg = sig_s[rows, ln]
                gated_ref[rows, ln] = (y * (zz * sg)).astype(BF)
                dz_ref[rows, ln] = (dg_ref[rows, ln] * y * (sg * (1.0 + zz * (1.0 - sg)))).astype(BF)

            return [functools.partial(f, g) for g in range(groups) for f in (y_part, r_part, end)]

        def vpu(with_g, b, buf, state, pieces=()):
            hs, hbs, qs = (list(s) for s in state)
            pieces = list(pieces)
            t0 = pl.multiple_of(b * T, T)
            bt = pltpu.roll(bt_s[...], lax.rem(lc - t0, lc), 1)
            ct = pltpu.roll(ct_s[...], lax.rem(lc - t0, lc), 1) if with_g else None
            base = jnp.minimum(chunk, ng - 1) * (lc * n)
            for k in range(T):
                t = t0 + k
                bb = jnp.broadcast_to(bt[:, k : k + 1], (n, 128))
                bb = jnp.concatenate([bb, bb], axis=1)
                if with_g:
                    cc = jnp.broadcast_to(ct[:, k : k + 1], (n, 128))
                    cc = jnp.concatenate([cc, cc], axis=1)
                at = pl.ds(pl.multiple_of(t * n, n), n)
                far = pl.ds(pl.multiple_of(base + t * n, n), n)
                for g in range(groups):
                    ln = lanes[g]
                    e = jnp.exp2(row(step_s, g, t, n) * rate2[:, ln])
                    hprev_ref[at, ln] = hbs[g]
                    hs[g] = e * hs[g] + bb * row(sd_s, g, t, n)
                    hbs[g] = hs[g].astype(BF)
                    if with_g:
                        hg_s[buf, pl.ds(k * n, n), ln] = hbs[g] + g_s[far, ln]
                        ag = cc * row(dy_s, g, t, n) + qs[g]
                        qs[g] = e * ag
                        agb = ag.astype(BF)
                        ag_ref[at, ln] = agb
                        wg_ref[at, ln] = agb * qg_s[far, ln]
                    else:
                        hg_s[buf, pl.ds(k * n, n), ln] = hbs[g]
                if k % 2 and pieces:
                    pieces.pop(0)()
            for f in pieces:
                f()
            return tuple(hs), tuple(hbs), tuple(qs)

        def run(with_g):
            many = range(groups)
            state = tuple(st_f[g + groups] for g in many), tuple(st_h[g] for g in many), tuple(st_q[g] for g in many)
            state = vpu(with_g, 0, 0, state)

            def body(j, state):
                state = vpu(with_g, 2 * j + 1, 1, state, mxu(2 * j, 0))
                return vpu(with_g, 2 * j + 2, 0, state, mxu(2 * j + 1, 1))

            state = lax.fori_loop(0, nb // 2 - 1, body, state)
            state = vpu(with_g, nb - 1, 1, state, mxu(nb - 2, 0))
            for f in mxu(nb - 1, 1):
                f()
            for g in many:
                st_f[g + groups] = state[0][g]
                st_h[g] = state[1][g]
                st_q[g] = state[2][g]

        live = jnp.logical_and(chunk < ng, chunk * lc < pfx)

        @pl.when(live)
        def _():
            mask = (positions(chunk) < pfx).astype(F32)
            split(dy_s, dy * mask)
            run(True)

            @pl.when(pfx < (chunk + 1) * lc)
            def _():
                keep = iota((lc * n, c), 0) + chunk * (lc * n) < pfx * n
                ag_ref[...] = jnp.where(keep, ag_ref[...].astype(F32), 0.0).astype(BF)

        @pl.when(jnp.logical_not(live))
        def _():
            run(False)

        part_ref[...] = mm(rc_s[...], fold(r + n, p, n))


def back_kernel(ng, prefix_ref, proj_ref, sw_ref, drive_ref, step_ref, dy_ref, h_ref, ag_ref, wg_ref, pin_ref, dlog_ref, skip_ref,
                part_ref, dpre_ref, ddrive_ref, gdecay_ref, gbias_ref,
                step_s, dy_s, p_s, acc_s, ct_s, bbd_s, rb_s, ds_s, v_s):
    lc, c = drive_ref.shape
    p = proj_ref.shape[1]
    n = dlog_ref.shape[0]
    r = p - 2 * n
    tn = T * n
    nb = lc // T
    groups = c // 256
    i = pl.program_id(0)
    chunk = pl.num_programs(0) - 1 - i
    rate2 = -jnp.exp(dlog_ref[...]) * LOG2E
    rate2b = rate2.astype(BF)
    lanes = [slice(g * 256, (g + 1) * 256) for g in range(groups)]

    @pl.when(i == 0)
    def _():
        p_s[...] = jnp.zeros_like(p_s)
        acc_s[...] = jnp.zeros_like(acc_s)
        gbias_ref[...] = jnp.zeros_like(gbias_ref)

    proj = proj_ref[...]
    split(step_s, step_ref[...])
    split(dy_s, dy_ref[...])
    ct_s[...] = mm_nt(pick(r + n, p, n), proj)
    bbd_s[...] = jnp.where(blockdiag(lc, n), mm(proj, spread(r, p, n)), 0.0).astype(BF)
    diag = blockdiag(T, n)
    ones = diag.astype(BF)

    def vpu(with_g, b, buf, state, pieces=()):
        ps, accs = (list(s) for s in state)
        pieces = list(pieces)
        t0 = pl.multiple_of(b * T, T)
        ct = pltpu.roll(ct_s[...], lax.rem(lc - t0, lc), 1)
        for k in range(T - 1, -1, -1):
            t = t0 + k
            cc = jnp.broadcast_to(ct[:, k : k + 1], (n, 128))
            cc = jnp.concatenate([cc, cc], axis=1)
            at = pl.ds(pl.multiple_of(t * n, n), n)
            for g in range(groups):
                ln = lanes[g]
                st = row(step_s, g, t, n)
                e = jnp.exp2(st * rate2[:, ln])
                ah = cc * row(dy_s, g, t, n) + ps[g]
                ps[g] = e * ah
                dsrc = ah.astype(BF)
                w = ps[g].astype(BF) * h_ref[at, ln]
                if with_g:
                    dsrc = dsrc + ag_ref[at, ln]
                    w = w + wg_ref[at, ln]
                ds_s[buf, pl.ds(k * n, n), ln] = dsrc
                v_s[buf, pl.ds(k * n, n), ln] = w * rate2b[:, ln]
                accs[g] = accs[g] + w.astype(F32) * st
            if k % 2 == 0 and pieces:
                pieces.pop(0)()
        for f in pieces:
            f()
        return tuple(ps), tuple(accs)

    def mxu(b, buf):
        rows = pl.ds(pl.multiple_of(b * T, T), T)
        kept = {}

        def s_part(g):
            kept["s", g] = mm(bbd_s[rows, :], ds_s[buf, :, lanes[g]])

        def v_part(g):
            kept["v", g] = mm(ones, v_s[buf, :, lanes[g]])

        def r_part(g):
            ln = lanes[g]
            sd = step_ref[rows, ln] * drive_ref[rows, ln].astype(F32)
            x = mm_nt(sd.astype(BF), ds_s[buf, :, ln])
            kept["r"] = x if g == 0 else kept["r"] + x
            if g == groups - 1:
                rb_s[rows, :] = jnp.where(diag, kept["r"], 0.0).astype(BF)

        def end(g):
            ln = lanes[g]
            step = step_ref[rows, ln]
            ssum = kept["s", g]
            drive = drive_ref[rows, ln].astype(F32)
            dpre = (kept["v", g] * LN2 + drive * ssum) * one_minus_exp(step)
            dpre_ref[rows, ln] = dpre.astype(BF)
            ddrive_ref[rows, ln] = skip_ref[:, ln] * dy_ref[rows, ln] + step * ssum
            gbias_ref[:, ln] += jnp.sum(dpre, axis=0, keepdims=True)

        return [functools.partial(f, g) for g in range(groups) for f in (s_part, v_part, r_part, end)]

    def run(with_g):
        many = range(groups)
        state = tuple(p_s[g] for g in many), tuple(acc_s[g] for g in many)
        state = vpu(with_g, nb - 1, 0, state)

        def body(j, state):
            b = nb - 1 - 2 * j
            state = vpu(with_g, b - 1, 1, state, mxu(b, 0))
            return vpu(with_g, b - 2, 0, state, mxu(b - 1, 1))

        state = lax.fori_loop(0, nb // 2 - 1, body, state)
        state = vpu(with_g, 0, 1, state, mxu(1, 0))
        for f in mxu(0, 1):
            f()
        for g in many:
            p_s[g] = state[0][g]
            acc_s[g] = state[1][g]

    live = jnp.logical_and(chunk < ng, chunk * lc < prefix_ref[0])

    @pl.when(live)
    def _():
        run(True)

    @pl.when(jnp.logical_not(live))
    def _():
        run(False)

    part_ref[...] = (pin_ref[...] + mm(rb_s[...], fold(r, p, n)) + mm_nt(dpre_ref[...], sw_ref[...])).astype(part_ref.dtype)
    gdecay_ref[...] = jnp.concatenate([acc_s[g] for g in range(groups)], axis=1) * (rate2 * LN2)


def whole(*s):
    return pl.BlockSpec(s, lambda i: (0,) * len(s))


SMEM = pl.BlockSpec(memory_space=pltpu.SMEM)


def front(prefix, proj, sw, bias, drive, z, dg, dlog, skip):
    l, c = drive.shape
    p = proj.shape[1]
    n = dlog.shape[0]
    ng = l // 2 // LC
    nc = l // LC
    s = jax.ShapeDtypeStruct
    fwd = lambda i: (jnp.maximum(i - ng, 0), 0)
    both = lambda i: (jnp.where(i < ng, ng - 1 - i, i - ng), 0)
    half = lambda i: (jnp.clip(i - ng, 0, ng - 1), 0)
    B = pl.BlockSpec
    lanes = c // 128
    v = pltpu.VMEM
    return pl.pallas_call(
        functools.partial(front_kernel, ng),
        grid=(ng + nc,),
        in_specs=[SMEM, B((LC, p), both), whole(*sw.shape), whole(1, c), B((LC, c), both), B((LC, c), fwd), B((LC, c), fwd), whole(n, c), whole(1, c)],
        out_specs=[B((LC, c), fwd), B((LC, c), fwd), B((LC, c), fwd), B((LC, c), fwd), B((LC * n, c), fwd), B((LC * n, c), half), B((LC * n, c), half), B((LC, p), fwd), whole(1, c)],
        out_shape=[s((l, c), BF), s((l, c), BF), s((l, c), F32), s((l, c), F32), s((l * n, c), BF), s((l // 2 * n, c), BF), s((l // 2 * n, c), BF), s((l, p), F32), s((1, c), F32)],
        scratch_shapes=[v((lanes, LC, 128), F32)] * 3 + [v((LC, c), F32), v((ng, LC, c), F32), v((n, LC), F32), v((n, LC), F32), v((LC, T * n), BF), v((LC, T * n), BF),
            v((2, T * n, c), BF), v((l // 2 * n, c), BF), v((l // 2 * n, c), BF), v((c // 128, n, 256), F32), v((c // 256, n, 256), BF), v((c // 256, n, 256), F32)],
        compiler_params=pltpu.CompilerParams(vmem_limit_bytes=56 << 20),
        name="front",
    )(prefix, proj, sw, bias.reshape(1, c), drive, z, dg, dlog, skip.reshape(1, c))


def back(prefix, proj, sw_wide, drive, step, dy, hprev, ag, wg, pin, dlog, skip):
    l, c = drive.shape
    p = proj.shape[1]
    n = dlog.shape[0]
    ng = l // 2 // LC
    nc = l // LC
    s = jax.ShapeDtypeStruct
    rev = lambda i: (nc - 1 - i, 0)
    half = lambda i: (jnp.minimum(nc - 1 - i, ng - 1), 0)
    B = pl.BlockSpec
    v = pltpu.VMEM
    return pl.pallas_call(
        functools.partial(back_kernel, ng),
        grid=(nc,),
        in_specs=[SMEM, B((LC, p), rev), whole(*sw_wide.shape), B((LC, c), rev), B((LC, c), rev), B((LC, c), rev), B((LC * n, c), rev), B((LC * n, c), half), B((LC * n, c), half), B((LC, p), rev), whole(n, c), whole(1, c)],
        out_specs=[B((LC, p), rev), B((LC, c), rev), B((LC, c), rev), whole(n, c), whole(1, c)],
        out_shape=[s((l, p), BF), s((l, c), BF), s((l, c), F32), s((n, c), F32), s((1, c), F32)],
        scratch_shapes=[v((c // 128, LC, 128), F32)] * 2 + [v((c // 256, n, 256), F32)] * 2 + [v((n, LC), F32), v((LC, T * n), BF), v((LC, T * n), BF), v((2, T * n, c), BF), v((2, T * n, c), BF)],
        compiler_params=pltpu.CompilerParams(vmem_limit_bytes=40 << 20),
        name="back",
    )(prefix, proj, sw_wide, drive, step, dy, hprev, ag, wg, pin, dlog, skip.reshape(1, c))


def exchange(value, name, size, bit):
    return lax.ppermute(value, name, [(j, j ^ (1 << bit)) for j in range(size)])


def bits_of(size):
    count = size.bit_length() - 1
    assert 1 << count == size
    return list(range(count))


def butterfly(value, name, size):
    total = value
    for bit in bits_of(size):
        low = total.astype(BF)
        total = low.astype(F32) + exchange(low, name, size, bit).astype(F32)
    return total


def scatter_sum(value, name, size, order):
    at = lax.axis_index(name)
    for bit in order:
        mine = (at >> bit) & 1
        half = value.shape[0] // 2
        send = lax.dynamic_slice_in_dim(value, (1 - mine) * half, half, 0).astype(BF)
        keep = lax.dynamic_slice_in_dim(value, mine * half, half, 0)
        value = keep.astype(F32) + exchange(send, name, size, bit).astype(F32)
    return value


def gather_rows(value, name, size, order):
    at = lax.axis_index(name)
    for bit in reversed(order):
        mine = (at >> bit) & 1
        other = exchange(value, name, size, bit)
        value = jnp.where(mine == 0, jnp.concatenate([value, other]), jnp.concatenate([other, value]))
    return value


def all_sum(value, name, size):
    order = bits_of(size)
    turned = order[1:] + order[:1]
    half = value.shape[0] // 2
    low = value.astype(BF)
    parts = []
    for piece, way in ((low[:half], order), (low[half:], turned)):
        mine = scatter_sum(piece, name, size, way)
        parts.append(gather_rows(mine.astype(BF), name, size, way))
    return jnp.concatenate(parts)


def shifted(values, by):
    if by == 0:
        return values
    if by > 0:
        return jnp.pad(values, ((by, 0), (0, 0)))[: values.shape[0]]
    return jnp.pad(values, ((0, -by), (0, 0)))[-by:]


def sigmoid(v):
    return 1.0 / (1.0 + jnp.exp(-v))


def on_device(sizes, tokens, prefix, norm_gain, in_weight, conv_weight, conv_bias, xproj_weight, step_weight, step_bias, decay_log, skip_gain, out_weight, out_cotangent):
    dp, tp = sizes
    seqs, length, width = tokens.shape
    assert seqs == 1
    channels = in_weight.shape[2]
    rank = step_weight.shape[0]
    taps = conv_weight.shape[0]
    n = decay_log.shape[0]
    low = tokens[0]
    xf = low.astype(F32)
    cot = out_cotangent[0]
    w_x = in_weight[:, 0, :]
    w_z = in_weight[:, 1, :]

    rs = lax.rsqrt(jnp.mean(xf * xf, axis=-1, keepdims=True) + epsilon)
    normed = (xf * rs * norm_gain).astype(BF)
    xpart = mm(normed, w_x)
    zpart = mm(normed, w_z)
    convout = conv_bias + sum(conv_weight[k] * shifted(xpart, taps - 1 - k) for k in range(taps))
    drive = (convout * sigmoid(convout)).astype(BF)
    proj = butterfly(mm(drive, xproj_weight), "tensor", tp).astype(BF)
    dgated = mm_nt(cot, out_weight)

    gated, dz, step, dy, hprev, ag, wg, pin, gskip = front(prefix, proj, step_weight, step_bias, drive, zpart, dgated, decay_log, skip_gain)

    t_order = bits_of(tp)
    rows = length // tp
    at = lax.axis_index("tensor")
    spot = 0
    part = length
    for bit in t_order:
        part //= 2
        spot = spot + ((at >> bit) & 1) * part
    mixed = scatter_sum(mm(gated, out_weight), "tensor", tp, t_order)
    mixed = (lax.dynamic_slice_in_dim(xf, spot, rows, 0) + mixed).astype(BF)
    block_out = gather_rows(mixed, "tensor", tp, t_order)

    tn = (((0,), (0,)), ((), ()))
    mm_tn = lambda a, b: lax.dot_general(a, b, tn, preferred_element_type=F32)
    g_out = mm_tn(gated, cot)
    g_in_z = mm_tn(normed, dz)
    early = all_sum(jnp.concatenate([g_in_z.astype(BF), g_out.astype(BF).reshape(-1, channels)]), "dp", dp)

    wide = jnp.pad(step_weight, ((0, 2 * n), (0, 0)))
    dpart, dpre, ddrive_scan, g_decay, g_bias = back(prefix, proj, wide, drive, step, dy, hprev, ag, wg, pin, decay_log, skip_gain)
    dproj = butterfly(dpart, "tensor", tp).astype(BF)
    g_step = mm_tn(proj[:, :rank], dpre)
    g_xproj = mm_tn(dproj, drive)
    ddrive = ddrive_scan + mm_nt(dproj, xproj_weight)
    sc = sigmoid(convout)
    dconv = ddrive * (sc * (1.0 + convout * (1.0 - sc)))
    g_conv = jnp.stack([jnp.sum(dconv * shifted(xpart, taps - 1 - k), axis=0) for k in range(taps)])
    g_convb = jnp.sum(dconv, axis=0, keepdims=True)
    dx = sum(conv_weight[k] * shifted(dconv, k - taps + 1) for k in range(taps)).astype(BF)
    g_in_x = mm_tn(normed, dx)
    dnormed = mm_nt(dx, w_x) + mm_nt(dz, w_z)
    g_norm = jnp.sum(dnormed * (xf * rs), axis=0).reshape(-1, channels)
    small = [g_conv, g_convb, g_bias, g_decay, gskip, g_step, g_xproj, g_norm]
    counts = [s.shape[0] for s in small]
    fill = -sum(counts) % (2 * dp)
    packed = jnp.concatenate([s.astype(BF) for s in small] + [jnp.zeros((fill, channels), BF), g_in_x.astype(BF)])
    late = all_sum(packed, "dp", dp).astype(F32)

    mine = scatter_sum(dnormed, "tensor", tp, t_order)
    my_x = lax.dynamic_slice_in_dim(xf, spot, rows, 0)
    my_rs = lax.dynamic_slice_in_dim(rs, spot, rows, 0)
    scaled = mine * norm_gain
    moved = my_rs * scaled - my_x * (my_rs * my_rs * my_rs) * jnp.mean(scaled * my_x, axis=-1, keepdims=True)
    moved = gather_rows(moved.astype(BF), "tensor", tp, t_order)
    grad_tokens = cot.astype(F32) + moved.astype(F32)

    out = []
    top = 0
    for count in counts:
        out.append(late[top : top + count])
        top += count
    g_conv, g_convb, g_bias, g_decay, gskip, g_step, g_xproj, g_norm = out
    g_in_x = late[top + fill :]
    early = early.astype(F32)
    g_in = jnp.stack([g_in_x, early[:width]], axis=1)
    g_out = early[width:].reshape(channels, width)
    g_norm = g_norm.reshape(-1)
    for bit in bits_of(tp):
        g_norm = g_norm + exchange(g_norm, "tensor", tp, bit)
    return (block_out[None], grad_tokens[None], g_norm, g_in, g_conv, g_convb[0], g_xproj.T, g_step, g_bias[0], g_decay, gskip[0], g_out)


def solution(mesh):
    placed = (
        P("dp", None, None),
        P("dp"),
        P(),
        P(None, None, "tensor"),
        P(None, "tensor"),
        P("tensor"),
        P("tensor", None),
        P(None, "tensor"),
        P("tensor"),
        P(None, "tensor"),
        P("tensor"),
        P("tensor", None),
        P("dp", None, None),
    )
    results = (
        P("dp", None, None),
        P("dp", None, None),
        P(),
        P(None, None, "tensor"),
        P(None, "tensor"),
        P("tensor"),
        P("tensor", None),
        P(None, "tensor"),
        P("tensor"),
        P(None, "tensor"),
        P("tensor"),
        P("tensor", None),
    )
    sizes = (mesh.shape["dp"], mesh.shape["tensor"])
    return jax.shard_map(functools.partial(on_device, sizes), mesh=mesh, in_specs=placed, out_specs=results, check_vma=False)
```

```python
import functools

import jax
import jax.numpy as jnp
from jax import lax
from jax.experimental import pallas as pl
from jax.experimental.pallas import tpu as pltpu
from jax.sharding import PartitionSpec as P

T = 16
LC = 128
PIECES = (5, 2, 0)
LOG2E = 1.4426950408889634
LN2 = 0.6931471805599453
F32 = jnp.float32
BF = jnp.bfloat16
NT = (((1,), (1,)), ((), ()))
STRIDED = True
epsilon = 1e-05


def iota(shape, d):
    return lax.broadcasted_iota(jnp.int32, shape, d)


def mm(a, b):
    return jnp.dot(a, b, preferred_element_type=F32)


def mm_nt(a, b):
    return lax.dot_general(a, b, NT, preferred_element_type=F32)


def row(ref, g, t, n):
    if STRIDED:
        pair = [ref[2 * g + j, pl.ds(t, 8, stride=0), :] for j in (0, 1)]
        wide = jnp.concatenate(pair, axis=1)
        return jnp.concatenate([wide] * (n // 8), axis=0)
    pair = [jnp.broadcast_to(ref[2 * g + j, pl.ds(t, 1), :], (n, 128)) for j in (0, 1)]
    return jnp.concatenate(pair, axis=1)


def spread(base, p, n):
    return (iota((p, T * n), 0) == base + lax.rem(iota((p, T * n), 1), n)).astype(BF)


def pick(base, p, n):
    return (iota((n, p), 1) == base + iota((n, p), 0)).astype(BF)


def fold(base, p, n):
    return (iota((T * n, p), 1) == base + lax.rem(iota((T * n, p), 0), n)).astype(BF)


def blockdiag(rows, n):
    return lax.rem(iota((rows, T * n), 0), T) == lax.div(iota((rows, T * n), 1), n)


def split(ref, value):
    for g in range(value.shape[1] // 128):
        ref[g] = value[:, g * 128 : (g + 1) * 128]


def softplus(x):
    e = jnp.exp2(jnp.abs(x) * -LOG2E)
    small = e * (1.0 - e * (0.5 - e * (1.0 / 3.0 - e * 0.25)))
    return jnp.maximum(x, 0.0) + jnp.where(e < 0.03125, small, jnp.log2(1.0 + e) * LN2)


def one_minus_exp(s):
    small = s * (1.0 - s * (0.5 - s * (1.0 / 6.0 - s * (1.0 / 24.0))))
    return jnp.where(s < 0.0625, small, 1.0 - jnp.exp2(s * -LOG2E))


def front_kernel(ng, prefix_ref, proj_ref, sw_ref, bias_ref, drive_ref, z_ref, dg_ref, dlog_ref, skip_ref,
                 gated_ref, dz_ref, step_ref, dy_ref, hprev_ref, ag_ref, wg_ref, part_ref, gskip_ref,
                 step_s, sd_s, dy_s, sig_s, keep_s, bt_s, ct_s, cbd_s, rc_s, hg_s, g_s, qg_s, st_f, st_h, st_q):
    lc, c = drive_ref.shape
    p = proj_ref.shape[1]
    n = dlog_ref.shape[0]
    r = p - 2 * n
    tn = T * n
    nb = lc // T
    groups = c // 256
    i = pl.program_id(0)
    pfx = prefix_ref[0]
    rate2 = -jnp.exp(dlog_ref[...]) * LOG2E
    lanes = [slice(g * 256, (g + 1) * 256) for g in range(groups)]

    def positions(chunk):
        return iota((lc, 1), 0) + chunk * lc

    def col(ref, t0, k):
        one = jnp.broadcast_to(pltpu.roll(ref[...], lax.rem(lc - t0, lc), 1)[:, k : k + 1], (n, 128))
        return jnp.concatenate([one, one], axis=1)

    @pl.when(i == 0)
    def _():
        st_f[...] = jnp.zeros_like(st_f)
        st_h[...] = jnp.zeros_like(st_h)
        st_q[...] = jnp.zeros_like(st_q)
        gskip_ref[...] = jnp.zeros_like(gskip_ref)

    proj = proj_ref[...]
    bt_s[...] = mm_nt(pick(r, p, n), proj)

    @pl.when(i < ng)
    def _():
        chunk = ng - 1 - i
        step = softplus(mm(proj[:, :r], sw_ref[...]) + bias_ref[...])
        keep_s[chunk] = step

        @pl.when(chunk * lc < pfx)
        def _():
            mask = (positions(chunk) < pfx).astype(F32)
            split(step_s, step)
            split(sd_s, step * drive_ref[...].astype(F32) * mask)
            base = chunk * (lc * n)

            def body(ir, state):
                t0 = (nb - 1 - ir) * T
                state = list(state)
                bt = bt_s[:, t0 : t0 + T]
                for k in range(T - 1, -1, -1):
                    t = t0 + k
                    bb = jnp.broadcast_to(bt[:, k : k + 1], (n, 128))
                    bb = jnp.concatenate([bb, bb], axis=1)
                    at = pl.ds(pl.multiple_of(base + t * n, n), n)
                    for g in range(groups):
                        q = jnp.exp2(row(step_s, g, t, n) * rate2[:, lanes[g]]) * state[g]
                        state[g] = q + bb * row(sd_s, g, t, n)
                        qg_s[at, lanes[g]] = q.astype(BF)
                        g_s[at, lanes[g]] = state[g].astype(BF)
                return tuple(state)

            out = tuple(st_f[g] for g in range(groups))
            for ir in range(nb):
                out = body(ir, out)
            for g in range(groups):
                st_f[g] = out[g]

    @pl.when(i >= ng)
    def _():
        chunk = i - ng

        @pl.when(chunk < ng)
        def _():
            step_ref[...] = keep_s[jnp.minimum(chunk, ng - 1)]

        @pl.when(chunk >= ng)
        def _():
            step_ref[...] = softplus(mm(proj[:, :r], sw_ref[...]) + bias_ref[...])

        step = step_ref[...]
        drive = drive_ref[...].astype(F32)
        z = z_ref[...]
        sig = 1.0 / (1.0 + jnp.exp2(z * -LOG2E))
        sig_s[...] = sig
        dy = dg_ref[...] * (z * sig)
        dy_ref[...] = dy
        gskip_ref[...] += jnp.sum(dy * drive, axis=0, keepdims=True)
        split(step_s, step)
        split(sd_s, step * drive)
        ct_s[...] = mm_nt(pick(r + n, p, n), proj)
        cbd_s[...] = jnp.where(blockdiag(lc, n), mm(proj, spread(r + n, p, n)), 0.0).astype(BF)
        diag = blockdiag(T, n)

        def mxu(b, buf):
            rows = pl.ds(b * T, T)
            kept = {}

            def y_part(g):
                kept[g] = mm(cbd_s[rows, :], hg_s[buf, :, lanes[g]])

            def r_part(g):
                x = mm_nt(dy_ref[rows, lanes[g]].astype(BF), hg_s[buf, :, lanes[g]])
                kept["r"] = x if g == 0 else kept["r"] + x
                if g == groups - 1:
                    rc_s[rows, :] = jnp.where(diag, kept["r"], 0.0).astype(BF)

            def end(g):
                ln = lanes[g]
                y = kept[g] + skip_ref[:, ln] * drive_ref[rows, ln].astype(F32)
                zz = z_ref[rows, ln]
                sg = sig_s[rows, ln]
                gated_ref[rows, ln] = (y * (zz * sg)).astype(BF)
                dz_ref[rows, ln] = (dg_ref[rows, ln] * y * (sg * (1.0 + zz * (1.0 - sg)))).astype(BF)

            return [functools.partial(f, g) for g in range(groups) for f in (y_part, r_part, end)]

        def vpu(with_g, b, buf, state, pieces=()):
            hs, hbs, qs = (list(s) for s in state)
            pieces = list(pieces)
            t0 = b * T
            bt = bt_s[:, t0 : t0 + T]
            ct = ct_s[:, t0 : t0 + T] if with_g else None
            base = jnp.minimum(chunk, ng - 1) * (lc * n)
            for k in range(T):
                t = t0 + k
                bb = jnp.broadcast_to(bt[:, k : k + 1], (n, 128))
                bb = jnp.concatenate([bb, bb], axis=1)
                if with_g:
                    cc = jnp.broadcast_to(ct[:, k : k + 1], (n, 128))
                    cc = jnp.concatenate([cc, cc], axis=1)
                at = pl.ds(t * n, n)
                far = pl.ds(pl.multiple_of(base + t * n, n), n)
                for g in range(groups):
                    ln = lanes[g]
                    e = jnp.exp2(row(step_s, g, t, n) * rate2[:, ln])
                    hprev_ref[at, ln] = hbs[g]
                    hs[g] = e * hs[g] + bb * row(sd_s, g, t, n)
                    hbs[g] = hs[g].astype(BF)
                    if with_g:
                        hg_s[buf, pl.ds(k * n, n), ln] = hbs[g] + g_s[far, ln]
                        ag = cc * row(dy_s, g, t, n) + qs[g]
                        qs[g] = e * ag
                        agb = ag.astype(BF)
                        ag_ref[at, ln] = agb
                        wg_ref[at, ln] = agb * qg_s[far, ln]
                    else:
                        hg_s[buf, pl.ds(k * n, n), ln] = hbs[g]
                if k % 2 and pieces:
                    pieces.pop(0)()
            for f in pieces:
                f()
            return tuple(hs), tuple(hbs), tuple(qs)

        def run(with_g):
            many = range(groups)
            state = tuple(st_f[g + groups] for g in many), tuple(st_h[g] for g in many), tuple(st_q[g] for g in many)
            state = vpu(with_g, 0, 0, state)
            for b in range(1, nb):
                state = vpu(with_g, b, b, state, mxu(b - 1, b - 1))
            for f in mxu(nb - 1, nb - 1):
                f()
            for g in many:
                st_f[g + groups] = state[0][g]
                st_h[g] = state[1][g]
                st_q[g] = state[2][g]

        live = jnp.logical_and(chunk < ng, chunk * lc < pfx)

        @pl.when(live)
        def _():
            mask = (positions(chunk) < pfx).astype(F32)
            split(dy_s, dy * mask)
            run(True)

            @pl.when(pfx < (chunk + 1) * lc)
            def _():
                keep = iota((lc * n, c), 0) + chunk * (lc * n) < pfx * n
                ag_ref[...] = jnp.where(keep, ag_ref[...].astype(F32), 0.0).astype(BF)

        @pl.when(jnp.logical_not(live))
        def _():
            run(False)

        part_ref[...] = mm(rc_s[...], fold(r + n, p, n))


def back_kernel(ng, top, low, far, prefix_ref, proj_ref, sw_ref, drive_ref, step_ref, dy_ref, h_ref, ag_ref, wg_ref, pin_ref, dlog_ref, skip_ref, pc_ref, ac_ref, bc_ref, *refs):
    (part_ref, dpre_ref, ddrive_ref, po_ref, ao_ref, gbias_ref, step_s, dy_s, p_s, ct_s, bbd_s, rb_s, ds_s, v_s, w_s) = refs[far:]
    lc, c = drive_ref.shape
    p = proj_ref.shape[1]
    n = dlog_ref.shape[0]
    r = p - 2 * n
    tn = T * n
    nb = lc // T
    groups = c // 256
    i = pl.program_id(0)
    chunk = top - i
    rate2 = -jnp.exp(dlog_ref[...]) * LOG2E
    rate2b = rate2.astype(BF)
    lanes = [slice(g * 256, (g + 1) * 256) for g in range(groups)]

    @pl.when(i == 0)
    def _():
        for g in range(groups):
            p_s[g] = pc_ref[:, lanes[g]]
        ao_ref[...] = ac_ref[...]
        gbias_ref[...] = bc_ref[...]

    proj = proj_ref[...]
    split(step_s, step_ref[...])
    split(dy_s, dy_ref[...])
    ct_s[...] = mm_nt(pick(r + n, p, n), proj)
    bbd_s[...] = jnp.where(blockdiag(lc, n), mm(proj, spread(r, p, n)), 0.0).astype(BF)
    diag = blockdiag(T, n)
    ones = diag.astype(BF)
    gather = (lax.rem(iota((n, tn // 2), 1), n) == iota((n, tn // 2), 0)).astype(BF)

    never = prefix_ref[0] < 0
    done = {}

    def vpu(with_g, b, buf, state, pieces=()):
        ps = list(state)
        seen = done.get(b + 3, {})
        pieces = list(pieces)
        held = [None] * groups
        t0 = b * T
        ct = ct_s[:, t0 : t0 + T]
        for k in range(T - 1, -1, -1):
            t = t0 + k
            for g in range(groups):
                key = {T - 1: ("s", g), T // 2: ("v", g), T // 4: ("w", g)}.get(k)
                if key in seen:
                    ps[g] = jnp.where(never, seen[key], ps[g])
            cc = jnp.broadcast_to(ct[:, k : k + 1], (n, 128))
            cc = jnp.concatenate([cc, cc], axis=1)
            at = pl.ds(t * n, n)
            for g in range(groups):
                ln = lanes[g]
                st = row(step_s, g, t, n)
                e = jnp.exp2(st * rate2[:, ln])
                ah = cc * row(dy_s, g, t, n) + ps[g]
                ps[g] = e * ah
                dsrc = ah.astype(BF)
                w = ps[g].astype(BF) * h_ref[at, ln]
                if with_g:
                    dsrc = dsrc + ag_ref[at, ln]
                    w = w + wg_ref[at, ln]
                ds_s[buf, pl.ds(k * n, n), ln] = dsrc
                v_s[buf, pl.ds(k * n, n), ln] = w * rate2b[:, ln]
                ws = w * st.astype(BF)
                if k % 2:
                    held[g] = ws
                else:
                    w_s[buf, pl.ds(k // 2 * n, n), ln] = held[g] + ws
            if k % 2 == 0 and pieces:
                pieces.pop(0)()
        for f in pieces:
            f()
        return tuple(ps)

    def mxu(b, buf):
        rows = pl.ds(b * T, T)
        kept = done[b] = {}

        def s_part(g):
            kept["s", g] = mm(bbd_s[rows, :], ds_s[buf, :, lanes[g]])

        def v_part(g):
            kept["v", g] = mm(ones, v_s[buf, :, lanes[g]])
            kept["w", g] = mm(gather, w_s[buf, :, lanes[g]])
            ao_ref[:, lanes[g]] += kept["w", g]

        def r_part(g):
            ln = lanes[g]
            sd = step_ref[rows, ln] * drive_ref[rows, ln].astype(F32)
            x = mm_nt(sd.astype(BF), ds_s[buf, :, ln])
            kept["r"] = x if g == 0 else kept["r"] + x
            if g == groups - 1:
                rb_s[rows, :] = jnp.where(diag, kept["r"], 0.0).astype(BF)

        def end(g):
            ln = lanes[g]
            step = step_ref[rows, ln]
            ssum = kept["s", g]
            drive = drive_ref[rows, ln].astype(F32)
            dpre = (kept["v", g] * LN2 + drive * ssum) * one_minus_exp(step)
            dpre_ref[rows, ln] = dpre.astype(BF)
            ddrive_ref[rows, ln] = skip_ref[:, ln] * dy_ref[rows, ln] + step * ssum
            gbias_ref[:, ln] += jnp.sum(dpre, axis=0, keepdims=True)

        return [functools.partial(f, g) for g in range(groups) for f in (s_part, v_part, r_part, end)]

    def run(with_g):
        done.clear()
        many = range(groups)
        state = tuple(p_s[g] for g in many)
        state = vpu(with_g, nb - 1, nb - 1, state)
        for b in range(nb - 2, -1, -1):
            state = vpu(with_g, b, b, state, mxu(b + 1, b + 1))
        for f in mxu(0, 0):
            f()
        for g in many:
            p_s[g] = state[g]

    if low >= ng:
        run(False)
    else:
        live = jnp.logical_and(chunk < ng, chunk * lc < prefix_ref[0])

        @pl.when(live)
        def _():
            run(True)

        @pl.when(jnp.logical_not(live))
        def _():
            run(False)

    part_ref[...] = (pin_ref[...] + mm(rb_s[...], fold(r, p, n)) + mm_nt(dpre_ref[...], sw_ref[...])).astype(part_ref.dtype)
    po_ref[...] = jnp.concatenate([p_s[g] for g in range(groups)], axis=1)


def whole(*s):
    return pl.BlockSpec(s, lambda i: (0,) * len(s))


SMEM = pl.BlockSpec(memory_space=pltpu.SMEM)


def head_kernel(low_ref, gain_ref, w_ref, cw_ref, cb_ref, xw_ref, normed_ref, x_ref, drive_ref, part_ref, rs_ref, edge_s):
    taps = cw_ref.shape[0]
    lc = low_ref.shape[0]

    @pl.when(pl.program_id(0) == 0)
    def _():
        edge_s[...] = jnp.zeros_like(edge_s)

    xf = low_ref[...].astype(F32)
    rs = lax.rsqrt(jnp.mean(xf * xf, axis=-1, keepdims=True) + epsilon)
    rs_ref[...] = rs
    normed = (xf * rs * gain_ref[...]).astype(BF)
    normed_ref[...] = normed
    x = mm(normed, w_ref[...])
    x_ref[...] = x
    wide = jnp.concatenate([edge_s[...], x], axis=0)
    edge_s[...] = x[lc - 8 :]
    out = cb_ref[...] + cw_ref[taps - 1 :, :] * x
    for k in range(taps - 1):
        at = 8 - (taps - 1) + k
        out = out + cw_ref[k : k + 1, :] * wide[at : at + lc]
    drive = (out * sigmoid(out)).astype(BF)
    drive_ref[...] = drive
    part_ref[...] = mm_nt(drive, xw_ref[...]).astype(BF)


def head(low, gain, w_all, conv_weight, conv_bias, xproj_t):
    l, d = low.shape
    c = w_all.shape[1] // 2
    p = xproj_t.shape[0]
    hc = 256
    by = lambda w: pl.BlockSpec((hc, w), lambda i: (i, 0))
    s = jax.ShapeDtypeStruct
    return pl.pallas_call(
        head_kernel,
        grid=(l // hc,),
        in_specs=[by(d), whole(1, d), whole(d, c), whole(*conv_weight.shape), whole(1, c), whole(p, c)],
        out_specs=[by(d), by(c), by(c), by(p), by(1)],
        out_shape=[s((l, d), BF), s((l, c), F32), s((l, c), BF), s((l, p), BF), s((l, 1), F32)],
        scratch_shapes=[pltpu.VMEM((8, c), F32)],
        compiler_params=pltpu.CompilerParams(vmem_limit_bytes=60 << 20),
        cost_estimate=pl.CostEstimate(flops=2 * l * d * c, transcendentals=l * c, bytes_accessed=4 * l * d + 2 * d * c + 6 * l * c),
        name="head",
    )(low, gain.reshape(1, d), w_all, conv_weight, conv_bias.reshape(1, c), xproj_t)


def gates_kernel(n_ref, w_ref, c_ref, o_ref, z_ref, dg_ref):
    z_ref[...] = mm(n_ref[...], w_ref[...])
    dg_ref[...] = mm_nt(c_ref[...], o_ref[...])


def gates(normed, w_all, cot, out_weight):
    l, d = normed.shape
    c = w_all.shape[1] // 2
    by = lambda w: pl.BlockSpec((256, w), lambda i: (i, 0))
    s = jax.ShapeDtypeStruct
    return pl.pallas_call(
        gates_kernel,
        grid=(l // 256,),
        in_specs=[by(d), pl.BlockSpec((d, c), lambda i: (0, 1)), by(d), whole(c, d)],
        out_specs=[by(c), by(c)],
        out_shape=[s((l, c), F32), s((l, c), F32)],
        compiler_params=pltpu.CompilerParams(vmem_limit_bytes=60 << 20),
        cost_estimate=pl.CostEstimate(flops=4 * l * d * c, transcendentals=0, bytes_accessed=4 * (l * d + d * c + 2 * l * c)),
        name="gates",
    )(normed, w_all, cot, out_weight)


def inner_kernel(rows_a, rows_b, bits_ref, dproj_ref, ds_ref, x_ref, xb_ref, drive_ref, dz_ref, normed_ref, low_ref, rs_ref, w_ref, xw_ref, cw_ref, cb_ref,
                 gb_ref, gd_ref, dlog_ref, gk_ref, proj_ref, dpre_ref, ka_ref, sa_ref, kb_ref, sb_ref, kn_ref, sn_ref, gn_ref, edge_s, gin_s, gx_s, gs_s, gc_s, gn_s, la_s, lb_s):
    taps = cw_ref.shape[0]
    lc, c = ds_ref.shape
    d = normed_ref.shape[1]
    p = dproj_ref.shape[1]
    n = gd_ref.shape[0]
    r = p - 2 * n
    i = pl.program_id(0)
    last = pl.num_programs(0) - 1
    tn = (((0,), (0,)), ((), ()))

    @pl.when(i == 0)
    def _():
        edge_s[...] = jnp.zeros_like(edge_s)
        gin_s[...] = jnp.zeros_like(gin_s)
        gx_s[...] = jnp.zeros_like(gx_s)
        gs_s[...] = jnp.zeros_like(gs_s)
        gc_s[...] = jnp.zeros_like(gc_s)
        gn_s[...] = jnp.zeros_like(gn_s)

    x = x_ref[...]
    before = jnp.where(i == last, 0.0, xb_ref[...])
    wide = jnp.concatenate([before, x], axis=0)
    moved = [wide[8 - (taps - 1) + k : 8 - (taps - 1) + k + lc] for k in range(taps - 1)] + [x]
    out = cb_ref[...]
    for k in range(taps):
        out = out + cw_ref[k : k + 1, :] * moved[k]
    sc = sigmoid(out)
    dproj = dproj_ref[...]
    ddrive = ds_ref[...] + mm(dproj, xw_ref[...])
    dconv = ddrive * (sc * (1.0 + out * (1.0 - sc)))
    gc_s[pl.ds(taps, 1), :] += jnp.sum(dconv, axis=0, keepdims=True)
    for k in range(taps):
        gc_s[pl.ds(k, 1), :] += jnp.sum(dconv * moved[k], axis=0, keepdims=True)
    ahead = jnp.concatenate([dconv, edge_s[...]], axis=0)
    edge_s[...] = dconv[:8]
    dx = cw_ref[taps - 1 :, :] * dconv
    for k in range(taps - 1):
        by = taps - 1 - k
        dx = dx + cw_ref[k : k + 1, :] * ahead[by : by + lc]
    dx = dx.astype(BF)
    normed = normed_ref[...]
    gin_s[...] += lax.dot_general(normed, dx, tn, preferred_element_type=F32)
    gx_s[...] += lax.dot_general(dproj, drive_ref[...], tn, preferred_element_type=F32)
    gs_s[...] += lax.dot_general(proj_ref[:, :r], dpre_ref[...], tn, preferred_element_type=F32)
    dn = mm_nt(dx, w_ref[:, :c]) + mm_nt(dz_ref[...], w_ref[:, c:])
    half = pl.num_programs(0) // 2

    @pl.when(i < half)
    def _():
        sn_ref[...] = dn.astype(BF)

    @pl.when(i >= half)
    def _():
        kn_ref[...] = dn.astype(BF)

    gn_s[...] += jnp.sum(dn * (low_ref[...].astype(F32) * rs_ref[...]), axis=0, keepdims=True)

    @pl.when(i == last)
    def _():
        gn_ref[...] = gn_s[...]
        lines = [gc_s[pl.ds(0, taps + 1), :], gb_ref[...], gk_ref[...]]
        lines = jnp.concatenate(lines + [jnp.zeros((16 - taps - 3, c), F32)], axis=0)
        top = 16 + n + r + p
        la_s[pl.ds(0, 16), :] = lines.astype(BF)
        la_s[pl.ds(16, n), :] = (gd_ref[...] * -jnp.exp(dlog_ref[...])).astype(BF)
        la_s[pl.ds(16 + n, r), :] = gs_s[...].astype(BF)
        la_s[pl.ds(16 + n + r, p), :] = gx_s[...].astype(BF)
        la_s[pl.ds(top, rows_a - top), :] = gin_s[pl.ds(0, rows_a - top), :].astype(BF)
        rest = d - (rows_a - top)
        lb_s[pl.ds(0, rest), :] = gin_s[pl.ds(rows_a - top, rest), :].astype(BF)
        lb_s[pl.ds(rest, rows_b - rest), :] = jnp.zeros((rows_b - rest, c), BF)
        for bit, total, keep_ref, send_ref in ((bits_ref[0], la_s, ka_ref, sa_ref), (bits_ref[1], lb_s, kb_ref, sb_ref)):
            rows = keep_ref.shape[0]
            keep_ref[...] = total[pl.ds(pl.multiple_of(bit * rows, 16), rows), :]
            send_ref[...] = total[pl.ds(pl.multiple_of((1 - bit) * rows, 16), rows), :]


def inner(rows_a, rows_b, bits, dproj, ddrive, x, drive, dz, normed, low, rs, w_all, xproj_t, conv_weight, conv_bias, g_bias, g_decay, decay_log, g_skip, proj, dpre):
    l, c = x.shape
    d = normed.shape[1]
    p = dproj.shape[1]
    n = g_decay.shape[0]
    hc = 256
    nc = l // hc
    by = lambda w: pl.BlockSpec((hc, w), lambda i: (nc - 1 - i, 0))
    s = jax.ShapeDtypeStruct
    v = pltpu.VMEM
    edge = pl.BlockSpec((8, c), lambda i: (jnp.maximum((nc - 1 - i) * (hc // 8) - 1, 0), 0))
    upper = pl.BlockSpec((hc, d), lambda i: (jnp.maximum(nc // 2 - 1 - i, 0), 0))
    lower = pl.BlockSpec((hc, d), lambda i: (jnp.minimum(nc - 1 - i, nc // 2 - 1), 0))
    return pl.pallas_call(
        functools.partial(inner_kernel, rows_a, rows_b),
        grid=(nc,),
        in_specs=[SMEM, by(p), by(c), by(c), edge, by(c), by(c), by(d), by(d), by(1), whole(d, 2 * c), whole(p, c), whole(*conv_weight.shape), whole(1, c),
                  whole(1, c), whole(n, c), whole(n, c), whole(1, c), by(p), by(c)],
        out_specs=[whole(rows_a // 2, c)] * 2 + [whole(rows_b // 2, c)] * 2 + [lower, upper, whole(1, d)],
        out_shape=[s((rows_a // 2, c), BF)] * 2 + [s((rows_b // 2, c), BF)] * 2 + [s((l // 2, d), BF)] * 2 + [s((1, d), F32)],
        scratch_shapes=[v((8, c), F32), v((d, c), F32), v((p, c), F32), v((p - 2 * n, c), F32), v((8, c), F32), v((1, d), F32), v((rows_a, c), BF), v((rows_b, c), BF)],
        compiler_params=pltpu.CompilerParams(vmem_limit_bytes=60 << 20),
        cost_estimate=pl.CostEstimate(flops=6 * l * d * c, transcendentals=l * c, bytes_accessed=10 * l * d),
        name="inner",
    )(bits, dproj, ddrive, x, x, drive, dz, normed, low, rs, w_all, xproj_t, conv_weight, conv_bias.reshape(1, c), g_bias, g_decay, decay_log, g_skip, proj, dpre)


def outer_kernel(order_ref, normed_ref, dz_ref, gated_ref, cot_ref, w_ref, kz_ref, sz_ref, ko_ref, so_ref, km_ref, sm_ref, z_s, o_s):
    i = pl.program_id(0)
    tn = (((0,), (0,)), ((), ()))

    @pl.when(i == 0)
    def _():
        z_s[...] = jnp.zeros_like(z_s)
        o_s[...] = jnp.zeros_like(o_s)

    z_s[...] += lax.dot_general(normed_ref[...], dz_ref[...], tn, preferred_element_type=F32)
    o_s[...] += lax.dot_general(gated_ref[...], cot_ref[...], tn, preferred_element_type=F32)
    mix = mm(gated_ref[...], w_ref[...]).astype(BF)
    half = pl.num_programs(0) // 2

    @pl.when(i < half)
    def _():
        sm_ref[...] = mix

    @pl.when(i >= half)
    def _():
        km_ref[...] = mix

    @pl.when(i == pl.num_programs(0) - 1)
    def _():
        for bit, total, keep_ref, send_ref in ((order_ref[1], z_s, kz_ref, sz_ref), (order_ref[2], o_s, ko_ref, so_ref)):
            rows = keep_ref.shape[0]
            keep_ref[...] = total[pl.ds(pl.multiple_of(bit * rows, 16), rows), :].astype(BF)
            send_ref[...] = total[pl.ds(pl.multiple_of((1 - bit) * rows, 16), rows), :].astype(BF)


def outer(bits, normed, dz, gated, cot, out_weight):
    l, d = normed.shape
    c = dz.shape[1]
    hc = 256
    nc = l // hc
    by = lambda w: pl.BlockSpec((hc, w), lambda i, order: (lax.rem(i + (1 - order[0]) * (nc // 2), nc), 0))
    full = lambda *q: pl.BlockSpec(q, lambda i, order: (0,) * len(q))
    s = jax.ShapeDtypeStruct
    v = pltpu.VMEM
    return pl.pallas_call(
        outer_kernel,
        grid_spec=pltpu.PrefetchScalarGridSpec(
            num_scalar_prefetch=1,
            grid=(nc,),
            in_specs=[by(d), by(c), by(c), by(d), full(c, d)],
            out_specs=[full(d // 2, c)] * 2 + [full(c // 2, d)] * 2 + [pl.BlockSpec((hc, d), lambda i, order: (jnp.maximum(i - nc // 2, 0), 0)), pl.BlockSpec((hc, d), lambda i, order: (jnp.minimum(i, nc // 2 - 1), 0))],
            scratch_shapes=[v((d, c), F32), v((c, d), F32)],
        ),
        out_shape=[s((d // 2, c), BF)] * 2 + [s((c // 2, d), BF)] * 2 + [s((l // 2, d), BF)] * 2,
        compiler_params=pltpu.CompilerParams(vmem_limit_bytes=60 << 20),
        cost_estimate=pl.CostEstimate(flops=6 * l * d * c, transcendentals=0, bytes_accessed=10 * l * d),
        name="outer",
    )(bits, normed, dz, gated, cot, out_weight)


def merge_kernel(kinds, bits_ref, *refs):
    take = list(refs)
    ins = [[take.pop(0) for _ in range(2 + EXTRA[kind])] for kind in kinds]
    for j, (kind, (one, two, *more)) in enumerate(zip(kinds, ins)):
        rows = one.shape[0]
        if kind == "join":
            out = take.pop(0)
            out[pl.ds(pl.multiple_of(bits_ref[j] * rows, 16), rows), :] = one[...]
            out[pl.ds(pl.multiple_of((1 - bits_ref[j]) * rows, 16), rows), :] = two[...]
        elif kind == "split":
            half = rows // 2
            for out, at in ((take.pop(0), bits_ref[j]), (take.pop(0), 1 - bits_ref[j])):
                part = pl.ds(pl.multiple_of(at * half, 16), half)
                out[...] = (one[part, :].astype(F32) + two[part, :].astype(F32)).astype(BF)
        else:
            total = one[...].astype(F32) + two[...].astype(F32)
            if kind == "shift":
                total = total + more[0][...].astype(F32)
            if kind == "norm":
                x_ref, rs_ref, gain_ref = more
                x, rs = x_ref[...].astype(F32), rs_ref[...]
                scaled = total * gain_ref[...]
                total = rs * scaled - x * (rs * rs * rs) * jnp.mean(scaled * x, axis=-1, keepdims=True)
            take.pop(0)[...] = total.astype(BF)


EXTRA = dict(join=0, split=0, sum=0, shift=1, norm=3)


def merge(items):
    kinds = tuple(item[0] for item in items)
    bits = jnp.stack([jnp.asarray(item[1], jnp.int32) for item in items])
    arrays = [v for item in items for v in item[2:]]
    shapes = []
    for kind, _, one, *_ in items:
        rows, cols = one.shape
        many = {"join": [2 * rows], "split": [rows // 2] * 2}.get(kind, [rows])
        shapes.append([jax.ShapeDtypeStruct((q, cols), BF) for q in many])
    vm = pl.BlockSpec(memory_space=pltpu.VMEM)
    flat = [q for group in shapes for q in group]
    out = list(pl.pallas_call(
        functools.partial(merge_kernel, kinds),
        in_specs=[SMEM] + [vm] * len(arrays),
        out_specs=[vm] * len(flat),
        out_shape=flat,
        compiler_params=pltpu.CompilerParams(vmem_limit_bytes=24 << 20),
        name="merge",
    )(bits, *arrays))
    return [[out.pop(0) for _ in group] for group in shapes]


def ending_kernel(bits_ref, cot_ref, na_ref, nb_ref, oa_ref, ob_ref, tok_ref, go_ref):
    for bit, one, two, out, add in ((bits_ref[0], na_ref, nb_ref, tok_ref, cot_ref), (bits_ref[1], oa_ref, ob_ref, go_ref, None)):
        rows = one.shape[0]
        for at, part in ((bit, one), (1 - bit, two)):
            where = pl.ds(pl.multiple_of(at * rows, 16), rows)
            value = part[...].astype(F32)
            out[where, :] = value if add is None else value + add[where, :].astype(F32)


def ending(bits, cot, na, nb, oa, ob):
    s = jax.ShapeDtypeStruct
    vm = pl.BlockSpec(memory_space=pltpu.VMEM)
    return pl.pallas_call(
        ending_kernel,
        in_specs=[SMEM] + [vm] * 5,
        out_specs=[vm] * 2,
        out_shape=[s(cot.shape, F32), s((2 * oa.shape[0], oa.shape[1]), F32)],
        compiler_params=pltpu.CompilerParams(vmem_limit_bytes=24 << 20),
        cost_estimate=pl.CostEstimate(flops=cot.size, transcendentals=0, bytes_accessed=12 * cot.size),
        name="ending",
    )(bits, cot, na, nb, oa, ob)


def last_kernel(n, r, p, taps, bits_ref, sa_ref, oa_ref, sb_ref, ob_ref, sz_ref, oz_ref, gin_ref, gc_ref, gcb_ref, gb_ref, gk_ref, gd_ref, gs_ref, gx_ref, a_s, b_s):
    for j, mine, other, whole_s in ((0, sa_ref, oa_ref, a_s), (1, sb_ref, ob_ref, b_s)):
        half = mine.shape[0]
        whole_s[pl.ds(pl.multiple_of(bits_ref[j] * half, 16), half), :] = mine[...]
        whole_s[pl.ds(pl.multiple_of((1 - bits_ref[j]) * half, 16), half), :] = other[...]
    lines = a_s[pl.ds(0, 16), :].astype(F32)
    gc_ref[...] = lines[:taps]
    gcb_ref[...] = lines[taps : taps + 1]
    gb_ref[...] = lines[taps + 1 : taps + 2]
    gk_ref[...] = lines[taps + 2 : taps + 3]
    gd_ref[...] = a_s[pl.ds(16, n), :].astype(F32)
    gs_ref[...] = a_s[pl.ds(16 + n, r), :].astype(F32)
    gx_ref[...] = a_s[pl.ds(16 + n + r, p), :].astype(F32)
    top = 16 + n + r + p
    half = sz_ref.shape[0]
    d = 2 * half
    cut = a_s.shape[0] - top
    gin_ref[pl.ds(0, cut), 0, :] = a_s[pl.ds(top, cut), :].astype(F32)
    gin_ref[pl.ds(cut, d - cut), 0, :] = b_s[pl.ds(0, d - cut), :].astype(F32)
    gin_ref[pl.ds(pl.multiple_of(bits_ref[2] * half, 16), half), 1, :] = sz_ref[...].astype(F32)
    gin_ref[pl.ds(pl.multiple_of((1 - bits_ref[2]) * half, 16), half), 1, :] = oz_ref[...].astype(F32)


def last(bits, sa, oa, sb, ob, sz, oz, n, r, p, taps):
    half, c = sz.shape
    s = jax.ShapeDtypeStruct
    vm = pl.BlockSpec(memory_space=pltpu.VMEM)
    return pl.pallas_call(
        functools.partial(last_kernel, n, r, p, taps),
        in_specs=[SMEM] + [vm] * 6,
        out_specs=[vm] * 8,
        out_shape=[s((2 * half, 2, c), F32), s((taps, c), F32), s((1, c), F32), s((1, c), F32), s((1, c), F32), s((n, c), F32), s((r, c), F32), s((p, c), F32)],
        scratch_shapes=[pltpu.VMEM((2 * sa.shape[0], c), BF), pltpu.VMEM((2 * sb.shape[0], c), BF)],
        compiler_params=pltpu.CompilerParams(vmem_limit_bytes=24 << 20),
        name="last",
    )(bits, sa, oa, sb, ob, sz, oz)


def front(prefix, proj, sw, bias, drive, z, dg, dlog, skip):
    l, c = drive.shape
    p = proj.shape[1]
    n = dlog.shape[0]
    ng = l // 2 // LC
    nc = l // LC
    s = jax.ShapeDtypeStruct
    fwd = lambda i: (jnp.maximum(i - ng, 0), 0)
    both = lambda i: (jnp.where(i < ng, ng - 1 - i, i - ng), 0)
    half = lambda i: (jnp.clip(i - ng, 0, ng - 1), 0)
    B = pl.BlockSpec
    lanes = c // 128
    v = pltpu.VMEM
    return pl.pallas_call(
        functools.partial(front_kernel, ng),
        grid=(ng + nc,),
        in_specs=[SMEM, B((LC, p), both), whole(*sw.shape), whole(1, c), B((LC, c), both), B((LC, c), fwd), B((LC, c), fwd), whole(n, c), whole(1, c)],
        out_specs=[B((LC, c), fwd), B((LC, c), fwd), B((LC, c), fwd), B((LC, c), fwd), B((LC * n, c), fwd), B((LC * n, c), half), B((LC * n, c), half), B((LC, p), fwd), whole(1, c)],
        out_shape=[s((l, c), BF), s((l, c), BF), s((l, c), F32), s((l, c), F32), s((l * n, c), BF), s((l // 2 * n, c), BF), s((l // 2 * n, c), BF), s((l, p), F32), s((1, c), F32)],
        scratch_shapes=[v((lanes, LC, 128), F32)] * 3 + [v((LC, c), F32), v((ng, LC, c), F32), v((n, LC), F32), v((n, LC), F32), v((LC, T * n), BF), v((LC, T * n), BF),
            v((LC // T, T * n, c), BF), v((l // 2 * n, c), BF), v((l // 2 * n, c), BF), v((c // 128, n, 256), F32), v((c // 256, n, 256), BF), v((c // 256, n, 256), F32)],
        compiler_params=pltpu.CompilerParams(vmem_limit_bytes=60 << 20),
        name="front",
    )(prefix, proj, sw, bias.reshape(1, c), drive, z, dg, dlog, skip.reshape(1, c))


def back(prefix, proj, sw_wide, drive, step, dy, hprev, ag, wg, pin, dlog, skip, carry, top, low, filled=()):
    l, c = drive.shape
    p = proj.shape[1]
    n = dlog.shape[0]
    ng = l // 2 // LC
    s = jax.ShapeDtypeStruct
    rev = lambda i: (top - i, 0)
    half = lambda i: (jnp.minimum(top - i, ng - 1), 0)
    B = pl.BlockSpec
    v = pltpu.VMEM
    ins = [SMEM, B((LC, p), rev), whole(*sw_wide.shape), B((LC, c), rev), B((LC, c), rev), B((LC, c), rev), B((LC * n, c), rev), B((LC * n, c), half), B((LC * n, c), half), B((LC, p), rev), whole(n, c), whole(1, c), whole(n, c), whole(n, c), whole(1, c)]
    steps = (top - low + 1) * LC * n * c
    return pl.pallas_call(
        functools.partial(back_kernel, ng, top, low, len(filled)),
        grid=(top - low + 1,),
        in_specs=ins + [B(memory_space=pl.ANY)] * len(filled),
        out_specs=[B((LC, p), rev), B((LC, c), rev), B((LC, c), rev), whole(n, c), whole(n, c), whole(1, c)],
        out_shape=[s((l, p), BF), s((l, c), BF), s((l, c), F32), s((n, c), F32), s((n, c), F32), s((1, c), F32)],
        input_output_aliases={len(ins) + j: j for j in range(len(filled))},
        scratch_shapes=[v((c // 128, LC, 128), F32)] * 2 + [v((c // 256, n, 256), F32), v((n, LC), F32), v((LC, T * n), BF), v((LC, T * n), BF), v((LC // T, T * n, c), BF), v((LC // T, T * n, c), BF), v((LC // T, T * n // 2, c), BF)],
        compiler_params=pltpu.CompilerParams(vmem_limit_bytes=60 << 20),
        cost_estimate=pl.CostEstimate(flops=steps * 4000, transcendentals=steps, bytes_accessed=steps * 4),
        name="back",
    )(prefix, proj, sw_wide, drive, step, dy, hprev, ag, wg, pin, dlog, skip.reshape(1, c), *carry, *filled)


def sigmoid(v):
    return 1.0 / (1.0 + jnp.exp(-v))


def exchange(value, name, size, bit):
    return lax.ppermute(value, name, [(j, j ^ (1 << bit)) for j in range(size)])


def bits_of(size):
    count = size.bit_length() - 1
    assert 1 << count == size
    return list(range(count))


class Chain:
    def __init__(self, name, size, order, keep, send, swap=True, middle=("sum", ())):
        order = list(order)
        self.name, self.size, self.keep, self.send, self.middle = name, size, keep, send, middle
        turn = [("swap", order.pop())] if swap else []
        self.steps = [("halve", bit) for bit in order] + turn + [("double", bit) for bit in reversed(order)]
        self.got = None

    def mine(self, bit):
        return (lax.axis_index(self.name) >> bit) & 1

    def start(self, send):
        self.send = send
        return exchange(send, self.name, self.size, self.steps[0][1])

    def item(self):
        kind, bit = self.steps.pop(0)
        after = self.steps[0]
        if kind == "double":
            return ("join", self.mine(bit), self.send, self.got)
        one = self.keep if kind == "halve" else self.send
        if kind == "halve" and after[0] == "halve":
            return ("split", self.mine(after[1]), one, self.got)
        if kind == "swap" or after[0] == "double":
            name, more = self.middle
            return (name, 0, one, self.got, *more)
        return ("sum", 0, one, self.got)

    def accept(self, arrays):
        self.send = arrays[-1]
        self.keep = arrays[0]
        self.got = None


def ready(chains):
    live = [c for c in chains if c.got is not None and len(c.steps) > 1]
    if live:
        for c, arrays in zip(live, merge([c.item() for c in live])):
            c.accept(arrays)


def under(chains, work, *inputs):
    chains = [c for c in chains if c.steps and c.got is None]
    sends, inputs = lax.optimization_barrier(([c.send for c in chains], inputs))
    got = [c.start(v) for c, v in zip(chains, sends)]
    result = work(*inputs)
    sends, got, result = lax.optimization_barrier((sends, got, result))
    for c, v, w in zip(chains, sends, got):
        c.send, c.got = v, w
    return result


def on_device(sizes, tokens, prefix, norm_gain, in_weight, conv_weight, conv_bias, xproj_weight, step_weight, step_bias, decay_log, skip_gain, out_weight, out_cotangent):
    dp, tp = sizes
    seqs, length, width = tokens.shape
    assert seqs == 1
    channels = in_weight.shape[2]
    rank = step_weight.shape[0]
    taps = conv_weight.shape[0]
    n = decay_log.shape[0]
    p = rank + 2 * n
    low = tokens[0]
    cot = out_cotangent[0]
    w_all = lax.optimization_barrier(in_weight.reshape(width, 2 * channels))
    xproj_t = xproj_weight.T
    order = bits_of(dp)
    turned = order[1:] + order[:1]
    t_order = bits_of(tp)
    at = lax.axis_index("tensor")
    at_dp = lax.axis_index("dp")
    spot = 0
    rows = length
    for bit in t_order:
        rows //= 2
        spot = spot + ((at >> bit) & 1) * rows
    part_of = lambda v: lax.dynamic_slice_in_dim(v, spot, rows, 0)
    bit_of = lambda v, bit: (v >> bit) & 1

    normed, xpart, drive, proj, rs = head(low, norm_gain, w_all, conv_weight, conv_bias, xproj_t)
    for bit in t_order[:-1]:
        proj = (proj.astype(F32) + exchange(proj, "tensor", tp, bit).astype(F32)).astype(BF)
    proj, n_in, c_in = lax.optimization_barrier((proj, normed, cot))
    other = exchange(proj, "tensor", tp, t_order[-1])
    zpart, dgated = gates(n_in, w_all, c_in, out_weight)
    my_x, my_rs = part_of(low), part_of(rs)
    other, zpart, dgated, my_x, my_rs = lax.optimization_barrier((other, zpart, dgated, my_x, my_rs))
    proj = (proj.astype(F32) + other.astype(F32)).astype(BF)

    gated, dz, step, dy, hprev, ag, wg, pin, g_skip = front(prefix, proj, step_weight, step_bias, drive, zpart, dgated, decay_log, skip_gain)

    picks = jnp.stack([bit_of(at, t_order[0]), bit_of(at_dp, order[0]), bit_of(at_dp, turned[0])]).astype(jnp.int32)
    kz, sz, ko, so, km, sm = outer(picks, normed, dz, gated, cot, out_weight)
    gz = Chain("dp", dp, order, kz, sz)
    go = Chain("dp", dp, turned, ko, so)
    mix = Chain("tensor", tp, t_order, km, sm, swap=False, middle=("shift", (my_x,)))
    chains = [gz, go, mix]
    wide = jnp.pad(step_weight, ((0, 2 * n), (0, 0)))
    nc = length // LC
    carry = (jnp.zeros((n, channels), F32), jnp.zeros((n, channels), F32), jnp.zeros((1, channels), F32))
    filled = ()
    top = nc - 1
    for low_chunk in PIECES:
        def piece(d, carry, filled, top=top, low_chunk=low_chunk):
            return back(prefix, proj, wide, drive, step, d, hprev, ag, wg, pin, decay_log, skip_gain, carry, top, low_chunk, filled)

        *filled, p1, a1, b1 = under(chains, piece, dy, carry, tuple(filled))
        ready(chains)
        carry = (p1, a1, b1)
        top = low_chunk - 1
    dpart, dpre, ddrive_scan = filled
    _, g_decay, g_bias = carry

    for bit in t_order[:-1]:
        dpart = (dpart.astype(F32) + exchange(dpart, "tensor", tp, bit).astype(F32)).astype(BF)
    cross = Chain("tensor", tp, t_order[-1:], dpart, dpart)
    under([cross] + chains, lambda: ())
    ready(chains)
    dproj = (cross.send.astype(F32) + cross.got.astype(F32)).astype(BF)
    total = 16 + n + p + rank + width
    total += -total % 256
    rows_a = total // 2
    ka, sa, kb, sb, lower, upper, g_norm = under(chains, lambda v: inner(rows_a, total - rows_a, picks[1:], v, ddrive_scan, xpart, drive, dz, normed, low, rs, w_all, xproj_t, conv_weight, conv_bias, g_bias, g_decay, decay_log, g_skip, proj, dpre), dproj)
    ready(chains)
    up = picks[0] == 1
    la = Chain("dp", dp, order, ka, sa)
    lb = Chain("dp", dp, turned, kb, sb)
    dn = Chain("tensor", tp, t_order, jnp.where(up, upper, lower), jnp.where(up, lower, upper), swap=False, middle=("norm", (my_x, my_rs, norm_gain.reshape(1, width))))
    turns = [("tensor", tp, bit) for bit in t_order] + [("dp", dp, bit) for bit in order]

    def gains(v):
        if turns:
            name, size, bit = turns.pop(0)
            v = v + exchange(v, name, size, bit)
        return v

    while len(la.steps) > 1:
        g_norm = under([la, lb, dn] + chains, gains, g_norm)
        ready([la, lb, dn] + chains)
    while turns:
        g_norm = gains(g_norm)
    for c in [dn] + chains:
        while c.steps and c.got is None:
            under([c], lambda: ())
            ready([c])
    flags = jnp.stack([dn.mine(dn.steps[0][1]), go.mine(go.steps[0][1])]).astype(jnp.int32)
    grad_tokens, g_out = under([la, lb], lambda v: ending(flags, v, dn.send, dn.got, go.send, go.got), cot)
    block_out = merge([mix.item()] if len(mix.steps) > 1 else [("join", mix.mine(mix.steps[0][1]), mix.send, mix.got)])[0][0]
    flags = jnp.stack([c.mine(c.steps[0][1]) for c in (la, lb, gz)]).astype(jnp.int32)
    g_in, g_conv, g_convb, g_bias, g_skip, g_decay, g_step, g_xproj = last(flags, la.send, la.got, lb.send, lb.got, gz.send, gz.got, n, rank, p, taps)
    return (block_out[None], grad_tokens[None], g_norm.reshape(-1), g_in, g_conv, g_convb[0], g_xproj.T, g_step, g_bias[0], g_decay, g_skip[0], g_out)


def solution(mesh):
    placed = (
        P("dp", None, None),
        P("dp"),
        P(),
        P(None, None, "tensor"),
        P(None, "tensor"),
        P("tensor"),
        P("tensor", None),
        P(None, "tensor"),
        P("tensor"),
        P(None, "tensor"),
        P("tensor"),
        P("tensor", None),
        P("dp", None, None),
    )
    results = (
        P("dp", None, None),
        P("dp", None, None),
        P(),
        P(None, None, "tensor"),
        P(None, "tensor"),
        P("tensor"),
        P("tensor", None),
        P(None, "tensor"),
        P("tensor"),
        P(None, "tensor"),
        P("tensor"),
        P("tensor", None),
    )
    sizes = (mesh.shape["dp"], mesh.shape["tensor"])
    return jax.shard_map(functools.partial(on_device, sizes), mesh=mesh, in_specs=placed, out_specs=results, check_vma=False)
```

```python
import functools

import jax
import jax.numpy as jnp
from jax import lax
from jax.experimental import pallas as pl
from jax.experimental.pallas import tpu as pltpu
from jax.sharding import PartitionSpec as P

T = 16
LC = 128
PIECES = (5, 2, 0)
LOG2E = 1.4426950408889634
LN2 = 0.6931471805599453
F32 = jnp.float32
BF = jnp.bfloat16
NT = (((1,), (1,)), ((), ()))
STRIDED = True
epsilon = 1e-05


def iota(shape, d):
    return lax.broadcasted_iota(jnp.int32, shape, d)


def mm(a, b):
    return jnp.dot(a, b, preferred_element_type=F32)


def mm_nt(a, b):
    return lax.dot_general(a, b, NT, preferred_element_type=F32)


def row(ref, g, t, n):
    if STRIDED:
        pair = [ref[2 * g + j, pl.ds(t, 8, stride=0), :] for j in (0, 1)]
        wide = jnp.concatenate(pair, axis=1)
        return jnp.concatenate([wide] * (n // 8), axis=0)
    pair = [jnp.broadcast_to(ref[2 * g + j, pl.ds(t, 1), :], (n, 128)) for j in (0, 1)]
    return jnp.concatenate(pair, axis=1)


def spread(base, p, n):
    return (iota((p, T * n), 0) == base + lax.rem(iota((p, T * n), 1), n)).astype(BF)


def pick(base, p, n):
    return (iota((n, p), 1) == base + iota((n, p), 0)).astype(BF)


def fold(base, p, n):
    return (iota((T * n, p), 1) == base + lax.rem(iota((T * n, p), 0), n)).astype(BF)


def blockdiag(rows, n):
    return lax.rem(iota((rows, T * n), 0), T) == lax.div(iota((rows, T * n), 1), n)


def split(ref, value):
    for g in range(value.shape[1] // 128):
        ref[g] = value[:, g * 128 : (g + 1) * 128]


def softplus(x):
    e = jnp.exp2(jnp.abs(x) * -LOG2E)
    small = e * (1.0 - e * (0.5 - e * (1.0 / 3.0 - e * 0.25)))
    return jnp.maximum(x, 0.0) + jnp.where(e < 0.03125, small, jnp.log2(1.0 + e) * LN2)


def one_minus_exp(s):
    small = s * (1.0 - s * (0.5 - s * (1.0 / 6.0 - s * (1.0 / 24.0))))
    return jnp.where(s < 0.0625, small, 1.0 - jnp.exp2(s * -LOG2E))


def front_kernel(ng, prefix_ref, proj_ref, sw_ref, bias_ref, drive_ref, z_ref, dg_ref, dlog_ref, skip_ref,
                 gated_ref, dz_ref, step_ref, dy_ref, hprev_ref, ag_ref, wg_ref, part_ref, gskip_ref,
                 step_s, sd_s, dy_s, sig_s, keep_s, bt_s, ct_s, cbd_s, rc_s, hg_s, g_s, qg_s, st_f, st_h, st_q):
    lc, c = drive_ref.shape
    p = proj_ref.shape[1]
    n = dlog_ref.shape[0]
    r = p - 2 * n
    tn = T * n
    nb = lc // T
    groups = c // 256
    i = pl.program_id(0)
    pfx = prefix_ref[0]
    rate2 = -jnp.exp(dlog_ref[...]) * LOG2E
    lanes = [slice(g * 256, (g + 1) * 256) for g in range(groups)]

    def positions(chunk):
        return iota((lc, 1), 0) + chunk * lc

    def col(ref, t0, k):
        one = jnp.broadcast_to(pltpu.roll(ref[...], lax.rem(lc - t0, lc), 1)[:, k : k + 1], (n, 128))
        return jnp.concatenate([one, one], axis=1)

    @pl.when(i == 0)
    def _():
        st_f[...] = jnp.zeros_like(st_f)
        st_h[...] = jnp.zeros_like(st_h)
        st_q[...] = jnp.zeros_like(st_q)
        gskip_ref[...] = jnp.zeros_like(gskip_ref)

    proj = proj_ref[...]
    bt_s[...] = mm_nt(pick(r, p, n), proj)

    @pl.when(i < ng)
    def _():
        chunk = ng - 1 - i
        step = softplus(mm(proj[:, :r], sw_ref[...]) + bias_ref[...])
        keep_s[chunk] = step

        @pl.when(chunk * lc < pfx)
        def _():
            mask = (positions(chunk) < pfx).astype(F32)
            split(step_s, step)
            split(sd_s, step * drive_ref[...].astype(F32) * mask)
            base = chunk * (lc * n)

            def body(ir, state):
                t0 = (nb - 1 - ir) * T
                state = list(state)
                bt = bt_s[:, t0 : t0 + T]
                for k in range(T - 1, -1, -1):
                    t = t0 + k
                    bb = jnp.broadcast_to(bt[:, k : k + 1], (n, 128))
                    bb = jnp.concatenate([bb, bb], axis=1)
                    at = pl.ds(pl.multiple_of(base + t * n, n), n)
                    for g in range(groups):
                        q = jnp.exp2(row(step_s, g, t, n) * rate2[:, lanes[g]]) * state[g]
                        state[g] = q + bb * row(sd_s, g, t, n)
                        qg_s[at, lanes[g]] = q.astype(BF)
                        g_s[at, lanes[g]] = state[g].astype(BF)
                return tuple(state)

            out = tuple(st_f[g] for g in range(groups))
            for ir in range(nb):
                out = body(ir, out)
            for g in range(groups):
                st_f[g] = out[g]

    @pl.when(i >= ng)
    def _():
        chunk = i - ng

        @pl.when(chunk < ng)
        def _():
            step_ref[...] = keep_s[jnp.minimum(chunk, ng - 1)]

        @pl.when(chunk >= ng)
        def _():
            step_ref[...] = softplus(mm(proj[:, :r], sw_ref[...]) + bias_ref[...])

        step = step_ref[...]
        drive = drive_ref[...].astype(F32)
        z = z_ref[...]
        sig = 1.0 / (1.0 + jnp.exp2(z * -LOG2E))
        sig_s[...] = sig
        dy = dg_ref[...] * (z * sig)
        dy_ref[...] = dy
        gskip_ref[...] += jnp.sum(dy * drive, axis=0, keepdims=True)
        split(step_s, step)
        split(sd_s, step * drive)
        ct_s[...] = mm_nt(pick(r + n, p, n), proj)
        cbd_s[...] = jnp.where(blockdiag(lc, n), mm(proj, spread(r + n, p, n)), 0.0).astype(BF)
        diag = blockdiag(T, n)

        def mxu(b, buf):
            rows = pl.ds(b * T, T)
            kept = {}

            def y_part(g):
                kept[g] = mm(cbd_s[rows, :], hg_s[buf, :, lanes[g]])

            def r_part(g):
                x = mm_nt(dy_ref[rows, lanes[g]].astype(BF), hg_s[buf, :, lanes[g]])
                kept["r"] = x if g == 0 else kept["r"] + x
                if g == groups - 1:
                    rc_s[rows, :] = jnp.where(diag, kept["r"], 0.0).astype(BF)

            def end(g):
                ln = lanes[g]
                y = kept[g] + skip_ref[:, ln] * drive_ref[rows, ln].astype(F32)
                zz = z_ref[rows, ln]
                sg = sig_s[rows, ln]
                gated_ref[rows, ln] = (y * (zz * sg)).astype(BF)
                dz_ref[rows, ln] = (dg_ref[rows, ln] * y * (sg * (1.0 + zz * (1.0 - sg)))).astype(BF)

            return [functools.partial(f, g) for g in range(groups) for f in (y_part, r_part, end)]

        def vpu(with_g, b, buf, state, pieces=()):
            hs, hbs, qs = (list(s) for s in state)
            pieces = list(pieces)
            t0 = b * T
            bt = bt_s[:, t0 : t0 + T]
            ct = ct_s[:, t0 : t0 + T] if with_g else None
            base = jnp.minimum(chunk, ng - 1) * (lc * n)
            for k in range(T):
                t = t0 + k
                bb = jnp.broadcast_to(bt[:, k : k + 1], (n, 128))
                bb = jnp.concatenate([bb, bb], axis=1)
                if with_g:
                    cc = jnp.broadcast_to(ct[:, k : k + 1], (n, 128))
                    cc = jnp.concatenate([cc, cc], axis=1)
                at = pl.ds(t * n, n)
                far = pl.ds(pl.multiple_of(base + t * n, n), n)
                for g in range(groups):
                    ln = lanes[g]
                    e = jnp.exp2(row(step_s, g, t, n) * rate2[:, ln])
                    hprev_ref[at, ln] = hbs[g]
                    hs[g] = e * hs[g] + bb * row(sd_s, g, t, n)
                    hbs[g] = hs[g].astype(BF)
                    if with_g:
                        hg_s[buf, pl.ds(k * n, n), ln] = hbs[g] + g_s[far, ln]
                        ag = cc * row(dy_s, g, t, n) + qs[g]
                        qs[g] = e * ag
                        agb = ag.astype(BF)
                        ag_ref[at, ln] = agb
                        wg_ref[at, ln] = agb * qg_s[far, ln]
                    else:
                        hg_s[buf, pl.ds(k * n, n), ln] = hbs[g]
                if k % 2 and pieces:
                    pieces.pop(0)()
            for f in pieces:
                f()
            return tuple(hs), tuple(hbs), tuple(qs)

        def run(with_g):
            many = range(groups)
            state = tuple(st_f[g + groups] for g in many), tuple(st_h[g] for g in many), tuple(st_q[g] for g in many)
            state = vpu(with_g, 0, 0, state)
            for b in range(1, nb):
                state = vpu(with_g, b, b, state, mxu(b - 1, b - 1))
            for f in mxu(nb - 1, nb - 1):
                f()
            for g in many:
                st_f[g + groups] = state[0][g]
                st_h[g] = state[1][g]
                st_q[g] = state[2][g]

        live = jnp.logical_and(chunk < ng, chunk * lc < pfx)

        @pl.when(live)
        def _():
            mask = (positions(chunk) < pfx).astype(F32)
            split(dy_s, dy * mask)
            run(True)

            @pl.when(pfx < (chunk + 1) * lc)
            def _():
                keep = iota((lc * n, c), 0) + chunk * (lc * n) < pfx * n
                ag_ref[...] = jnp.where(keep, ag_ref[...].astype(F32), 0.0).astype(BF)

        @pl.when(jnp.logical_not(live))
        def _():
            run(False)

        part_ref[...] = mm(rc_s[...], fold(r + n, p, n))


def back_kernel(ng, top, low, far, prefix_ref, proj_ref, sw_ref, drive_ref, step_ref, dy_ref, h_ref, pin_ref, dlog_ref, skip_ref, *refs):
    (part_ref, dpre_ref, ddrive_ref, po_ref, ao_ref, gbias_ref, step_s, dy_s, p_s, ct_s, bbd_s, rb_s, ds_s, v_s, w_s, sw_s) = refs[far:]
    lc, c = drive_ref.shape
    p = proj_ref.shape[1]
    n = dlog_ref.shape[0]
    r = p - 2 * n
    tn = T * n
    nb = lc // T
    groups = c // 256
    i = pl.program_id(0)
    chunk = top - i
    rate2 = -jnp.exp(dlog_ref[...]) * LOG2E
    rate2b = rate2.astype(BF)
    lanes = [slice(g * 256, (g + 1) * 256) for g in range(groups)]

    @pl.when(i == 0)
    def _():
        sw_s[...] = jnp.zeros_like(sw_s)
        sw_s[pl.ds(0, r), :] = sw_ref[...]
        if far >= 6:
            pc_ref, ac_ref, bc_ref = refs[far - 6 : far - 3]
            for g in range(groups):
                p_s[g] = pc_ref[:, lanes[g]]
            ao_ref[...] = ac_ref[...]
            gbias_ref[...] = bc_ref[...]
        else:
            p_s[...] = jnp.zeros_like(p_s)
            ao_ref[...] = jnp.zeros_like(ao_ref)
            gbias_ref[...] = jnp.zeros_like(gbias_ref)

    ag_ref, wg_ref = refs[:2] if low < ng else (None, None)
    proj = proj_ref[...]
    split(step_s, step_ref[...])
    split(dy_s, dy_ref[...])
    ct_s[...] = mm_nt(pick(r + n, p, n), proj)
    bbd_s[...] = jnp.where(blockdiag(lc, n), mm(proj, spread(r, p, n)), 0.0).astype(BF)
    diag = blockdiag(T, n)
    ones = diag.astype(BF)
    gather = (lax.rem(iota((n, tn // 2), 1), n) == iota((n, tn // 2), 0)).astype(BF)

    never = prefix_ref[0] < 0
    done = {}

    def vpu(with_g, b, buf, state, pieces=()):
        ps = list(state)
        seen = done.get(b + 3, {})
        pieces = list(pieces)
        held = [None] * groups
        t0 = b * T
        ct = ct_s[:, t0 : t0 + T]
        for k in range(T - 1, -1, -1):
            t = t0 + k
            for g in range(groups):
                key = {T - 1: ("s", g), T // 2: ("v", g), T // 4: ("w", g)}.get(k)
                if key in seen:
                    ps[g] = jnp.where(never, seen[key], ps[g])
            cc = jnp.broadcast_to(ct[:, k : k + 1], (n, 128))
            cc = jnp.concatenate([cc, cc], axis=1)
            at = pl.ds(t * n, n)
            for g in range(groups):
                ln = lanes[g]
                st = row(step_s, g, t, n)
                e = jnp.exp2(st * rate2[:, ln])
                ah = cc * row(dy_s, g, t, n) + ps[g]
                ps[g] = e * ah
                dsrc = ah.astype(BF)
                w = ps[g].astype(BF) * h_ref[at, ln]
                if with_g:
                    dsrc = dsrc + ag_ref[at, ln]
                    w = w + wg_ref[at, ln]
                ds_s[buf, pl.ds(k * n, n), ln] = dsrc
                v_s[buf, pl.ds(k * n, n), ln] = w * rate2b[:, ln]
                ws = w * st.astype(BF)
                if k % 2:
                    held[g] = ws
                else:
                    w_s[buf, pl.ds(k // 2 * n, n), ln] = held[g] + ws
            if k % 2 == 0 and pieces:
                pieces.pop(0)()
        for f in pieces:
            f()
        return tuple(ps)

    def mxu(b, buf):
        rows = pl.ds(b * T, T)
        kept = done[b] = {}

        def s_part(g):
            kept["s", g] = mm(bbd_s[rows, :], ds_s[buf, :, lanes[g]])

        def v_part(g):
            kept["v", g] = mm(ones, v_s[buf, :, lanes[g]])
            kept["w", g] = mm(gather, w_s[buf, :, lanes[g]])
            ao_ref[:, lanes[g]] += kept["w", g]

        def r_part(g):
            ln = lanes[g]
            sd = step_ref[rows, ln] * drive_ref[rows, ln].astype(F32)
            x = mm_nt(sd.astype(BF), ds_s[buf, :, ln])
            kept["r"] = x if g == 0 else kept["r"] + x
            if g == groups - 1:
                rb_s[rows, :] = jnp.where(diag, kept["r"], 0.0).astype(BF)

        def end(g):
            ln = lanes[g]
            step = step_ref[rows, ln]
            ssum = kept["s", g]
            drive = drive_ref[rows, ln].astype(F32)
            dpre = (kept["v", g] * LN2 + drive * ssum) * one_minus_exp(step)
            dpre_ref[rows, ln] = dpre.astype(BF)
            ddrive_ref[rows, ln] = skip_ref[:, ln] * dy_ref[rows, ln] + step * ssum
            gbias_ref[:, ln] += jnp.sum(dpre, axis=0, keepdims=True)

        return [functools.partial(f, g) for g in range(groups) for f in (s_part, v_part, r_part, end)]

    def run(with_g):
        done.clear()
        many = range(groups)
        state = tuple(p_s[g] for g in many)
        state = vpu(with_g, nb - 1, nb - 1, state)
        for b in range(nb - 2, -1, -1):
            state = vpu(with_g, b, b, state, mxu(b + 1, b + 1))
        for f in mxu(0, 0):
            f()
        for g in many:
            p_s[g] = state[g]

    if low >= ng:
        run(False)
    else:
        live = jnp.logical_and(chunk < ng, chunk * lc < prefix_ref[0])

        @pl.when(live)
        def _():
            run(True)

        @pl.when(jnp.logical_not(live))
        def _():
            run(False)

    part_ref[...] = (pin_ref[...] + mm(rb_s[...], fold(r, p, n)) + mm_nt(dpre_ref[...], sw_s[...])).astype(part_ref.dtype)
    po_ref[...] = jnp.concatenate([p_s[g] for g in range(groups)], axis=1)


def whole(*s):
    return pl.BlockSpec(s, lambda i: (0,) * len(s))


SMEM = pl.BlockSpec(memory_space=pltpu.SMEM)


def head_kernel(low_ref, gain_ref, w_ref, cw_ref, cb_ref, xw_ref, normed_ref, x_ref, slope_ref, drive_ref, part_ref, rs_ref, edge_s):
    taps = cw_ref.shape[0]
    lc = low_ref.shape[0]

    @pl.when(pl.program_id(0) == 0)
    def _():
        edge_s[...] = jnp.zeros_like(edge_s)

    xf = low_ref[...].astype(F32)
    rs = lax.rsqrt(jnp.mean(xf * xf, axis=-1, keepdims=True) + epsilon)
    rs_ref[...] = rs
    normed = (xf * rs * gain_ref[...]).astype(BF)
    normed_ref[...] = normed
    x = mm(normed, w_ref[...])
    x_ref[...] = x.astype(BF)
    wide = jnp.concatenate([edge_s[...], x], axis=0)
    edge_s[...] = x[lc - 8 :]
    out = cb_ref[...] + cw_ref[taps - 1 :, :] * x
    for k in range(taps - 1):
        at = 8 - (taps - 1) + k
        out = out + cw_ref[k : k + 1, :] * wide[at : at + lc]
    sc = sigmoid(out)
    act = out * sc
    slope_ref[...] = sc * (1.0 + out - act)
    drive = act.astype(BF)
    drive_ref[...] = drive
    part_ref[...] = mm_nt(drive, xw_ref[...]).astype(BF)


def head(low, gain, w_all, conv_weight, conv_bias, xproj_t):
    l, d = low.shape
    c = w_all.shape[1] // 2
    p = xproj_t.shape[0]
    hc = 256
    by = lambda w: pl.BlockSpec((hc, w), lambda i: (i, 0))
    s = jax.ShapeDtypeStruct
    return pl.pallas_call(
        head_kernel,
        grid=(l // hc,),
        in_specs=[by(d), whole(1, d), whole(d, c), whole(*conv_weight.shape), whole(1, c), whole(p, c)],
        out_specs=[by(d), by(c), by(c), by(c), by(p), by(1)],
        out_shape=[s((l, d), BF), s((l, c), BF), s((l, c), F32), s((l, c), BF), s((l, p), BF), s((l, 1), F32)],
        scratch_shapes=[pltpu.VMEM((8, c), F32)],
        compiler_params=pltpu.CompilerParams(vmem_limit_bytes=60 << 20),
        cost_estimate=pl.CostEstimate(flops=2 * l * d * c, transcendentals=l * c, bytes_accessed=4 * l * d + 2 * d * c + 6 * l * c),
        name="head",
    )(low, gain.reshape(1, d), w_all, conv_weight, conv_bias.reshape(1, c), xproj_t)


def gates_kernel(n_ref, w_ref, c_ref, o_ref, z_ref, dg_ref):
    z_ref[...] = mm(n_ref[...], w_ref[...])
    dg_ref[...] = mm_nt(c_ref[...], o_ref[...])


def gates(normed, w_all, cot, out_weight):
    l, d = normed.shape
    c = w_all.shape[1] // 2
    by = lambda w: pl.BlockSpec((256, w), lambda i: (i, 0))
    s = jax.ShapeDtypeStruct
    return pl.pallas_call(
        gates_kernel,
        grid=(l // 256,),
        in_specs=[by(d), pl.BlockSpec((d, c), lambda i: (0, 1)), by(d), whole(c, d)],
        out_specs=[by(c), by(c)],
        out_shape=[s((l, c), F32), s((l, c), F32)],
        compiler_params=pltpu.CompilerParams(vmem_limit_bytes=60 << 20),
        cost_estimate=pl.CostEstimate(flops=4 * l * d * c, transcendentals=0, bytes_accessed=4 * (l * d + d * c + 2 * l * c)),
        name="gates",
    )(normed, w_all, cot, out_weight)


def inner_kernel(rows_a, rows_b, bits_ref, dproj_ref, ds_ref, x_ref, slope_ref, drive_ref, dz_ref, normed_ref, low_ref, rs_ref, w_ref, xw_ref, cw_ref,
                 gb_ref, gd_ref, dlog_ref, gk_ref, proj_ref, dpre_ref, ka_ref, sa_ref, kb_ref, sb_ref, kn_ref, sn_ref, gn_ref, edge_s, gin_s, gx_s, gs_s, gc_s, gn_s, la_s, lb_s):
    taps = cw_ref.shape[0]
    lc, c = ds_ref.shape
    d = normed_ref.shape[1]
    p = dproj_ref.shape[1]
    n = gd_ref.shape[0]
    r = p - 2 * n
    i = pl.program_id(0)
    last = pl.num_programs(0) - 1
    tn = (((0,), (0,)), ((), ()))

    @pl.when(i == 0)
    def _():
        edge_s[...] = jnp.zeros_like(edge_s)
        gin_s[...] = jnp.zeros_like(gin_s)
        gx_s[...] = jnp.zeros_like(gx_s)
        gs_s[...] = jnp.zeros_like(gs_s)
        gc_s[...] = jnp.zeros_like(gc_s)
        gn_s[...] = jnp.zeros_like(gn_s)

    dproj = dproj_ref[...]
    x = x_ref[...].astype(F32)
    dconv = (ds_ref[...] + mm(dproj, xw_ref[...])) * slope_ref[...]
    gc_s[pl.ds(taps, 1), :] += jnp.sum(dconv, axis=0, keepdims=True)
    ahead = jnp.concatenate([dconv, edge_s[...]], axis=0)
    edge_s[...] = dconv[:8]
    dx = cw_ref[taps - 1 :, :] * dconv
    gc_s[pl.ds(taps - 1, 1), :] += jnp.sum(dconv * x, axis=0, keepdims=True)
    for k in range(taps - 1):
        by = taps - 1 - k
        moved = ahead[by : by + lc]
        dx = dx + cw_ref[k : k + 1, :] * moved
        gc_s[pl.ds(k, 1), :] += jnp.sum(moved * x, axis=0, keepdims=True)
    dx = dx.astype(BF)
    normed = normed_ref[...]
    gin_s[...] += lax.dot_general(normed, dx, tn, preferred_element_type=F32)
    gx_s[...] += lax.dot_general(dproj, drive_ref[...], tn, preferred_element_type=F32)
    gs_s[...] += lax.dot_general(proj_ref[:, :r], dpre_ref[...], tn, preferred_element_type=F32)
    dn = mm_nt(jnp.concatenate([dx, dz_ref[...]], axis=1), w_ref[...])
    half = pl.num_programs(0) // 2

    keeps = (i < half) == (bits_ref[2] == 1)

    @pl.when(jnp.logical_not(keeps))
    def _():
        sn_ref[...] = dn.astype(BF)

    @pl.when(keeps)
    def _():
        kn_ref[...] = dn.astype(BF)

    gn_s[...] += jnp.sum(dn * (low_ref[...].astype(F32) * rs_ref[...]), axis=0, keepdims=True)

    @pl.when(i == last)
    def _():
        gn_ref[...] = gn_s[...]
        lines = [gc_s[pl.ds(0, taps + 1), :], gb_ref[...], gk_ref[...]]
        lines = jnp.concatenate(lines + [jnp.zeros((16 - taps - 3, c), F32)], axis=0)
        top = 16 + n + r + p
        la_s[pl.ds(0, 16), :] = lines.astype(BF)
        la_s[pl.ds(16, n), :] = (gd_ref[...] * -jnp.exp(dlog_ref[...])).astype(BF)
        la_s[pl.ds(16 + n, r), :] = gs_s[...].astype(BF)
        la_s[pl.ds(16 + n + r, p), :] = gx_s[...].astype(BF)
        la_s[pl.ds(top, rows_a - top), :] = gin_s[pl.ds(0, rows_a - top), :].astype(BF)
        rest = d - (rows_a - top)
        lb_s[pl.ds(0, rest), :] = gin_s[pl.ds(rows_a - top, rest), :].astype(BF)
        if rows_b > rest:
            lb_s[pl.ds(rest, rows_b - rest), :] = jnp.zeros((rows_b - rest, c), BF)
        for bit, total, keep_ref, send_ref in ((bits_ref[0], la_s, ka_ref, sa_ref), (bits_ref[1], lb_s, kb_ref, sb_ref)):
            rows = keep_ref.shape[0]
            keep_ref[...] = total[pl.ds(pl.multiple_of(bit * rows, 8), rows), :]
            send_ref[...] = total[pl.ds(pl.multiple_of((1 - bit) * rows, 8), rows), :]


def inner(rows_a, rows_b, bits, dproj, ddrive, x, slope, drive, dz, normed, low, rs, w_all, xproj_t, conv_weight, g_bias, g_decay, decay_log, g_skip, proj, dpre):
    l, c = x.shape
    d = normed.shape[1]
    p = dproj.shape[1]
    n = g_decay.shape[0]
    hc = 256
    nc = l // hc
    by = lambda w: pl.BlockSpec((hc, w), lambda i, bits: (nc - 1 - i, 0))
    full = lambda *q: pl.BlockSpec(q, lambda i, bits: (0,) * len(q))
    s = jax.ShapeDtypeStruct
    v = pltpu.VMEM
    early = lambda i: jnp.maximum(nc // 2 - 1 - i, 0)
    late = lambda i: jnp.minimum(nc - 1 - i, nc // 2 - 1)
    kept = pl.BlockSpec((hc, d), lambda i, bits: (jnp.where(bits[2] == 1, early(i), late(i)), 0))
    sent = pl.BlockSpec((hc, d), lambda i, bits: (jnp.where(bits[2] == 1, late(i), early(i)), 0))
    return pl.pallas_call(
        functools.partial(inner_kernel, rows_a, rows_b),
        grid_spec=pltpu.PrefetchScalarGridSpec(
            num_scalar_prefetch=1,
            grid=(nc,),
            in_specs=[by(p), by(c), by(c), by(c), by(c), by(c), by(d), by(d), by(1), full(d, 2 * c), full(p, c), full(*conv_weight.shape),
                      full(1, c), full(n, c), full(n, c), full(1, c), by(p), by(c)],
            out_specs=[full(rows_a // 2, c)] * 2 + [full(rows_b // 2, c)] * 2 + [kept, sent, full(1, d)],
            scratch_shapes=[v((8, c), F32), v((d, c), F32), v((p, c), F32), v((p - 2 * n, c), F32), v((8, c), F32), v((1, d), F32), v((rows_a, c), BF), v((rows_b, c), BF)],
        ),
        out_shape=[s((rows_a // 2, c), BF)] * 2 + [s((rows_b // 2, c), BF)] * 2 + [s((l // 2, d), BF)] * 2 + [s((1, d), F32)],
        compiler_params=pltpu.CompilerParams(vmem_limit_bytes=60 << 20),
        cost_estimate=pl.CostEstimate(flops=6 * l * d * c, transcendentals=l * c, bytes_accessed=10 * l * d),
        name="inner",
    )(bits, dproj, ddrive, x, slope, drive, dz, normed, low, rs, w_all, xproj_t, conv_weight, g_bias, g_decay, decay_log, g_skip, proj, dpre)


def outer_kernel(order_ref, normed_ref, dz_ref, cols_ref, cot_ref, rows_ref, low_ref, w_ref, kz_ref, sz_ref, ko_ref, so_ref, km_ref, sm_ref):
    tn = (((0,), (0,)), ((), ()))
    for step, z_ref, o_ref, m_ref in ((0, sz_ref, so_ref, sm_ref), (1, kz_ref, ko_ref, km_ref)):
        @pl.when(pl.program_id(0) == step)
        def _(z_ref=z_ref, o_ref=o_ref, m_ref=m_ref):
            z_ref[...] = lax.dot_general(normed_ref[...], dz_ref[...], tn, preferred_element_type=F32).astype(BF)
            o_ref[...] = lax.dot_general(cols_ref[...], cot_ref[...], tn, preferred_element_type=F32).astype(BF)
            mix = mm(rows_ref[...], w_ref[...])
            m_ref[...] = (mix + jnp.where(order_ref[3] == 0, low_ref[...].astype(F32), 0.0)).astype(BF)


def outer(bits, normed, dz, gated, cot, low, out_weight):
    l, d = normed.shape
    c = dz.shape[1]
    full = lambda *q: pl.BlockSpec(q, lambda i, order: (0,) * len(q))
    half = lambda w, j: pl.BlockSpec((l, w // 2), lambda i, order: (0, lax.rem(i + 1 + order[j], 2)))
    rows = lambda w: pl.BlockSpec((l // 2, w), lambda i, order: (lax.rem(i + 1 + order[2], 2), 0))
    s = jax.ShapeDtypeStruct
    return pl.pallas_call(
        outer_kernel,
        grid_spec=pltpu.PrefetchScalarGridSpec(
            num_scalar_prefetch=1,
            grid=(2,),
            in_specs=[half(d, 0), full(l, c), half(c, 1), full(l, d), rows(c), rows(d), full(c, d)],
            out_specs=[full(d // 2, c)] * 2 + [full(c // 2, d)] * 2 + [full(l // 2, d)] * 2,
        ),
        out_shape=[s((d // 2, c), BF)] * 2 + [s((c // 2, d), BF)] * 2 + [s((l // 2, d), BF)] * 2,
        compiler_params=pltpu.CompilerParams(vmem_limit_bytes=60 << 20),
        cost_estimate=pl.CostEstimate(flops=6 * l * d * c, transcendentals=0, bytes_accessed=10 * l * d),
        name="outer",
    )(bits, normed, dz, gated, cot, gated, low, out_weight)


def merge_kernel(kinds, bits_ref, *refs):
    take = list(refs)
    ins = [[take.pop(0) for _ in range(2 + EXTRA[kind])] for kind in kinds]
    for j, (kind, (one, two, *more)) in enumerate(zip(kinds, ins)):
        rows = one.shape[0]
        if kind == "join":
            out = take.pop(0)
            out[pl.ds(pl.multiple_of(bits_ref[j] * rows, 8), rows), :] = one[...]
            out[pl.ds(pl.multiple_of((1 - bits_ref[j]) * rows, 8), rows), :] = two[...]
        elif kind == "split":
            half = rows // 2
            for out, at in ((take.pop(0), bits_ref[j]), (take.pop(0), 1 - bits_ref[j])):
                part = pl.ds(pl.multiple_of(at * half, 8), half)
                out[...] = (one[part, :].astype(F32) + two[part, :].astype(F32)).astype(BF)
        else:
            total = one[...].astype(F32) + two[...].astype(F32)
            if kind == "shift":
                total = total + more[0][...].astype(F32)
            if kind == "norm":
                x_ref, rs_ref, gain_ref = more
                x, rs = x_ref[...].astype(F32), rs_ref[...]
                scaled = total * gain_ref[...]
                total = rs * scaled - x * (rs * rs * rs) * jnp.mean(scaled * x, axis=-1, keepdims=True)
            take.pop(0)[...] = total.astype(BF)


EXTRA = dict(join=0, split=0, sum=0, shift=1, norm=3)


def once(*shape):
    return pl.BlockSpec(shape, lambda i: (0,) * len(shape), pipeline_mode=pl.Buffered(1))


def merge(items):
    kinds = tuple(item[0] for item in items)
    bits = jnp.stack([jnp.asarray(item[1], jnp.int32) for item in items])
    arrays = [v for item in items for v in item[2:]]
    shapes = []
    for kind, _, one, *_ in items:
        rows, cols = one.shape
        many = {"join": [2 * rows], "split": [rows // 2] * 2}.get(kind, [rows])
        shapes.append([jax.ShapeDtypeStruct((q, cols), BF) for q in many])
    flat = [q for group in shapes for q in group]
    homes = [len(group) == 2 and j == 0 for group in shapes for j in range(len(group))]
    out = list(pl.pallas_call(
        functools.partial(merge_kernel, kinds),
        grid=(1,),
        in_specs=[SMEM] + [once(*v.shape) for v in arrays],
        out_specs=[once(*v.shape) for v in flat],
        out_shape=[pltpu.HBM(q.shape, q.dtype) if kept else q for q, kept in zip(flat, homes)],
        compiler_params=pltpu.CompilerParams(vmem_limit_bytes=24 << 20),
        name="merge",
    )(bits, *arrays))
    return [[out.pop(0) for _ in group] for group in shapes]


def ending_kernel(bits_ref, cot_ref, na_ref, nb_ref, oa_ref, ob_ref, tok_ref, go_ref):
    for bit, one, two, out, add in ((bits_ref[0], na_ref, nb_ref, tok_ref, cot_ref), (bits_ref[1], oa_ref, ob_ref, go_ref, None)):
        rows = one.shape[0]
        for at, part in ((bit, one), (1 - bit, two)):
            where = pl.ds(pl.multiple_of(at * rows, 8), rows)
            value = part[...].astype(F32)
            out[where, :] = value if add is None else value + add[where, :].astype(F32)


def ending(bits, cot, na, nb, oa, ob):
    s = jax.ShapeDtypeStruct
    vm = pl.BlockSpec(memory_space=pltpu.VMEM)
    return pl.pallas_call(
        ending_kernel,
        in_specs=[SMEM] + [vm] * 5,
        out_specs=[vm] * 2,
        out_shape=[s(cot.shape, F32), s((2 * oa.shape[0], oa.shape[1]), F32)],
        compiler_params=pltpu.CompilerParams(vmem_limit_bytes=24 << 20),
        cost_estimate=pl.CostEstimate(flops=cot.size, transcendentals=0, bytes_accessed=12 * cot.size),
        name="ending",
    )(bits, cot, na, nb, oa, ob)


def last_kernel(n, r, p, taps, bits_ref, sa_ref, oa_ref, sb_ref, ob_ref, sz_ref, oz_ref, gin_ref, gc_ref, gcb_ref, gb_ref, gk_ref, gd_ref, gs_ref, gx_ref, a_s, b_s):
    for j, mine, other, whole_s in ((0, sa_ref, oa_ref, a_s), (1, sb_ref, ob_ref, b_s)):
        half = mine.shape[0]
        whole_s[pl.ds(pl.multiple_of(bits_ref[j] * half, 8), half), :] = mine[...]
        whole_s[pl.ds(pl.multiple_of((1 - bits_ref[j]) * half, 8), half), :] = other[...]
    lines = a_s[pl.ds(0, 16), :].astype(F32)
    gc_ref[...] = lines[:taps]
    gcb_ref[...] = lines[taps : taps + 1]
    gb_ref[...] = lines[taps + 1 : taps + 2]
    gk_ref[...] = lines[taps + 2 : taps + 3]
    gd_ref[...] = a_s[pl.ds(16, n), :].astype(F32)
    gs_ref[...] = a_s[pl.ds(16 + n, r), :].astype(F32)
    gx_ref[...] = a_s[pl.ds(16 + n + r, p), :].astype(F32)
    top = 16 + n + r + p
    half = sz_ref.shape[0]
    d = 2 * half
    cut = a_s.shape[0] - top
    gin_ref[pl.ds(0, cut), 0, :] = a_s[pl.ds(top, cut), :].astype(F32)
    gin_ref[pl.ds(cut, d - cut), 0, :] = b_s[pl.ds(0, d - cut), :].astype(F32)
    gin_ref[pl.ds(pl.multiple_of(bits_ref[2] * half, 8), half), 1, :] = sz_ref[...].astype(F32)
    gin_ref[pl.ds(pl.multiple_of((1 - bits_ref[2]) * half, 8), half), 1, :] = oz_ref[...].astype(F32)


def last(bits, sa, oa, sb, ob, sz, oz, n, r, p, taps):
    half, c = sz.shape
    s = jax.ShapeDtypeStruct
    vm = pl.BlockSpec(memory_space=pltpu.VMEM)
    return pl.pallas_call(
        functools.partial(last_kernel, n, r, p, taps),
        in_specs=[SMEM] + [vm] * 6,
        out_specs=[vm] * 8,
        out_shape=[s((2 * half, 2, c), F32), s((taps, c), F32), s((1, c), F32), s((1, c), F32), s((1, c), F32), s((n, c), F32), s((r, c), F32), s((p, c), F32)],
        scratch_shapes=[pltpu.VMEM((2 * sa.shape[0], c), BF), pltpu.VMEM((2 * sb.shape[0], c), BF)],
        compiler_params=pltpu.CompilerParams(vmem_limit_bytes=24 << 20),
        name="last",
    )(bits, sa, oa, sb, ob, sz, oz)


def front(prefix, proj, sw, bias, drive, z, dg, dlog, skip):
    l, c = drive.shape
    p = proj.shape[1]
    n = dlog.shape[0]
    ng = l // 2 // LC
    nc = l // LC
    s = jax.ShapeDtypeStruct
    fwd = lambda i: (jnp.maximum(i - ng, 0), 0)
    both = lambda i: (jnp.where(i < ng, ng - 1 - i, i - ng), 0)
    half = lambda i: (jnp.clip(i - ng, 0, ng - 1), 0)
    B = pl.BlockSpec
    lanes = c // 128
    v = pltpu.VMEM
    return pl.pallas_call(
        functools.partial(front_kernel, ng),
        grid=(ng + nc,),
        in_specs=[SMEM, B((LC, p), both), whole(*sw.shape), whole(1, c), B((LC, c), both), B((LC, c), fwd), B((LC, c), fwd), whole(n, c), whole(1, c)],
        out_specs=[B((LC, c), fwd), B((LC, c), fwd), B((LC, c), fwd), B((LC, c), fwd), B((LC * n, c), fwd), B((LC * n, c), half), B((LC * n, c), half), B((LC, p), fwd), whole(1, c)],
        out_shape=[s((l, c), BF), s((l, c), BF), s((l, c), F32), s((l, c), F32), s((l * n, c), BF), s((l // 2 * n, c), BF), s((l // 2 * n, c), BF), s((l, p), F32), s((1, c), F32)],
        scratch_shapes=[v((lanes, LC, 128), F32)] * 3 + [v((LC, c), F32), v((ng, LC, c), F32), v((n, LC), F32), v((n, LC), F32), v((LC, T * n), BF), v((LC, T * n), BF),
            v((LC // T, T * n, c), BF), v((l // 2 * n, c), BF), v((l // 2 * n, c), BF), v((c // 128, n, 256), F32), v((c // 256, n, 256), BF), v((c // 256, n, 256), F32)],
        compiler_params=pltpu.CompilerParams(vmem_limit_bytes=60 << 20),
        name="front",
    )(prefix, proj, sw, bias.reshape(1, c), drive, z, dg, dlog, skip.reshape(1, c))


def back(prefix, proj, sw, drive, step, dy, hprev, ag, wg, pin, dlog, skip, carry, top, low, filled=()):
    l, c = drive.shape
    p = proj.shape[1]
    n = dlog.shape[0]
    ng = l // 2 // LC
    s = jax.ShapeDtypeStruct
    rev = lambda i: (top - i, 0)
    half = lambda i: (jnp.minimum(top - i, ng - 1), 0)
    B = pl.BlockSpec
    v = pltpu.VMEM
    ins = [SMEM, B((LC, p), rev), whole(*sw.shape), B((LC, c), rev), B((LC, c), rev), B((LC, c), rev), B((LC * n, c), rev), B((LC, p), rev), whole(n, c), whole(1, c)]
    extra, more = [], []
    if low < ng:
        extra, more = [ag, wg], [B((LC * n, c), half)] * 2
    if filled:
        extra, more = extra + list(carry) + list(filled), more + [whole(n, c), whole(n, c), whole(1, c)] + [B(memory_space=pl.ANY)] * 3
    first = len(ins) + len(extra) - 3
    return pl.pallas_call(
        functools.partial(back_kernel, ng, top, low, len(extra)),
        grid=(top - low + 1,),
        in_specs=ins + more,
        out_specs=[B((LC, p), rev), B((LC, c), rev), B((LC, c), rev), whole(n, c), whole(n, c), whole(1, c)],
        out_shape=[s((l, p), BF), s((l, c), BF), s((l, c), F32), s((n, c), F32), s((n, c), F32), s((1, c), F32)],
        input_output_aliases={first + j: j for j in range(3)} if filled else {},
        scratch_shapes=[v((c // 128, LC, 128), F32)] * 2 + [v((c // 256, n, 256), F32), v((n, LC), F32), v((LC, T * n), BF), v((LC, T * n), BF), v((LC // T, T * n, c), BF), v((LC // T, T * n, c), BF), v((LC // T, T * n // 2, c), BF), v((p, c), BF)],
        compiler_params=pltpu.CompilerParams(vmem_limit_bytes=60 << 20),
        cost_estimate=pl.CostEstimate(flops=(top - low + 1) * LC * n * c * 4000, transcendentals=0, bytes_accessed=(top - low + 1) * LC * n * c * 4),
        name="back",
    )(prefix, proj, sw, drive, step, dy, hprev, pin, dlog, skip.reshape(1, c), *extra)


def sigmoid(v):
    return 1.0 / (1.0 + jnp.exp(-v))


def exchange(value, name, size, bit):
    return lax.ppermute(value, name, [(j, j ^ (1 << bit)) for j in range(size)])


def bits_of(size):
    count = size.bit_length() - 1
    assert 1 << count == size
    return list(range(count))


class Chain:
    def __init__(self, name, size, order, keep, send, swap=True, middle=("sum", ())):
        order = list(order)
        self.name, self.size, self.keep, self.send, self.middle = name, size, keep, send, middle
        turn = [("swap", order.pop())] if swap else []
        self.steps = [("halve", bit) for bit in order] + turn + [("double", bit) for bit in reversed(order)]
        self.got = None

    def mine(self, bit):
        return (lax.axis_index(self.name) >> bit) & 1

    def start(self, send):
        self.send = send
        return exchange(send, self.name, self.size, self.steps[0][1])

    def item(self):
        kind, bit = self.steps.pop(0)
        after = self.steps[0]
        if kind == "double":
            return ("join", self.mine(bit), self.send, self.got)
        one = pltpu.with_memory_space_constraint(self.keep, pltpu.HBM) if kind == "halve" else self.send
        if kind == "halve" and after[0] == "halve":
            return ("split", self.mine(after[1]), one, self.got)
        if kind == "swap" or after[0] == "double":
            name, more = self.middle
            return (name, 0, one, self.got, *more)
        return ("sum", 0, one, self.got)

    def ended(self):
        return len(self.steps) == 1 and self.got is not None

    def accept(self, arrays):
        self.send = arrays[-1]
        self.keep = arrays[0]
        self.got = None


def ready(chains):
    live = [c for c in chains if c.got is not None and len(c.steps) > 1 and c not in PENDING]
    if live:
        for c, arrays in zip(live, merge([c.item() for c in live])):
            c.accept(arrays)


PENDING = []


def under(chains, work, *inputs, slow=()):
    waiting = [c for c in PENDING if c.got is not None]
    PENDING[:] = list(slow)
    chains = [c for c in chains if c.steps and c.got is None] + list(slow)
    sends, inputs = lax.optimization_barrier(([c.send for c in chains], inputs))
    got = [c.start(v) for c, v in zip(chains, sends)]
    result = work(*inputs)
    hold = len(chains) - len(slow)
    old = [c.got for c in waiting]
    heads, firsts, old, result = lax.optimization_barrier((sends[:hold], got[:hold], old, result))
    for c, v, w in zip(chains, list(heads) + list(sends[hold:]), list(firsts) + list(got[hold:])):
        c.send, c.got = v, w
    for c, w in zip(waiting, old):
        c.got = w
    return result


def on_device(sizes, tokens, prefix, norm_gain, in_weight, conv_weight, conv_bias, xproj_weight, step_weight, step_bias, decay_log, skip_gain, out_weight, out_cotangent):
    dp, tp = sizes
    seqs, length, width = tokens.shape
    assert seqs == 1
    channels = in_weight.shape[2]
    rank = step_weight.shape[0]
    taps = conv_weight.shape[0]
    n = decay_log.shape[0]
    p = rank + 2 * n
    low = tokens[0]
    cot = out_cotangent[0]
    w_all = lax.optimization_barrier(in_weight.reshape(width, 2 * channels))
    xproj_t = xproj_weight.T
    order = bits_of(dp)
    turned = order[1:] + order[:1]
    t_order = bits_of(tp)
    at = lax.axis_index("tensor")
    at_dp = lax.axis_index("dp")
    spot = 0
    rows = length
    for bit in t_order:
        rows //= 2
        spot = spot + ((at >> bit) & 1) * rows
    part_of = lambda v: lax.dynamic_slice_in_dim(v, spot, rows, 0)
    bit_of = lambda v, bit: (v >> bit) & 1

    normed, xpart, slope, drive, proj, rs = head(low, norm_gain, w_all, conv_weight, conv_bias, xproj_t)
    for bit in t_order[:-1]:
        proj = (proj.astype(F32) + exchange(proj, "tensor", tp, bit).astype(F32)).astype(BF)
    proj, n_in, c_in = lax.optimization_barrier((proj, normed, cot))
    other = exchange(proj, "tensor", tp, t_order[-1])
    zpart, dgated = gates(n_in, w_all, c_in, out_weight)
    other, zpart, dgated = lax.optimization_barrier((other, zpart, dgated))
    proj = (proj.astype(F32) + other.astype(F32)).astype(BF)

    gated, dz, step, dy, hprev, ag, wg, pin, g_skip = front(prefix, proj, step_weight, step_bias, drive, zpart, dgated, decay_log, skip_gain)

    picks = jnp.stack([bit_of(at_dp, order[0]), bit_of(at_dp, turned[0]), bit_of(at, t_order[0]), at]).astype(jnp.int32)
    kz, sz, ko, so, km, sm = outer(picks, normed, dz, gated, cot, low, out_weight)
    gz = Chain("dp", dp, order, kz, sz)
    go = Chain("dp", dp, turned, ko, so)
    mix = Chain("tensor", tp, t_order, km, sm, swap=False)
    chains = [gz, go, mix]
    nc = length // LC
    carry = ()
    filled = ()
    top = nc - 1
    for low_chunk in PIECES:
        def piece(d, carry, filled, top=top, low_chunk=low_chunk):
            return back(prefix, proj, step_weight, drive, step, d, hprev, ag, wg, pin, decay_log, skip_gain, carry, top, low_chunk, filled)

        *filled, p1, a1, b1 = under(chains, piece, dy, carry, tuple(filled))
        ready(chains)
        carry = (p1, a1, b1)
        top = low_chunk - 1
    dpart, dpre, ddrive_scan = filled
    _, g_decay, g_bias = carry

    for bit in t_order[:-1]:
        dpart = (dpart.astype(F32) + exchange(dpart, "tensor", tp, bit).astype(F32)).astype(BF)
    cross = Chain("tensor", tp, t_order[-1:], dpart, dpart)
    my_x, my_rs = under([cross, mix], lambda v, w: (part_of(v), part_of(w)), low, rs)
    dproj = (cross.send.astype(F32) + cross.got.astype(F32)).astype(BF)
    total = 16 + n + p + rank + width
    total += -total % (16 << (len(order) - 1))
    rows_a = total // 2
    ka, sa, kb, sb, kn, sn, g_norm = under([gz, go], lambda v: inner(rows_a, total - rows_a, picks, v, ddrive_scan, xpart, slope, drive, dz, normed, low, rs, w_all, xproj_t, conv_weight, g_bias, g_decay, decay_log, g_skip, proj, dpre), dproj)
    la = Chain("dp", dp, order, ka, sa)
    lb = Chain("dp", dp, turned, kb, sb)
    dn = Chain("tensor", tp, t_order, kn, sn, swap=False, middle=("norm", (my_x, my_rs, norm_gain.reshape(1, width))))
    turns = [("tensor", tp, bit) for bit in reversed(t_order)] + [("dp", dp, bit) for bit in order]

    def gains(v):
        if turns:
            name, size, bit = turns.pop(0)
            v = v + exchange(v, name, size, bit)
        return v

    late = [[], [gz], [go]]
    while not la.ended():
        extra = late.pop(0) if late else [c for c in (gz, go) if not c.ended()]
        ready(extra + [la, lb, dn])
        final = len(la.steps) == 1
        slow = [dn] if dn.got is None and len(dn.steps) > 1 and dn.steps[0][1] != t_order[0] else []
        now = [dn] if dn.got is None and not slow and not final else []
        g_norm = under([la, lb] + now + extra, gains, g_norm, slow=slow)
    while turns:
        g_norm = gains(g_norm)
    for c in (dn, gz, go):
        while not c.ended():
            ready([c])
            under([c], lambda: ())
    flags = jnp.stack([c.mine(c.steps[0][1]) for c in (la, lb, gz)]).astype(jnp.int32)
    g_in, g_conv, g_convb, g_bias, g_skip, g_decay, g_step, g_xproj = last(flags, la.send, la.got, lb.send, lb.got, gz.send, gz.got, n, rank, p, taps)
    flags = jnp.stack([dn.mine(dn.steps[0][1]), go.mine(go.steps[0][1])]).astype(jnp.int32)
    grad_tokens, g_out = ending(flags, cot, dn.send, dn.got, go.send, go.got)
    block_out = merge([mix.item()] if len(mix.steps) > 1 else [("join", mix.mine(mix.steps[0][1]), mix.send, mix.got)])[0][0]
    return (block_out[None], grad_tokens[None], g_norm.reshape(-1), g_in, g_conv, g_convb[0], g_xproj.T, g_step, g_bias[0], g_decay, g_skip[0], g_out)


def solution(mesh):
    placed = (
        P("dp", None, None),
        P("dp"),
        P(),
        P(None, None, "tensor"),
        P(None, "tensor"),
        P("tensor"),
        P("tensor", None),
        P(None, "tensor"),
        P("tensor"),
        P(None, "tensor"),
        P("tensor"),
        P("tensor", None),
        P("dp", None, None),
    )
    results = (
        P("dp", None, None),
        P("dp", None, None),
        P(),
        P(None, None, "tensor"),
        P(None, "tensor"),
        P("tensor"),
        P("tensor", None),
        P(None, "tensor"),
        P("tensor"),
        P(None, "tensor"),
        P("tensor"),
        P("tensor", None),
    )
    sizes = (mesh.shape["dp"], mesh.shape["tensor"])
    return jax.shard_map(functools.partial(on_device, sizes), mesh=mesh, in_specs=placed, out_specs=results, check_vma=False)
```

```python
import functools

import jax
import jax.numpy as jnp
from jax import lax
from jax.experimental import pallas as pl
from jax.experimental.pallas import tpu as pltpu
from jax.sharding import PartitionSpec as P

T = 16
LC = 128
PIECES = (5, 2, 0)
LOG2E = 1.4426950408889634
LN2 = 0.6931471805599453
F32 = jnp.float32
BF = jnp.bfloat16
NT = (((1,), (1,)), ((), ()))
STRIDED = True
epsilon = 1e-05


def iota(shape, d):
    return lax.broadcasted_iota(jnp.int32, shape, d)


def mm(a, b):
    return jnp.dot(a, b, preferred_element_type=F32)


def mm_nt(a, b):
    return lax.dot_general(a, b, NT, preferred_element_type=F32)


def row(ref, g, t, n):
    if STRIDED:
        pair = [ref[2 * g + j, pl.ds(t, 8, stride=0), :] for j in (0, 1)]
        wide = jnp.concatenate(pair, axis=1)
        return jnp.concatenate([wide] * (n // 8), axis=0)
    pair = [jnp.broadcast_to(ref[2 * g + j, pl.ds(t, 1), :], (n, 128)) for j in (0, 1)]
    return jnp.concatenate(pair, axis=1)


def spread(base, p, n):
    return (iota((p, T * n), 0) == base + lax.rem(iota((p, T * n), 1), n)).astype(BF)


def pick(base, p, n):
    return (iota((n, p), 1) == base + iota((n, p), 0)).astype(BF)


def fold(base, p, n):
    return (iota((T * n, p), 1) == base + lax.rem(iota((T * n, p), 0), n)).astype(BF)


def blockdiag(rows, n):
    return lax.rem(iota((rows, T * n), 0), T) == lax.div(iota((rows, T * n), 1), n)


def split(ref, value):
    for g in range(value.shape[1] // 128):
        ref[g] = value[:, g * 128 : (g + 1) * 128]


def softplus(x):
    e = jnp.exp2(jnp.abs(x) * -LOG2E)
    small = e * (1.0 - e * (0.5 - e * (1.0 / 3.0 - e * 0.25)))
    return jnp.maximum(x, 0.0) + jnp.where(e < 0.03125, small, jnp.log2(1.0 + e) * LN2)


def one_minus_exp(s):
    small = s * (1.0 - s * (0.5 - s * (1.0 / 6.0 - s * (1.0 / 24.0))))
    return jnp.where(s < 0.0625, small, 1.0 - jnp.exp2(s * -LOG2E))


def front_kernel(ng, nc, order_ref, proj_ref, sw_ref, bias_ref, drive_ref, z_ref, dg_ref, dlog_ref, skip_ref, normed_hbm, cot_hbm, low_hbm, w_hbm,
                 gated_ref, dz_ref, step_ref, dy_ref, hprev_ref, ag_ref, wg_ref, part_ref, gskip_ref, kz_ref, sz_ref, ko_ref, so_ref, km_ref, sm_ref,
                 step_s, sd_s, dy_s, sig_s, keep_s, bt_s, ct_s, cbd_s, rc_s, hg_s, g_s, qg_s, st_f, st_h, st_q, gated_s, dzs_s, normed_ref, cot_ref, low_ref, w_ref, sems):
    lc, c = drive_ref.shape
    p = proj_ref.shape[1]
    n = dlog_ref.shape[0]
    r = p - 2 * n
    tn = T * n
    nb = lc // T
    groups = c // 256
    i = pl.program_id(0)
    pfx = order_ref[4]
    rate2 = -jnp.exp(dlog_ref[...]) * LOG2E
    lanes = [slice(g * 256, (g + 1) * 256) for g in range(groups)]

    def positions(chunk):
        return iota((lc, 1), 0) + chunk * lc

    def col(ref, t0, k):
        one = jnp.broadcast_to(pltpu.roll(ref[...], lax.rem(lc - t0, lc), 1)[:, k : k + 1], (n, 128))
        return jnp.concatenate([one, one], axis=1)

    @pl.when(i == 0)
    def _():
        st_f[...] = jnp.zeros_like(st_f)
        st_h[...] = jnp.zeros_like(st_h)
        st_q[...] = jnp.zeros_like(st_q)
        gskip_ref[...] = jnp.zeros_like(gskip_ref)

    proj = proj_ref[...]
    bt_s[...] = mm_nt(pick(r, p, n), proj)

    @pl.when(i < ng)
    def _():
        chunk = ng - 1 - i
        step = softplus(mm(proj[:, :r], sw_ref[...]) + bias_ref[...])
        keep_s[chunk] = step

        @pl.when(chunk * lc < pfx)
        def _():
            mask = (positions(chunk) < pfx).astype(F32)
            split(step_s, step)
            split(sd_s, step * drive_ref[...].astype(F32) * mask)
            base = chunk * (lc * n)

            def body(ir, state):
                t0 = (nb - 1 - ir) * T
                state = list(state)
                bt = bt_s[:, t0 : t0 + T]
                for k in range(T - 1, -1, -1):
                    t = t0 + k
                    bb = jnp.broadcast_to(bt[:, k : k + 1], (n, 128))
                    bb = jnp.concatenate([bb, bb], axis=1)
                    at = pl.ds(pl.multiple_of(base + t * n, n), n)
                    for g in range(groups):
                        q = jnp.exp2(row(step_s, g, t, n) * rate2[:, lanes[g]]) * state[g]
                        state[g] = q + bb * row(sd_s, g, t, n)
                        qg_s[at, lanes[g]] = q.astype(BF)
                        g_s[at, lanes[g]] = state[g].astype(BF)
                return tuple(state)

            out = tuple(st_f[g] for g in range(groups))
            for ir in range(nb):
                out = body(ir, out)
            for g in range(groups):
                st_f[g] = out[g]

    @pl.when(jnp.logical_and(i >= ng, i < ng + nc))
    def _():
        chunk = i - ng

        @pl.when(chunk < ng)
        def _():
            step_ref[...] = keep_s[jnp.minimum(chunk, ng - 1)]

        @pl.when(chunk >= ng)
        def _():
            step_ref[...] = softplus(mm(proj[:, :r], sw_ref[...]) + bias_ref[...])

        step = step_ref[...]
        drive = drive_ref[...].astype(F32)
        z = z_ref[...]
        sig = 1.0 / (1.0 + jnp.exp2(z * -LOG2E))
        sig_s[...] = sig
        dy = dg_ref[...] * (z * sig)
        dy_ref[...] = dy
        gskip_ref[...] += jnp.sum(dy * drive, axis=0, keepdims=True)
        split(step_s, step)
        split(sd_s, step * drive)
        ct_s[...] = mm_nt(pick(r + n, p, n), proj)
        cbd_s[...] = jnp.where(blockdiag(lc, n), mm(proj, spread(r + n, p, n)), 0.0).astype(BF)
        diag = blockdiag(T, n)

        def mxu(b, buf):
            rows = pl.ds(b * T, T)
            kept = {}

            def y_part(g):
                kept[g] = mm(cbd_s[rows, :], hg_s[buf, :, lanes[g]])

            def r_part(g):
                x = mm_nt(dy_ref[rows, lanes[g]].astype(BF), hg_s[buf, :, lanes[g]])
                kept["r"] = x if g == 0 else kept["r"] + x
                if g == groups - 1:
                    rc_s[rows, :] = jnp.where(diag, kept["r"], 0.0).astype(BF)

            def end(g):
                ln = lanes[g]
                y = kept[g] + skip_ref[:, ln] * drive_ref[rows, ln].astype(F32)
                zz = z_ref[rows, ln]
                sg = sig_s[rows, ln]
                gated_ref[rows, ln] = (y * (zz * sg)).astype(BF)
                dz_ref[rows, ln] = (dg_ref[rows, ln] * y * (sg * (1.0 + zz * (1.0 - sg)))).astype(BF)

            return [functools.partial(f, g) for g in range(groups) for f in (y_part, r_part, end)]

        def vpu(with_g, b, buf, state, pieces=()):
            hs, hbs, qs = (list(s) for s in state)
            pieces = list(pieces)
            t0 = b * T
            bt = bt_s[:, t0 : t0 + T]
            ct = ct_s[:, t0 : t0 + T] if with_g else None
            base = jnp.minimum(chunk, ng - 1) * (lc * n)
            for k in range(T):
                t = t0 + k
                bb = jnp.broadcast_to(bt[:, k : k + 1], (n, 128))
                bb = jnp.concatenate([bb, bb], axis=1)
                if with_g:
                    cc = jnp.broadcast_to(ct[:, k : k + 1], (n, 128))
                    cc = jnp.concatenate([cc, cc], axis=1)
                at = pl.ds(t * n, n)
                far = pl.ds(pl.multiple_of(base + t * n, n), n)
                for g in range(groups):
                    ln = lanes[g]
                    e = jnp.exp2(row(step_s, g, t, n) * rate2[:, ln])
                    hprev_ref[at, ln] = hbs[g]
                    hs[g] = e * hs[g] + bb * row(sd_s, g, t, n)
                    hbs[g] = hs[g].astype(BF)
                    if with_g:
                        hg_s[buf, pl.ds(k * n, n), ln] = hbs[g] + g_s[far, ln]
                        ag = cc * row(dy_s, g, t, n) + qs[g]
                        qs[g] = e * ag
                        agb = ag.astype(BF)
                        ag_ref[at, ln] = agb
                        wg_ref[at, ln] = agb * qg_s[far, ln]
                    else:
                        hg_s[buf, pl.ds(k * n, n), ln] = hbs[g]
                if k % 2 and pieces:
                    pieces.pop(0)()
            for f in pieces:
                f()
            return tuple(hs), tuple(hbs), tuple(qs)

        def run(with_g):
            many = range(groups)
            state = tuple(st_f[g + groups] for g in many), tuple(st_h[g] for g in many), tuple(st_q[g] for g in many)
            state = vpu(with_g, 0, 0, state)
            for b in range(1, nb):
                state = vpu(with_g, b, b, state, mxu(b - 1, b - 1))
            for f in mxu(nb - 1, nb - 1):
                f()
            for g in many:
                st_f[g + groups] = state[0][g]
                st_h[g] = state[1][g]
                st_q[g] = state[2][g]

        live = jnp.logical_and(chunk < ng, chunk * lc < pfx)

        @pl.when(live)
        def _():
            mask = (positions(chunk) < pfx).astype(F32)
            split(dy_s, dy * mask)
            run(True)

            @pl.when(pfx < (chunk + 1) * lc)
            def _():
                keep = iota((lc * n, c), 0) + chunk * (lc * n) < pfx * n
                ag_ref[...] = jnp.where(keep, ag_ref[...].astype(F32), 0.0).astype(BF)

        @pl.when(jnp.logical_not(live))
        def _():
            run(False)

        part_ref[...] = mm(rc_s[...], fold(r + n, p, n))
        spot = pl.ds(pl.multiple_of(chunk * lc, lc), lc)
        gated_s[spot, :] = gated_ref[...]
        dzs_s[spot, :] = dz_ref[...]

    tn_dims = (((0,), (0,)), ((), ()))
    copies = [pltpu.make_async_copy(a, b, sems.at[j]) for j, (a, b) in enumerate(((normed_hbm, normed_ref), (cot_hbm, cot_ref), (low_hbm, low_ref), (w_hbm, w_ref)))]

    @pl.when(i == 1)
    def _():
        for copy in copies:
            copy.start()

    @pl.when(i == ng + nc)
    def _():
        for copy in copies:
            copy.wait()

    for late, (zo_ref, oo_ref, mo_ref) in enumerate(((sz_ref, so_ref, sm_ref), (kz_ref, ko_ref, km_ref))):
        @pl.when(i == ng + nc + late)
        def _(late=late, zo_ref=zo_ref, oo_ref=oo_ref, mo_ref=mo_ref):
            side = lambda j: order_ref[j] if late else 1 - order_ref[j]
            rows = gated_s.shape[0] // 2
            wide = normed_ref[:, pl.ds(pl.multiple_of(side(0) * (normed_ref.shape[1] // 2), 128), normed_ref.shape[1] // 2)]
            zo_ref[...] = lax.dot_general(wide, dzs_s[...], tn_dims, preferred_element_type=F32).astype(BF)
            cols = gated_s[:, pl.ds(pl.multiple_of(side(1) * (c // 2), 128), c // 2)]
            oo_ref[...] = lax.dot_general(cols, cot_ref[...], tn_dims, preferred_element_type=F32).astype(BF)
            here = pl.ds(pl.multiple_of(side(2) * rows, 8), rows)
            mix = mm(gated_s[here, :], w_ref[...])
            mo_ref[...] = (mix + jnp.where(order_ref[3] == 0, low_ref[here, :].astype(F32), 0.0)).astype(BF)


def back_kernel(ng, top, low, far, prefix_ref, proj_ref, sw_ref, drive_ref, step_ref, dy_ref, h_ref, pin_ref, dlog_ref, skip_ref, *refs):
    (part_ref, dpre_ref, ddrive_ref, po_ref, ao_ref, gbias_ref, step_s, dy_s, p_s, ct_s, bbd_s, rb_s, ds_s, v_s, w_s, sw_s) = refs[far:]
    lc, c = drive_ref.shape
    p = proj_ref.shape[1]
    n = dlog_ref.shape[0]
    r = p - 2 * n
    tn = T * n
    nb = lc // T
    groups = c // 256
    i = pl.program_id(0)
    chunk = top - i
    rate2 = -jnp.exp(dlog_ref[...]) * LOG2E
    rate2b = rate2.astype(BF)
    lanes = [slice(g * 256, (g + 1) * 256) for g in range(groups)]

    @pl.when(i == 0)
    def _():
        sw_s[...] = jnp.zeros_like(sw_s)
        sw_s[pl.ds(0, r), :] = sw_ref[...]
        if far >= 6:
            pc_ref, ac_ref, bc_ref = refs[far - 6 : far - 3]
            for g in range(groups):
                p_s[g] = pc_ref[:, lanes[g]]
            ao_ref[...] = ac_ref[...]
            gbias_ref[...] = bc_ref[...]
        else:
            p_s[...] = jnp.zeros_like(p_s)
            ao_ref[...] = jnp.zeros_like(ao_ref)
            gbias_ref[...] = jnp.zeros_like(gbias_ref)

    ag_ref, wg_ref = refs[:2] if low < ng else (None, None)
    proj = proj_ref[...]
    split(step_s, step_ref[...])
    split(dy_s, dy_ref[...])
    ct_s[...] = mm_nt(pick(r + n, p, n), proj)
    bbd_s[...] = jnp.where(blockdiag(lc, n), mm(proj, spread(r, p, n)), 0.0).astype(BF)
    diag = blockdiag(T, n)
    ones = diag.astype(BF)
    gather = (lax.rem(iota((n, tn // 2), 1), n) == iota((n, tn // 2), 0)).astype(BF)

    never = prefix_ref[0] < 0
    done = {}

    def vpu(with_g, b, buf, state, pieces=()):
        ps = list(state)
        seen = done.get(b + 3, {})
        pieces = list(pieces)
        held = [None] * groups
        t0 = b * T
        ct = ct_s[:, t0 : t0 + T]
        for k in range(T - 1, -1, -1):
            t = t0 + k
            for g in range(groups):
                key = {T - 1: ("s", g), T // 2: ("v", g), T // 4: ("w", g)}.get(k)
                if key in seen:
                    ps[g] = jnp.where(never, seen[key], ps[g])
            cc = jnp.broadcast_to(ct[:, k : k + 1], (n, 128))
            cc = jnp.concatenate([cc, cc], axis=1)
            at = pl.ds(t * n, n)
            for g in range(groups):
                ln = lanes[g]
                st = row(step_s, g, t, n)
                e = jnp.exp2(st * rate2[:, ln])
                ah = cc * row(dy_s, g, t, n) + ps[g]
                ps[g] = e * ah
                dsrc = ah.astype(BF)
                w = ps[g].astype(BF) * h_ref[at, ln]
                if with_g:
                    dsrc = dsrc + ag_ref[at, ln]
                    w = w + wg_ref[at, ln]
                ds_s[buf, pl.ds(k * n, n), ln] = dsrc
                v_s[buf, pl.ds(k * n, n), ln] = w * rate2b[:, ln]
                ws = w * st.astype(BF)
                if k % 2:
                    held[g] = ws
                else:
                    w_s[buf, pl.ds(k // 2 * n, n), ln] = held[g] + ws
            if k % 2 == 0 and pieces:
                pieces.pop(0)()
        for f in pieces:
            f()
        return tuple(ps)

    def mxu(b, buf):
        rows = pl.ds(b * T, T)
        kept = done[b] = {}

        def s_part(g):
            kept["s", g] = mm(bbd_s[rows, :], ds_s[buf, :, lanes[g]])

        def v_part(g):
            kept["v", g] = mm(ones, v_s[buf, :, lanes[g]])
            kept["w", g] = mm(gather, w_s[buf, :, lanes[g]])
            ao_ref[:, lanes[g]] += kept["w", g]

        def r_part(g):
            ln = lanes[g]
            sd = step_ref[rows, ln] * drive_ref[rows, ln].astype(F32)
            x = mm_nt(sd.astype(BF), ds_s[buf, :, ln])
            kept["r"] = x if g == 0 else kept["r"] + x
            if g == groups - 1:
                rb_s[rows, :] = jnp.where(diag, kept["r"], 0.0).astype(BF)

        def end(g):
            ln = lanes[g]
            step = step_ref[rows, ln]
            ssum = kept["s", g]
            drive = drive_ref[rows, ln].astype(F32)
            dpre = (kept["v", g] * LN2 + drive * ssum) * one_minus_exp(step)
            dpre_ref[rows, ln] = dpre.astype(BF)
            ddrive_ref[rows, ln] = skip_ref[:, ln] * dy_ref[rows, ln] + step * ssum
            gbias_ref[:, ln] += jnp.sum(dpre, axis=0, keepdims=True)

        return [functools.partial(f, g) for g in range(groups) for f in (s_part, v_part, r_part, end)]

    def run(with_g):
        done.clear()
        many = range(groups)
        state = tuple(p_s[g] for g in many)
        state = vpu(with_g, nb - 1, nb - 1, state)
        for b in range(nb - 2, -1, -1):
            state = vpu(with_g, b, b, state, mxu(b + 1, b + 1))
        for f in mxu(0, 0):
            f()
        for g in many:
            p_s[g] = state[g]

    if low >= ng:
        run(False)
    else:
        live = jnp.logical_and(chunk < ng, chunk * lc < prefix_ref[0])

        @pl.when(live)
        def _():
            run(True)

        @pl.when(jnp.logical_not(live))
        def _():
            run(False)

    part_ref[...] = (pin_ref[...] + mm(rb_s[...], fold(r, p, n)) + mm_nt(dpre_ref[...], sw_s[...])).astype(part_ref.dtype)
    po_ref[...] = jnp.concatenate([p_s[g] for g in range(groups)], axis=1)


def whole(*s):
    return pl.BlockSpec(s, lambda i: (0,) * len(s))


SMEM = pl.BlockSpec(memory_space=pltpu.SMEM)


def head_kernel(low_ref, gain_ref, w_ref, cw_ref, cb_ref, xw_ref, normed_ref, x_ref, slope_ref, drive_ref, part_ref, rs_ref, edge_s):
    taps = cw_ref.shape[0]
    lc = low_ref.shape[0]

    @pl.when(pl.program_id(0) == 0)
    def _():
        edge_s[...] = jnp.zeros_like(edge_s)

    xf = low_ref[...].astype(F32)
    rs = lax.rsqrt(jnp.mean(xf * xf, axis=-1, keepdims=True) + epsilon)
    rs_ref[...] = rs
    normed = (xf * rs * gain_ref[...]).astype(BF)
    normed_ref[...] = normed
    x = mm(normed, w_ref[...])
    x_ref[...] = x.astype(BF)
    wide = jnp.concatenate([edge_s[...], x], axis=0)
    edge_s[...] = x[lc - 8 :]
    out = cb_ref[...] + cw_ref[taps - 1 :, :] * x
    for k in range(taps - 1):
        at = 8 - (taps - 1) + k
        out = out + cw_ref[k : k + 1, :] * wide[at : at + lc]
    sc = sigmoid(out)
    act = out * sc
    slope_ref[...] = sc * (1.0 + out - act)
    drive = act.astype(BF)
    drive_ref[...] = drive
    part_ref[...] = mm_nt(drive, xw_ref[...]).astype(BF)


def head(low, gain, w_all, conv_weight, conv_bias, xproj_t):
    l, d = low.shape
    c = w_all.shape[1] // 2
    p = xproj_t.shape[0]
    hc = 256
    by = lambda w: pl.BlockSpec((hc, w), lambda i: (i, 0))
    s = jax.ShapeDtypeStruct
    return pl.pallas_call(
        head_kernel,
        grid=(l // hc,),
        in_specs=[by(d), whole(1, d), whole(d, c), whole(*conv_weight.shape), whole(1, c), whole(p, c)],
        out_specs=[by(d), by(c), by(c), by(c), by(p), by(1)],
        out_shape=[s((l, d), BF), s((l, c), BF), s((l, c), F32), s((l, c), BF), s((l, p), BF), s((l, 1), F32)],
        scratch_shapes=[pltpu.VMEM((8, c), F32)],
        compiler_params=pltpu.CompilerParams(vmem_limit_bytes=60 << 20),
        cost_estimate=pl.CostEstimate(flops=2 * l * d * c, transcendentals=l * c, bytes_accessed=4 * l * d + 2 * d * c + 6 * l * c),
        name="head",
    )(low, gain.reshape(1, d), w_all, conv_weight, conv_bias.reshape(1, c), xproj_t)


def gates_kernel(n_ref, w_ref, c_ref, o_ref, z_ref, dg_ref):
    z_ref[...] = mm(n_ref[...], w_ref[...])
    dg_ref[...] = mm_nt(c_ref[...], o_ref[...])


def gates(normed, w_all, cot, out_weight):
    l, d = normed.shape
    c = w_all.shape[1] // 2
    by = lambda w: pl.BlockSpec((256, w), lambda i: (i, 0))
    s = jax.ShapeDtypeStruct
    return pl.pallas_call(
        gates_kernel,
        grid=(l // 256,),
        in_specs=[by(d), pl.BlockSpec((d, c), lambda i: (0, 1)), by(d), whole(c, d)],
        out_specs=[by(c), by(c)],
        out_shape=[s((l, c), F32), s((l, c), F32)],
        compiler_params=pltpu.CompilerParams(vmem_limit_bytes=60 << 20),
        cost_estimate=pl.CostEstimate(flops=4 * l * d * c, transcendentals=0, bytes_accessed=4 * (l * d + d * c + 2 * l * c)),
        name="gates",
    )(normed, w_all, cot, out_weight)


def inner_kernel(rows_a, rows_b, bits_ref, dproj_ref, ds_ref, x_ref, slope_ref, drive_ref, dz_ref, normed_ref, low_ref, rs_ref, w_ref, xw_ref, cw_ref,
                 gb_ref, gd_ref, dlog_ref, gk_ref, proj_ref, dpre_ref, ka_ref, sa_ref, kb_ref, sb_ref, kn_ref, sn_ref, gn_ref, edge_s, gin_s, gx_s, gs_s, gc_s, gn_s, la_s, lb_s):
    taps = cw_ref.shape[0]
    lc, c = ds_ref.shape
    d = normed_ref.shape[1]
    p = dproj_ref.shape[1]
    n = gd_ref.shape[0]
    r = p - 2 * n
    i = pl.program_id(0)
    last = pl.num_programs(0) - 1
    tn = (((0,), (0,)), ((), ()))

    @pl.when(i == 0)
    def _():
        edge_s[...] = jnp.zeros_like(edge_s)
        gin_s[...] = jnp.zeros_like(gin_s)
        gx_s[...] = jnp.zeros_like(gx_s)
        gs_s[...] = jnp.zeros_like(gs_s)
        gc_s[...] = jnp.zeros_like(gc_s)
        gn_s[...] = jnp.zeros_like(gn_s)

    dproj = dproj_ref[...]
    x = x_ref[...].astype(F32)
    dconv = (ds_ref[...] + mm(dproj, xw_ref[...])) * slope_ref[...]
    gc_s[pl.ds(taps, 1), :] += jnp.sum(dconv, axis=0, keepdims=True)
    ahead = jnp.concatenate([dconv, edge_s[...]], axis=0)
    edge_s[...] = dconv[:8]
    dx = cw_ref[taps - 1 :, :] * dconv
    gc_s[pl.ds(taps - 1, 1), :] += jnp.sum(dconv * x, axis=0, keepdims=True)
    for k in range(taps - 1):
        by = taps - 1 - k
        moved = ahead[by : by + lc]
        dx = dx + cw_ref[k : k + 1, :] * moved
        gc_s[pl.ds(k, 1), :] += jnp.sum(moved * x, axis=0, keepdims=True)
    dx = dx.astype(BF)
    normed = normed_ref[...]
    gin_s[...] += lax.dot_general(normed, dx, tn, preferred_element_type=F32)
    gx_s[...] += lax.dot_general(dproj, drive_ref[...], tn, preferred_element_type=F32)
    gs_s[...] += lax.dot_general(proj_ref[:, :r], dpre_ref[...], tn, preferred_element_type=F32)
    dn = mm_nt(jnp.concatenate([dx, dz_ref[...]], axis=1), w_ref[...])
    half = pl.num_programs(0) // 2

    keeps = (i < half) == (bits_ref[2] == 1)

    @pl.when(jnp.logical_not(keeps))
    def _():
        sn_ref[...] = dn.astype(BF)

    @pl.when(keeps)
    def _():
        kn_ref[...] = dn.astype(BF)

    gn_s[...] += jnp.sum(dn * (low_ref[...].astype(F32) * rs_ref[...]), axis=0, keepdims=True)

    @pl.when(i == last)
    def _():
        gn_ref[...] = gn_s[...]
        lines = [gc_s[pl.ds(0, taps + 1), :], gb_ref[...], gk_ref[...]]
        lines = jnp.concatenate(lines + [jnp.zeros((16 - taps - 3, c), F32)], axis=0)
        top = 16 + n + r + p
        la_s[pl.ds(0, 16), :] = lines.astype(BF)
        la_s[pl.ds(16, n), :] = (gd_ref[...] * -jnp.exp(dlog_ref[...])).astype(BF)
        la_s[pl.ds(16 + n, r), :] = gs_s[...].astype(BF)
        la_s[pl.ds(16 + n + r, p), :] = gx_s[...].astype(BF)
        la_s[pl.ds(top, rows_a - top), :] = gin_s[pl.ds(0, rows_a - top), :].astype(BF)
        rest = d - (rows_a - top)
        lb_s[pl.ds(0, rest), :] = gin_s[pl.ds(rows_a - top, rest), :].astype(BF)
        if rows_b > rest:
            lb_s[pl.ds(rest, rows_b - rest), :] = jnp.zeros((rows_b - rest, c), BF)
        for bit, total, keep_ref, send_ref in ((bits_ref[0], la_s, ka_ref, sa_ref), (bits_ref[1], lb_s, kb_ref, sb_ref)):
            rows = keep_ref.shape[0]
            keep_ref[...] = total[pl.ds(pl.multiple_of(bit * rows, 8), rows), :]
            send_ref[...] = total[pl.ds(pl.multiple_of((1 - bit) * rows, 8), rows), :]


def inner(rows_a, rows_b, bits, dproj, ddrive, x, slope, drive, dz, normed, low, rs, w_all, xproj_t, conv_weight, g_bias, g_decay, decay_log, g_skip, proj, dpre):
    l, c = x.shape
    d = normed.shape[1]
    p = dproj.shape[1]
    n = g_decay.shape[0]
    hc = 256
    nc = l // hc
    by = lambda w: pl.BlockSpec((hc, w), lambda i, bits: (nc - 1 - i, 0))
    full = lambda *q: pl.BlockSpec(q, lambda i, bits: (0,) * len(q))
    s = jax.ShapeDtypeStruct
    v = pltpu.VMEM
    early = lambda i: jnp.maximum(nc // 2 - 1 - i, 0)
    late = lambda i: jnp.minimum(nc - 1 - i, nc // 2 - 1)
    kept = pl.BlockSpec((hc, d), lambda i, bits: (jnp.where(bits[2] == 1, early(i), late(i)), 0))
    sent = pl.BlockSpec((hc, d), lambda i, bits: (jnp.where(bits[2] == 1, late(i), early(i)), 0))
    return pl.pallas_call(
        functools.partial(inner_kernel, rows_a, rows_b),
        grid_spec=pltpu.PrefetchScalarGridSpec(
            num_scalar_prefetch=1,
            grid=(nc,),
            in_specs=[by(p), by(c), by(c), by(c), by(c), by(c), by(d), by(d), by(1), full(d, 2 * c), full(p, c), full(*conv_weight.shape),
                      full(1, c), full(n, c), full(n, c), full(1, c), by(p), by(c)],
            out_specs=[full(rows_a // 2, c)] * 2 + [full(rows_b // 2, c)] * 2 + [kept, sent, full(1, d)],
            scratch_shapes=[v((8, c), F32), v((d, c), F32), v((p, c), F32), v((p - 2 * n, c), F32), v((8, c), F32), v((1, d), F32), v((rows_a, c), BF), v((rows_b, c), BF)],
        ),
        out_shape=[s((rows_a // 2, c), BF)] * 2 + [s((rows_b // 2, c), BF)] * 2 + [s((l // 2, d), BF)] * 2 + [s((1, d), F32)],
        compiler_params=pltpu.CompilerParams(vmem_limit_bytes=60 << 20),
        cost_estimate=pl.CostEstimate(flops=6 * l * d * c, transcendentals=l * c, bytes_accessed=10 * l * d),
        name="inner",
    )(bits, dproj, ddrive, x, slope, drive, dz, normed, low, rs, w_all, xproj_t, conv_weight, g_bias, g_decay, decay_log, g_skip, proj, dpre)


def merge_kernel(kinds, bits_ref, *refs):
    take = list(refs)
    ins = [[take.pop(0) for _ in range(2 + EXTRA[kind])] for kind in kinds]
    for j, (kind, (one, two, *more)) in enumerate(zip(kinds, ins)):
        rows = one.shape[0]
        if kind == "join":
            out = take.pop(0)
            out[pl.ds(pl.multiple_of(bits_ref[j] * rows, 8), rows), :] = one[...]
            out[pl.ds(pl.multiple_of((1 - bits_ref[j]) * rows, 8), rows), :] = two[...]
        elif kind == "split":
            half = rows // 2
            for out, at in ((take.pop(0), bits_ref[j]), (take.pop(0), 1 - bits_ref[j])):
                part = pl.ds(pl.multiple_of(at * half, 8), half)
                out[...] = (one[part, :].astype(F32) + two[part, :].astype(F32)).astype(BF)
        else:
            total = one[...].astype(F32) + two[...].astype(F32)
            if kind == "shift":
                total = total + more[0][...].astype(F32)
            if kind == "norm":
                x_ref, rs_ref, gain_ref = more
                x, rs = x_ref[...].astype(F32), rs_ref[...]
                scaled = total * gain_ref[...]
                total = rs * scaled - x * (rs * rs * rs) * jnp.mean(scaled * x, axis=-1, keepdims=True)
            take.pop(0)[...] = total.astype(BF)


EXTRA = dict(join=0, split=0, sum=0, shift=1, norm=3)


def once(*shape):
    return pl.BlockSpec(shape, lambda i: (0,) * len(shape), pipeline_mode=pl.Buffered(1))


def merge(items):
    kinds = tuple(item[0] for item in items)
    bits = jnp.stack([jnp.asarray(item[1], jnp.int32) for item in items])
    arrays = [v for item in items for v in item[2:]]
    shapes = []
    for kind, _, one, *_ in items:
        rows, cols = one.shape
        many = {"join": [2 * rows], "split": [rows // 2] * 2}.get(kind, [rows])
        shapes.append([jax.ShapeDtypeStruct((q, cols), BF) for q in many])
    flat = [q for group in shapes for q in group]
    homes = [len(group) == 2 and j == 0 for group in shapes for j in range(len(group))]
    out = list(pl.pallas_call(
        functools.partial(merge_kernel, kinds),
        grid=(1,),
        in_specs=[SMEM] + [once(*v.shape) for v in arrays],
        out_specs=[once(*v.shape) for v in flat],
        out_shape=[pltpu.HBM(q.shape, q.dtype) if kept else q for q, kept in zip(flat, homes)],
        compiler_params=pltpu.CompilerParams(vmem_limit_bytes=24 << 20),
        name="merge",
    )(bits, *arrays))
    return [[out.pop(0) for _ in group] for group in shapes]


def joined_kernel(bits_ref, one_ref, two_ref, *refs):
    out_ref = refs[-1]
    rows = one_ref.shape[0]
    for at, part in ((bits_ref[0], one_ref), (1 - bits_ref[0], two_ref)):
        where = pl.ds(pl.multiple_of(at * rows, 8), rows)
        value = part[...].astype(F32)
        out_ref[where, :] = value if len(refs) == 1 else value + refs[0][where, :].astype(F32)


def joined(bit, one, two, *add):
    vm = pl.BlockSpec(memory_space=pltpu.VMEM)
    shape = (2 * one.shape[0], one.shape[1])
    return pl.pallas_call(
        joined_kernel,
        in_specs=[SMEM] + [vm] * (2 + len(add)),
        out_specs=vm,
        out_shape=jax.ShapeDtypeStruct(shape, F32),
        compiler_params=pltpu.CompilerParams(vmem_limit_bytes=24 << 20),
        name="joined",
    )(bit.astype(jnp.int32).reshape(1), one, two, *add)


def last_kernel(n, r, p, taps, bits_ref, sa_ref, oa_ref, sb_ref, ob_ref, sz_ref, oz_ref, gin_ref, gc_ref, gcb_ref, gb_ref, gk_ref, gd_ref, gs_ref, gx_ref, all_s, z_s):
    top = 16 + n + r + p
    hc = gin_ref.shape[0]

    @pl.when(pl.program_id(0) == 0)
    def _():
        base = 0
        for j, mine, other, whole_s in ((0, sa_ref, oa_ref, all_s), (1, sb_ref, ob_ref, all_s), (2, sz_ref, oz_ref, z_s)):
            half = mine.shape[0]
            base = 0 if j == 2 else base
            whole_s[pl.ds(pl.multiple_of(base + bits_ref[j] * half, 8), half), :] = mine[...]
            whole_s[pl.ds(pl.multiple_of(base + (1 - bits_ref[j]) * half, 8), half), :] = other[...]
            base += 2 * half
        lines = all_s[pl.ds(0, 16), :].astype(F32)
        gc_ref[...] = lines[:taps]
        gcb_ref[...] = lines[taps : taps + 1]
        gb_ref[...] = lines[taps + 1 : taps + 2]
        gk_ref[...] = lines[taps + 2 : taps + 3]
        gd_ref[...] = all_s[pl.ds(16, n), :].astype(F32)
        gs_ref[...] = all_s[pl.ds(16 + n, r), :].astype(F32)
        gx_ref[...] = all_s[pl.ds(16 + n + r, p), :].astype(F32)

    at = pl.program_id(0) * hc
    gin_ref[:, 0, :] = all_s[pl.ds(pl.multiple_of(top + at, 8), hc), :].astype(F32)
    gin_ref[:, 1, :] = z_s[pl.ds(pl.multiple_of(at, 8), hc), :].astype(F32)


def last(bits, sa, oa, sb, ob, sz, oz, n, r, p, taps):
    half, c = sz.shape
    hc = 256
    s = jax.ShapeDtypeStruct
    small = [s((taps, c), F32), s((1, c), F32), s((1, c), F32), s((1, c), F32), s((n, c), F32), s((r, c), F32), s((p, c), F32)]
    arrays = [sa, oa, sb, ob, sz, oz]
    return pl.pallas_call(
        functools.partial(last_kernel, n, r, p, taps),
        grid=(2 * half // hc,),
        in_specs=[SMEM] + [once(*v.shape) for v in arrays],
        out_specs=[pl.BlockSpec((hc, 2, c), lambda i: (i, 0, 0))] + [whole(*v.shape) for v in small],
        out_shape=[s((2 * half, 2, c), F32)] + small,
        scratch_shapes=[pltpu.VMEM((2 * sa.shape[0] + 2 * sb.shape[0], c), BF), pltpu.VMEM((2 * half, c), BF)],
        compiler_params=pltpu.CompilerParams(vmem_limit_bytes=24 << 20),
        name="last",
    )(bits, *arrays)


def front(order, proj, sw, bias, drive, z, dg, dlog, skip, normed, cot, low, out_weight):
    l, c = drive.shape
    d = low.shape[1]
    p = proj.shape[1]
    n = dlog.shape[0]
    ng = l // 2 // LC
    nc = l // LC
    s = jax.ShapeDtypeStruct
    fwd = lambda i, o: (jnp.clip(i - ng, 0, nc - 1), 0)
    both = lambda i, o: (jnp.where(i < ng, ng - 1 - i, jnp.minimum(i - ng, nc - 1)), 0)
    half = lambda i, o: (jnp.clip(i - ng, 0, ng - 1), 0)
    full = lambda *q: pl.BlockSpec(q, lambda i, o: (0,) * len(q))
    once = lambda *q: pl.BlockSpec(q, lambda i, o: (0,) * len(q), pipeline_mode=pl.Buffered(1))
    B = pl.BlockSpec
    lanes = c // 128
    v = pltpu.VMEM
    return pl.pallas_call(
        functools.partial(front_kernel, ng, nc),
        grid_spec=pltpu.PrefetchScalarGridSpec(
            num_scalar_prefetch=1,
            grid=(ng + nc + 2,),
            in_specs=[B((LC, p), both), full(*sw.shape), full(1, c), B((LC, c), both), B((LC, c), fwd), B((LC, c), fwd), full(n, c), full(1, c),
                      ] + [B(memory_space=pl.ANY)] * 4,
            out_specs=[B((LC, c), fwd), B((LC, c), fwd), B((LC, c), fwd), B((LC, c), fwd), B((LC * n, c), fwd), B((LC * n, c), half), B((LC * n, c), half), B((LC, p), fwd), full(1, c)]
                + [once(d // 2, c)] * 2 + [once(c // 2, d)] * 2 + [once(l // 2, d)] * 2,
            scratch_shapes=[v((lanes, LC, 128), F32)] * 3 + [v((LC, c), F32), v((ng, LC, c), F32), v((n, LC), F32), v((n, LC), F32), v((LC, T * n), BF), v((LC, T * n), BF),
                v((LC // T, T * n, c), BF), v((l // 2 * n, c), BF), v((l // 2 * n, c), BF), v((c // 128, n, 256), F32), v((c // 256, n, 256), BF), v((c // 256, n, 256), F32), v((l, c), BF), v((l, c), BF),
                v((l, d), BF), v((l, d), BF), v((l, d), BF), v((c, d), BF), pltpu.SemaphoreType.DMA((4,))],
        ),
        out_shape=[s((l, c), BF), s((l, c), BF), s((l, c), F32), s((l, c), F32), s((l * n, c), BF), s((l // 2 * n, c), BF), s((l // 2 * n, c), BF), s((l, p), F32), s((1, c), F32)]
            + [s((d // 2, c), BF)] * 2 + [s((c // 2, d), BF)] * 2 + [s((l // 2, d), BF)] * 2,
        compiler_params=pltpu.CompilerParams(vmem_limit_bytes=60 << 20),
        name="front",
    )(order, proj, sw, bias.reshape(1, c), drive, z, dg, dlog, skip.reshape(1, c), normed, cot, low, out_weight)


def back(prefix, proj, sw, drive, step, dy, hprev, ag, wg, pin, dlog, skip, carry, top, low, filled=()):
    l, c = drive.shape
    p = proj.shape[1]
    n = dlog.shape[0]
    ng = l // 2 // LC
    s = jax.ShapeDtypeStruct
    rev = lambda i: (top - i, 0)
    half = lambda i: (jnp.minimum(top - i, ng - 1), 0)
    B = pl.BlockSpec
    v = pltpu.VMEM
    ins = [SMEM, B((LC, p), rev), whole(*sw.shape), B((LC, c), rev), B((LC, c), rev), B((LC, c), rev), B((LC * n, c), rev), B((LC, p), rev), whole(n, c), whole(1, c)]
    extra, more = [], []
    if low < ng:
        extra, more = [ag, wg], [B((LC * n, c), half)] * 2
    if filled:
        extra, more = extra + list(carry) + list(filled), more + [whole(n, c), whole(n, c), whole(1, c)] + [B(memory_space=pl.ANY)] * 3
    first = len(ins) + len(extra) - 3
    return pl.pallas_call(
        functools.partial(back_kernel, ng, top, low, len(extra)),
        grid=(top - low + 1,),
        in_specs=ins + more,
        out_specs=[B((LC, p), rev), B((LC, c), rev), B((LC, c), rev), whole(n, c), whole(n, c), whole(1, c)],
        out_shape=[s((l, p), BF), s((l, c), BF), s((l, c), F32), s((n, c), F32), s((n, c), F32), s((1, c), F32)],
        input_output_aliases={first + j: j for j in range(3)} if filled else {},
        scratch_shapes=[v((c // 128, LC, 128), F32)] * 2 + [v((c // 256, n, 256), F32), v((n, LC), F32), v((LC, T * n), BF), v((LC, T * n), BF), v((LC // T, T * n, c), BF), v((LC // T, T * n, c), BF), v((LC // T, T * n // 2, c), BF), v((p, c), BF)],
        compiler_params=pltpu.CompilerParams(vmem_limit_bytes=60 << 20),
        cost_estimate=pl.CostEstimate(flops=(top - low + 1) * LC * n * c * 4000, transcendentals=0, bytes_accessed=(top - low + 1) * LC * n * c * 4),
        name="back",
    )(prefix, proj, sw, drive, step, dy, hprev, pin, dlog, skip.reshape(1, c), *extra)


def sigmoid(v):
    return 1.0 / (1.0 + jnp.exp(-v))


def exchange(value, name, size, bit):
    return lax.ppermute(value, name, [(j, j ^ (1 << bit)) for j in range(size)])


def bits_of(size):
    count = size.bit_length() - 1
    assert 1 << count == size
    return list(range(count))


class Chain:
    def __init__(self, name, size, order, keep, send, swap=True, middle=("sum", ())):
        order = list(order)
        self.name, self.size, self.keep, self.send, self.middle = name, size, keep, send, middle
        turn = [("swap", order.pop())] if swap else []
        self.steps = [("halve", bit) for bit in order] + turn + [("double", bit) for bit in reversed(order)]
        self.got = None

    def mine(self, bit):
        return (lax.axis_index(self.name) >> bit) & 1

    def start(self, send):
        self.send = send
        return exchange(send, self.name, self.size, self.steps[0][1])

    def item(self):
        kind, bit = self.steps.pop(0)
        after = self.steps[0]
        if kind == "double":
            return ("join", self.mine(bit), self.send, self.got)
        one = pltpu.with_memory_space_constraint(self.keep, pltpu.HBM) if kind == "halve" else self.send
        if kind == "halve" and after[0] == "halve":
            return ("split", self.mine(after[1]), one, self.got)
        if kind == "swap" or after[0] == "double":
            name, more = self.middle
            return (name, 0, one, self.got, *more)
        return ("sum", 0, one, self.got)

    def ended(self):
        return len(self.steps) == 1 and self.got is not None

    def accept(self, arrays):
        self.send = arrays[-1]
        self.keep = arrays[0]
        self.got = None


def ready(chains):
    live = [c for c in chains if c.got is not None and len(c.steps) > 1 and c not in PENDING]
    if live:
        for c, arrays in zip(live, merge([c.item() for c in live])):
            c.accept(arrays)


PENDING = []


def under(chains, work, *inputs, slow=()):
    waiting = [c for c in PENDING if c.got is not None]
    PENDING[:] = list(slow)
    chains = [c for c in chains if c.steps and c.got is None] + list(slow)
    sends, inputs = lax.optimization_barrier(([c.send for c in chains], inputs))
    got = [c.start(v) for c, v in zip(chains, sends)]
    result = work(*inputs)
    hold = len(chains) - len(slow)
    old = [c.got for c in waiting]
    heads, firsts, old, result = lax.optimization_barrier((sends[:hold], got[:hold], old, result))
    for c, v, w in zip(chains, list(heads) + list(sends[hold:]), list(firsts) + list(got[hold:])):
        c.send, c.got = v, w
    for c, w in zip(waiting, old):
        c.got = w
    return result


def on_device(sizes, tokens, prefix, norm_gain, in_weight, conv_weight, conv_bias, xproj_weight, step_weight, step_bias, decay_log, skip_gain, out_weight, out_cotangent):
    dp, tp = sizes
    seqs, length, width = tokens.shape
    assert seqs == 1
    channels = in_weight.shape[2]
    rank = step_weight.shape[0]
    taps = conv_weight.shape[0]
    n = decay_log.shape[0]
    p = rank + 2 * n
    low = tokens[0]
    cot = out_cotangent[0]
    w_all = lax.optimization_barrier(in_weight.reshape(width, 2 * channels))
    xproj_t = xproj_weight.T
    order = bits_of(dp)
    turned = order[1:] + order[:1]
    t_order = bits_of(tp)
    at = lax.axis_index("tensor")
    at_dp = lax.axis_index("dp")
    spot = 0
    rows = length
    for bit in t_order:
        rows //= 2
        spot = spot + ((at >> bit) & 1) * rows
    part_of = lambda v: lax.dynamic_slice_in_dim(v, spot, rows, 0)
    bit_of = lambda v, bit: (v >> bit) & 1

    normed, xpart, slope, drive, proj, rs = head(low, norm_gain, w_all, conv_weight, conv_bias, xproj_t)
    for bit in t_order[:-1]:
        proj = (proj.astype(F32) + exchange(proj, "tensor", tp, bit).astype(F32)).astype(BF)
    proj, n_in, c_in = lax.optimization_barrier((proj, normed, cot))
    other = exchange(proj, "tensor", tp, t_order[-1])
    zpart, dgated = gates(n_in, w_all, c_in, out_weight)
    other, zpart, dgated = lax.optimization_barrier((other, zpart, dgated))
    proj = (proj.astype(F32) + other.astype(F32)).astype(BF)

    picks = jnp.stack([bit_of(at_dp, order[0]), bit_of(at_dp, turned[0]), bit_of(at, t_order[0]), at, prefix[0]]).astype(jnp.int32)
    gated, dz, step, dy, hprev, ag, wg, pin, g_skip, kz, sz, ko, so, km, sm = front(picks, proj, step_weight, step_bias, drive, zpart, dgated, decay_log, skip_gain, normed, cot, low, out_weight)
    gz = Chain("dp", dp, order, kz, sz)
    go = Chain("dp", dp, turned, ko, so)
    mix = Chain("tensor", tp, t_order, km, sm, swap=False)
    chains = [gz, go, mix]
    nc = length // LC
    carry = ()
    filled = ()
    top = nc - 1
    for low_chunk in PIECES:
        def piece(d, carry, filled, top=top, low_chunk=low_chunk):
            return back(prefix, proj, step_weight, drive, step, d, hprev, ag, wg, pin, decay_log, skip_gain, carry, top, low_chunk, filled)

        *filled, p1, a1, b1 = under(chains, piece, dy, carry, tuple(filled))
        ready(chains)
        carry = (p1, a1, b1)
        top = low_chunk - 1
    dpart, dpre, ddrive_scan = filled
    _, g_decay, g_bias = carry

    for bit in t_order[:-1]:
        dpart = (dpart.astype(F32) + exchange(dpart, "tensor", tp, bit).astype(F32)).astype(BF)
    cross = Chain("tensor", tp, t_order[-1:], dpart, dpart)
    my_x, my_rs = under([gz, go, cross, mix], lambda v, w: (part_of(v), part_of(w)), low, rs)
    ready([gz, go])
    dproj = (cross.send.astype(F32) + cross.got.astype(F32)).astype(BF)
    total = 16 + n + p + rank + width
    total += -total % (16 << (len(order) - 1))
    rows_a = total // 2
    ka, sa, kb, sb, kn, sn, g_norm = under([gz, go], lambda v: inner(rows_a, total - rows_a, picks, v, ddrive_scan, xpart, slope, drive, dz, normed, low, rs, w_all, xproj_t, conv_weight, g_bias, g_decay, decay_log, g_skip, proj, dpre), dproj)
    la = Chain("dp", dp, order, ka, sa)
    lb = Chain("dp", dp, turned, kb, sb)
    dn = Chain("tensor", tp, t_order, kn, sn, swap=False, middle=("norm", (my_x, my_rs, norm_gain.reshape(1, width))))
    turns = [("tensor", tp, bit) for bit in reversed(t_order)] + [("dp", dp, bit) for bit in order]

    def gains(v):
        if turns:
            name, size, bit = turns.pop(0)
            v = v + exchange(v, name, size, bit)
        return v

    def closing(v, one, two, *out):
        joint = merge([("join", mix.mine(mix.steps[0][1]), *out)])[0][0] if mix.ended() else None
        return gains(v), joined(go.mine(go.steps[0][1]), one, two), joint

    block_out = None
    late = [[]]
    g_out = None
    while not la.ended():
        extra = late.pop(0) if late else [c for c in (gz, go) if not c.ended()]
        ready(extra + [la, lb, dn])
        final = len(la.steps) == 1
        slow = [dn] if dn.got is None and len(dn.steps) > 1 and dn.steps[0][1] != t_order[0] else []
        now = [dn] if dn.got is None and not slow and not final else []
        if final and go.ended():
            g_norm, g_out, block_out = under([la, lb] + now + extra, closing, g_norm, go.send, go.got, mix.send, mix.got, slow=slow)
        else:
            g_norm = under([la, lb] + now + extra, gains, g_norm, slow=slow)
    while turns:
        g_norm = gains(g_norm)
    for c in (dn, gz, go):
        while not c.ended():
            ready([c])
            under([c], lambda: ())
    flags = jnp.stack([c.mine(c.steps[0][1]) for c in (la, lb, gz)]).astype(jnp.int32)
    g_in, g_conv, g_convb, g_bias, g_skip, g_decay, g_step, g_xproj = last(flags, la.send, la.got, lb.send, lb.got, gz.send, gz.got, n, rank, p, taps)
    grad_tokens = joined(dn.mine(dn.steps[0][1]), dn.send, dn.got, cot)
    if g_out is None:
        g_out = joined(go.mine(go.steps[0][1]), go.send, go.got)
    if block_out is None:
        while not mix.ended():
            under([mix], lambda: ())
            ready([mix])
        block_out = merge([mix.item()] if len(mix.steps) > 1 else [("join", mix.mine(mix.steps[0][1]), mix.send, mix.got)])[0][0]
    return (block_out[None], grad_tokens[None], g_norm.reshape(-1), g_in, g_conv, g_convb[0], g_xproj.T, g_step, g_bias[0], g_decay, g_skip[0], g_out)


def solution(mesh):
    placed = (
        P("dp", None, None),
        P("dp"),
        P(),
        P(None, None, "tensor"),
        P(None, "tensor"),
        P("tensor"),
        P("tensor", None),
        P(None, "tensor"),
        P("tensor"),
        P(None, "tensor"),
        P("tensor"),
        P("tensor", None),
        P("dp", None, None),
    )
    results = (
        P("dp", None, None),
        P("dp", None, None),
        P(),
        P(None, None, "tensor"),
        P(None, "tensor"),
        P("tensor"),
        P("tensor", None),
        P(None, "tensor"),
        P("tensor"),
        P(None, "tensor"),
        P("tensor"),
        P("tensor", None),
    )
    sizes = (mesh.shape["dp"], mesh.shape["tensor"])
    return jax.shard_map(functools.partial(on_device, sizes), mesh=mesh, in_specs=placed, out_specs=results, check_vma=False)
```

```python
import functools

import jax
import jax.numpy as jnp
from jax import lax
from jax.experimental import pallas as pl
from jax.experimental.pallas import tpu as pltpu
from jax.sharding import PartitionSpec as P

T = 16
LC = 128
PIECES = (5, 2, 0)
LOG2E = 1.4426950408889634
LN2 = 0.6931471805599453
F32 = jnp.float32
BF = jnp.bfloat16
NT = (((1,), (1,)), ((), ()))
STRIDED = True
epsilon = 1e-05


def iota(shape, d):
    return lax.broadcasted_iota(jnp.int32, shape, d)


def mm(a, b):
    return jnp.dot(a, b, preferred_element_type=F32)


def mm_nt(a, b):
    return lax.dot_general(a, b, NT, preferred_element_type=F32)


def row(ref, g, t, n):
    if STRIDED:
        pair = [ref[2 * g + j, pl.ds(t, 8, stride=0), :] for j in (0, 1)]
        wide = jnp.concatenate(pair, axis=1)
        return jnp.concatenate([wide] * (n // 8), axis=0)
    pair = [jnp.broadcast_to(ref[2 * g + j, pl.ds(t, 1), :], (n, 128)) for j in (0, 1)]
    return jnp.concatenate(pair, axis=1)


def spread(base, p, n):
    return (iota((p, T * n), 0) == base + lax.rem(iota((p, T * n), 1), n)).astype(BF)


def pick(base, p, n):
    return (iota((n, p), 1) == base + iota((n, p), 0)).astype(BF)


def fold(base, p, n):
    return (iota((T * n, p), 1) == base + lax.rem(iota((T * n, p), 0), n)).astype(BF)


def blockdiag(rows, n):
    return lax.rem(iota((rows, T * n), 0), T) == lax.div(iota((rows, T * n), 1), n)


def split(ref, value):
    for g in range(value.shape[1] // 128):
        ref[g] = value[:, g * 128 : (g + 1) * 128]


def softplus(x):
    e = jnp.exp2(jnp.abs(x) * -LOG2E)
    small = e * (1.0 - e * (0.5 - e * (1.0 / 3.0 - e * 0.25)))
    return jnp.maximum(x, 0.0) + jnp.where(e < 0.03125, small, jnp.log2(1.0 + e) * LN2)


def one_minus_exp(s):
    small = s * (1.0 - s * (0.5 - s * (1.0 / 6.0 - s * (1.0 / 24.0))))
    return jnp.where(s < 0.0625, small, 1.0 - jnp.exp2(s * -LOG2E))


def front_kernel(ng, nc, order_ref, proj_ref, sw_ref, bias_ref, drive_ref, z_ref, dg_ref, dlog_ref, skip_ref, normed_hbm, cot_hbm, low_hbm, w_hbm,
                 gated_ref, dz_ref, step_ref, dy_ref, hprev_ref, ag_ref, wg_ref, part_ref, gskip_ref, kz_ref, sz_ref, ko_ref, so_ref, km_ref, sm_ref,
                 step_s, sd_s, dy_s, sig_s, keep_s, bt_s, ct_s, cbd_s, rc_s, hg_s, g_s, qg_s, st_f, st_h, st_q, gated_s, dzs_s, normed_ref, cot_ref, low_ref, w_ref, sems):
    lc, c = drive_ref.shape
    p = proj_ref.shape[1]
    n = dlog_ref.shape[0]
    r = p - 2 * n
    tn = T * n
    nb = lc // T
    groups = c // 256
    i = pl.program_id(0)
    pfx = order_ref[4]
    rate2 = -jnp.exp(dlog_ref[...]) * LOG2E
    lanes = [slice(g * 256, (g + 1) * 256) for g in range(groups)]

    def positions(chunk):
        return iota((lc, 1), 0) + chunk * lc

    def col(ref, t0, k):
        one = jnp.broadcast_to(pltpu.roll(ref[...], lax.rem(lc - t0, lc), 1)[:, k : k + 1], (n, 128))
        return jnp.concatenate([one, one], axis=1)

    @pl.when(i == 0)
    def _():
        st_f[...] = jnp.zeros_like(st_f)
        st_h[...] = jnp.zeros_like(st_h)
        st_q[...] = jnp.zeros_like(st_q)
        gskip_ref[...] = jnp.zeros_like(gskip_ref)

    proj = proj_ref[...]
    bt_s[...] = mm_nt(pick(r, p, n), proj)

    @pl.when(i < ng)
    def _():
        chunk = ng - 1 - i
        step = softplus(mm(proj[:, :r], sw_ref[...]) + bias_ref[...])
        keep_s[chunk] = step

        @pl.when(chunk * lc < pfx)
        def _():
            mask = (positions(chunk) < pfx).astype(F32)
            split(step_s, step)
            split(sd_s, step * drive_ref[...].astype(F32) * mask)
            base = chunk * (lc * n)

            def body(ir, state):
                t0 = (nb - 1 - ir) * T
                state = list(state)
                bt = bt_s[:, t0 : t0 + T]
                for k in range(T - 1, -1, -1):
                    t = t0 + k
                    bb = jnp.broadcast_to(bt[:, k : k + 1], (n, 128))
                    bb = jnp.concatenate([bb, bb], axis=1)
                    at = pl.ds(pl.multiple_of(base + t * n, n), n)
                    for g in range(groups):
                        q = jnp.exp2(row(step_s, g, t, n) * rate2[:, lanes[g]]) * state[g]
                        state[g] = q + bb * row(sd_s, g, t, n)
                        qg_s[at, lanes[g]] = q.astype(BF)
                        g_s[at, lanes[g]] = state[g].astype(BF)
                return tuple(state)

            out = tuple(st_f[g] for g in range(groups))
            for ir in range(nb):
                out = body(ir, out)
            for g in range(groups):
                st_f[g] = out[g]

    @pl.when(jnp.logical_and(i >= ng, i < ng + nc))
    def _():
        chunk = i - ng

        @pl.when(chunk < ng)
        def _():
            step_ref[...] = keep_s[jnp.minimum(chunk, ng - 1)]

        @pl.when(chunk >= ng)
        def _():
            step_ref[...] = softplus(mm(proj[:, :r], sw_ref[...]) + bias_ref[...])

        step = step_ref[...]
        drive = drive_ref[...].astype(F32)
        z = z_ref[...]
        sig = 1.0 / (1.0 + jnp.exp2(z * -LOG2E))
        sig_s[...] = sig
        dy = dg_ref[...] * (z * sig)
        dy_ref[...] = dy
        gskip_ref[...] += jnp.sum(dy * drive, axis=0, keepdims=True)
        split(step_s, step)
        split(sd_s, step * drive)
        ct_s[...] = mm_nt(pick(r + n, p, n), proj)
        cbd_s[...] = jnp.where(blockdiag(lc, n), mm(proj, spread(r + n, p, n)), 0.0).astype(BF)
        diag = blockdiag(T, n)

        def mxu(b, buf):
            rows = pl.ds(b * T, T)
            kept = {}

            def y_part(g):
                kept[g] = mm(cbd_s[rows, :], hg_s[buf, :, lanes[g]])

            def r_part(g):
                x = mm_nt(dy_ref[rows, lanes[g]].astype(BF), hg_s[buf, :, lanes[g]])
                kept["r"] = x if g == 0 else kept["r"] + x
                if g == groups - 1:
                    rc_s[rows, :] = jnp.where(diag, kept["r"], 0.0).astype(BF)

            def end(g):
                ln = lanes[g]
                y = kept[g] + skip_ref[:, ln] * drive_ref[rows, ln].astype(F32)
                zz = z_ref[rows, ln]
                sg = sig_s[rows, ln]
                gated_ref[rows, ln] = (y * (zz * sg)).astype(BF)
                dz_ref[rows, ln] = (dg_ref[rows, ln] * y * (sg * (1.0 + zz * (1.0 - sg)))).astype(BF)

            return [functools.partial(f, g) for g in range(groups) for f in (y_part, r_part, end)]

        def vpu(with_g, b, buf, state, pieces=()):
            hs, hbs, qs = (list(s) for s in state)
            pieces = list(pieces)
            t0 = b * T
            bt = bt_s[:, t0 : t0 + T]
            ct = ct_s[:, t0 : t0 + T] if with_g else None
            base = jnp.minimum(chunk, ng - 1) * (lc * n)
            for k in range(T):
                t = t0 + k
                bb = jnp.broadcast_to(bt[:, k : k + 1], (n, 128))
                bb = jnp.concatenate([bb, bb], axis=1)
                if with_g:
                    cc = jnp.broadcast_to(ct[:, k : k + 1], (n, 128))
                    cc = jnp.concatenate([cc, cc], axis=1)
                at = pl.ds(t * n, n)
                far = pl.ds(pl.multiple_of(base + t * n, n), n)
                for g in range(groups):
                    ln = lanes[g]
                    e = jnp.exp2(row(step_s, g, t, n) * rate2[:, ln])
                    hprev_ref[at, ln] = hbs[g]
                    hs[g] = e * hs[g] + bb * row(sd_s, g, t, n)
                    hbs[g] = hs[g].astype(BF)
                    if with_g:
                        hg_s[buf, pl.ds(k * n, n), ln] = hbs[g] + g_s[far, ln]
                        ag = cc * row(dy_s, g, t, n) + qs[g]
                        qs[g] = e * ag
                        agb = ag.astype(BF)
                        ag_ref[at, ln] = agb
                        wg_ref[at, ln] = agb * qg_s[far, ln]
                    else:
                        hg_s[buf, pl.ds(k * n, n), ln] = hbs[g]
                if k % 2 and pieces:
                    pieces.pop(0)()
            for f in pieces:
                f()
            return tuple(hs), tuple(hbs), tuple(qs)

        def run(with_g):
            many = range(groups)
            state = tuple(st_f[g + groups] for g in many), tuple(st_h[g] for g in many), tuple(st_q[g] for g in many)
            state = vpu(with_g, 0, 0, state)
            for b in range(1, nb):
                state = vpu(with_g, b, b, state, mxu(b - 1, b - 1))
            for f in mxu(nb - 1, nb - 1):
                f()
            for g in many:
                st_f[g + groups] = state[0][g]
                st_h[g] = state[1][g]
                st_q[g] = state[2][g]

        live = jnp.logical_and(chunk < ng, chunk * lc < pfx)

        @pl.when(live)
        def _():
            mask = (positions(chunk) < pfx).astype(F32)
            split(dy_s, dy * mask)
            run(True)

            @pl.when(pfx < (chunk + 1) * lc)
            def _():
                keep = iota((lc * n, c), 0) + chunk * (lc * n) < pfx * n
                ag_ref[...] = jnp.where(keep, ag_ref[...].astype(F32), 0.0).astype(BF)

        @pl.when(jnp.logical_not(live))
        def _():
            run(False)

        part_ref[...] = mm(rc_s[...], fold(r + n, p, n))
        spot = pl.ds(pl.multiple_of(chunk * lc, lc), lc)
        gated_s[spot, :] = gated_ref[...]
        dzs_s[spot, :] = dz_ref[...]

    tn_dims = (((0,), (0,)), ((), ()))
    copies = [pltpu.make_async_copy(a, b, sems.at[j]) for j, (a, b) in enumerate(((normed_hbm, normed_ref), (cot_hbm, cot_ref), (low_hbm, low_ref), (w_hbm, w_ref)))]

    @pl.when(i == 1)
    def _():
        for copy in copies:
            copy.start()

    @pl.when(i == ng + nc)
    def _():
        for copy in copies:
            copy.wait()

    for late, (zo_ref, oo_ref, mo_ref) in enumerate(((sz_ref, so_ref, sm_ref), (kz_ref, ko_ref, km_ref))):
        @pl.when(i == ng + nc + late)
        def _(late=late, zo_ref=zo_ref, oo_ref=oo_ref, mo_ref=mo_ref):
            side = lambda j: order_ref[j] if late else 1 - order_ref[j]
            rows = gated_s.shape[0] // 2
            wide = normed_ref[:, pl.ds(pl.multiple_of(side(0) * (normed_ref.shape[1] // 2), 128), normed_ref.shape[1] // 2)]
            zo_ref[...] = lax.dot_general(wide, dzs_s[...], tn_dims, preferred_element_type=F32).astype(BF)
            cols = gated_s[:, pl.ds(pl.multiple_of(side(1) * (c // 2), 128), c // 2)]
            oo_ref[...] = lax.dot_general(cols, cot_ref[...], tn_dims, preferred_element_type=F32).astype(BF)
            here = pl.ds(pl.multiple_of(side(2) * rows, 8), rows)
            mix = mm(gated_s[here, :], w_ref[...])
            mo_ref[...] = (mix + jnp.where(order_ref[3] == 0, low_ref[here, :].astype(F32), 0.0)).astype(BF)


def back_kernel(ng, top, low, far, prefix_ref, proj_ref, sw_ref, drive_ref, step_ref, dy_ref, h_ref, pin_ref, dlog_ref, skip_ref, *refs):
    (part_ref, dpre_ref, ddrive_ref, po_ref, ao_ref, gbias_ref, step_s, dy_s, p_s, ct_s, bbd_s, rb_s, ds_s, v_s, w_s, sw_s) = refs[far:]
    lc, c = drive_ref.shape
    p = proj_ref.shape[1]
    n = dlog_ref.shape[0]
    r = p - 2 * n
    tn = T * n
    nb = lc // T
    groups = c // 256
    i = pl.program_id(0)
    chunk = top - i
    rate2 = -jnp.exp(dlog_ref[...]) * LOG2E
    rate2b = rate2.astype(BF)
    lanes = [slice(g * 256, (g + 1) * 256) for g in range(groups)]

    @pl.when(i == 0)
    def _():
        sw_s[...] = jnp.zeros_like(sw_s)
        sw_s[pl.ds(0, r), :] = sw_ref[...]
        if far >= 6:
            pc_ref, ac_ref, bc_ref = refs[far - 6 : far - 3]
            for g in range(groups):
                p_s[g] = pc_ref[:, lanes[g]]
            ao_ref[...] = ac_ref[...]
            gbias_ref[...] = bc_ref[...]
        else:
            p_s[...] = jnp.zeros_like(p_s)
            ao_ref[...] = jnp.zeros_like(ao_ref)
            gbias_ref[...] = jnp.zeros_like(gbias_ref)

    ag_ref, wg_ref = refs[:2] if low < ng else (None, None)
    proj = proj_ref[...]
    split(step_s, step_ref[...])
    split(dy_s, dy_ref[...])
    ct_s[...] = mm_nt(pick(r + n, p, n), proj)
    bbd_s[...] = jnp.where(blockdiag(lc, n), mm(proj, spread(r, p, n)), 0.0).astype(BF)
    diag = blockdiag(T, n)
    ones = diag.astype(BF)
    gather = (lax.rem(iota((n, tn // 2), 1), n) == iota((n, tn // 2), 0)).astype(BF)

    never = prefix_ref[0] < 0
    done = {}

    def vpu(with_g, b, buf, state, pieces=()):
        ps = list(state)
        seen = done.get(b + 3, {})
        pieces = list(pieces)
        held = [None] * groups
        t0 = b * T
        ct = ct_s[:, t0 : t0 + T]
        for k in range(T - 1, -1, -1):
            t = t0 + k
            for g in range(groups):
                key = {T - 1: ("s", g), T // 2: ("v", g), T // 4: ("w", g)}.get(k)
                if key in seen:
                    ps[g] = jnp.where(never, seen[key], ps[g])
            cc = jnp.broadcast_to(ct[:, k : k + 1], (n, 128))
            cc = jnp.concatenate([cc, cc], axis=1)
            at = pl.ds(t * n, n)
            for g in range(groups):
                ln = lanes[g]
                st = row(step_s, g, t, n)
                e = jnp.exp2(st * rate2[:, ln])
                ah = cc * row(dy_s, g, t, n) + ps[g]
                ps[g] = e * ah
                dsrc = ah.astype(BF)
                w = ps[g].astype(BF) * h_ref[at, ln]
                if with_g:
                    dsrc = dsrc + ag_ref[at, ln]
                    w = w + wg_ref[at, ln]
                ds_s[buf, pl.ds(k * n, n), ln] = dsrc
                v_s[buf, pl.ds(k * n, n), ln] = w * rate2b[:, ln]
                ws = w * st.astype(BF)
                if k % 2:
                    held[g] = ws
                else:
                    w_s[buf, pl.ds(k // 2 * n, n), ln] = held[g] + ws
            if k % 2 == 0 and pieces:
                pieces.pop(0)()
        for f in pieces:
            f()
        return tuple(ps)

    def mxu(b, buf):
        rows = pl.ds(b * T, T)
        kept = done[b] = {}

        def s_part(g):
            kept["s", g] = mm(bbd_s[rows, :], ds_s[buf, :, lanes[g]])

        def v_part(g):
            kept["v", g] = mm(ones, v_s[buf, :, lanes[g]])
            kept["w", g] = mm(gather, w_s[buf, :, lanes[g]])
            ao_ref[:, lanes[g]] += kept["w", g]

        def r_part(g):
            ln = lanes[g]
            sd = step_ref[rows, ln] * drive_ref[rows, ln].astype(F32)
            x = mm_nt(sd.astype(BF), ds_s[buf, :, ln])
            kept["r"] = x if g == 0 else kept["r"] + x
            if g == groups - 1:
                rb_s[rows, :] = jnp.where(diag, kept["r"], 0.0).astype(BF)

        def end(g):
            ln = lanes[g]
            step = step_ref[rows, ln]
            ssum = kept["s", g]
            drive = drive_ref[rows, ln].astype(F32)
            dpre = (kept["v", g] * LN2 + drive * ssum) * one_minus_exp(step)
            dpre_ref[rows, ln] = dpre.astype(BF)
            ddrive_ref[rows, ln] = skip_ref[:, ln] * dy_ref[rows, ln] + step * ssum
            gbias_ref[:, ln] += jnp.sum(dpre, axis=0, keepdims=True)

        return [functools.partial(f, g) for g in range(groups) for f in (s_part, v_part, r_part, end)]

    def run(with_g):
        done.clear()
        many = range(groups)
        state = tuple(p_s[g] for g in many)
        state = vpu(with_g, nb - 1, nb - 1, state)
        for b in range(nb - 2, -1, -1):
            state = vpu(with_g, b, b, state, mxu(b + 1, b + 1))
        for f in mxu(0, 0):
            f()
        for g in many:
            p_s[g] = state[g]

    if low >= ng:
        run(False)
    else:
        live = jnp.logical_and(chunk < ng, chunk * lc < prefix_ref[0])

        @pl.when(live)
        def _():
            run(True)

        @pl.when(jnp.logical_not(live))
        def _():
            run(False)

    part_ref[...] = (pin_ref[...] + mm(rb_s[...], fold(r, p, n)) + mm_nt(dpre_ref[...], sw_s[...])).astype(part_ref.dtype)
    po_ref[...] = jnp.concatenate([p_s[g] for g in range(groups)], axis=1)


def whole(*s):
    return pl.BlockSpec(s, lambda i: (0,) * len(s))


SMEM = pl.BlockSpec(memory_space=pltpu.SMEM)


def head_kernel(low_ref, gain_ref, w_ref, cw_ref, cb_ref, xw_ref, normed_ref, x_ref, slope_ref, drive_ref, part_ref, rs_ref, edge_s):
    taps = cw_ref.shape[0]
    lc = low_ref.shape[0]

    @pl.when(pl.program_id(0) == 0)
    def _():
        edge_s[...] = jnp.zeros_like(edge_s)

    xf = low_ref[...].astype(F32)
    rs = lax.rsqrt(jnp.mean(xf * xf, axis=-1, keepdims=True) + epsilon)
    rs_ref[...] = rs
    normed = (xf * rs * gain_ref[...]).astype(BF)
    normed_ref[...] = normed
    x = mm(normed, w_ref[...])
    x_ref[...] = x.astype(BF)
    wide = jnp.concatenate([edge_s[...], x], axis=0)
    edge_s[...] = x[lc - 8 :]
    out = cb_ref[...] + cw_ref[taps - 1 :, :] * x
    for k in range(taps - 1):
        at = 8 - (taps - 1) + k
        out = out + cw_ref[k : k + 1, :] * wide[at : at + lc]
    sc = sigmoid(out)
    act = out * sc
    slope_ref[...] = sc * (1.0 + out - act)
    drive = act.astype(BF)
    drive_ref[...] = drive
    part_ref[...] = mm_nt(drive, xw_ref[...]).astype(BF)


def head(low, gain, w_all, conv_weight, conv_bias, xproj_t):
    l, d = low.shape
    c = w_all.shape[1] // 2
    p = xproj_t.shape[0]
    hc = 256
    by = lambda w: pl.BlockSpec((hc, w), lambda i: (i, 0))
    s = jax.ShapeDtypeStruct
    return pl.pallas_call(
        head_kernel,
        grid=(l // hc,),
        in_specs=[by(d), whole(1, d), whole(d, c), whole(*conv_weight.shape), whole(1, c), whole(p, c)],
        out_specs=[by(d), by(c), by(c), by(c), by(p), by(1)],
        out_shape=[s((l, d), BF), s((l, c), BF), s((l, c), F32), s((l, c), BF), s((l, p), BF), s((l, 1), F32)],
        scratch_shapes=[pltpu.VMEM((8, c), F32)],
        compiler_params=pltpu.CompilerParams(vmem_limit_bytes=60 << 20),
        cost_estimate=pl.CostEstimate(flops=2 * l * d * c, transcendentals=l * c, bytes_accessed=4 * l * d + 2 * d * c + 6 * l * c),
        name="head",
    )(low, gain.reshape(1, d), w_all, conv_weight, conv_bias.reshape(1, c), xproj_t)


def gates_kernel(n_ref, w_ref, c_ref, o_ref, z_ref, dg_ref):
    z_ref[...] = mm(n_ref[...], w_ref[...])
    dg_ref[...] = mm_nt(c_ref[...], o_ref[...])


def gates(normed, w_all, cot, out_weight):
    l, d = normed.shape
    c = w_all.shape[1] // 2
    by = lambda w: pl.BlockSpec((256, w), lambda i: (i, 0))
    s = jax.ShapeDtypeStruct
    return pl.pallas_call(
        gates_kernel,
        grid=(l // 256,),
        in_specs=[by(d), pl.BlockSpec((d, c), lambda i: (0, 1)), by(d), whole(c, d)],
        out_specs=[by(c), by(c)],
        out_shape=[s((l, c), F32), s((l, c), F32)],
        compiler_params=pltpu.CompilerParams(vmem_limit_bytes=60 << 20),
        cost_estimate=pl.CostEstimate(flops=4 * l * d * c, transcendentals=0, bytes_accessed=4 * (l * d + d * c + 2 * l * c)),
        name="gates",
    )(normed, w_all, cot, out_weight)


def inner_kernel(rows_a, rows_b, bits_ref, dproj_ref, ds_ref, x_ref, slope_ref, drive_ref, dz_ref, normed_ref, low_ref, rs_ref, w_ref, xw_ref, cw_ref,
                 gb_ref, gd_ref, dlog_ref, gk_ref, proj_ref, dpre_ref, ka_ref, sa_ref, kb_ref, sb_ref, kn_ref, sn_ref, gn_ref, edge_s, gin_s, gx_s, gs_s, gc_s, gn_s, la_s, lb_s):
    taps = cw_ref.shape[0]
    lc, c = ds_ref.shape
    d = normed_ref.shape[1]
    p = dproj_ref.shape[1]
    n = gd_ref.shape[0]
    r = p - 2 * n
    i = pl.program_id(0)
    last = pl.num_programs(0) - 1
    tn = (((0,), (0,)), ((), ()))

    @pl.when(i == 0)
    def _():
        edge_s[...] = jnp.zeros_like(edge_s)
        gin_s[...] = jnp.zeros_like(gin_s)
        gx_s[...] = jnp.zeros_like(gx_s)
        gs_s[...] = jnp.zeros_like(gs_s)
        gc_s[...] = jnp.zeros_like(gc_s)
        gn_s[...] = jnp.zeros_like(gn_s)

    dproj = dproj_ref[...]
    x = x_ref[...].astype(F32)
    dconv = (ds_ref[...] + mm(dproj, xw_ref[...])) * slope_ref[...]
    gc_s[pl.ds(taps, 1), :] += jnp.sum(dconv, axis=0, keepdims=True)
    ahead = jnp.concatenate([dconv, edge_s[...]], axis=0)
    edge_s[...] = dconv[:8]
    dx = cw_ref[taps - 1 :, :] * dconv
    gc_s[pl.ds(taps - 1, 1), :] += jnp.sum(dconv * x, axis=0, keepdims=True)
    for k in range(taps - 1):
        by = taps - 1 - k
        moved = ahead[by : by + lc]
        dx = dx + cw_ref[k : k + 1, :] * moved
        gc_s[pl.ds(k, 1), :] += jnp.sum(moved * x, axis=0, keepdims=True)
    dx = dx.astype(BF)
    normed = normed_ref[...]
    gin_s[...] += lax.dot_general(normed, dx, tn, preferred_element_type=F32)
    gx_s[...] += lax.dot_general(dproj, drive_ref[...], tn, preferred_element_type=F32)
    gs_s[...] += lax.dot_general(proj_ref[:, :r], dpre_ref[...], tn, preferred_element_type=F32)
    dn = mm_nt(jnp.concatenate([dx, dz_ref[...]], axis=1), w_ref[...])
    half = pl.num_programs(0) // 2

    keeps = (i < half) == (bits_ref[2] == 1)

    @pl.when(jnp.logical_not(keeps))
    def _():
        sn_ref[...] = dn.astype(BF)

    @pl.when(keeps)
    def _():
        kn_ref[...] = dn.astype(BF)

    gn_s[...] += jnp.sum(dn * (low_ref[...].astype(F32) * rs_ref[...]), axis=0, keepdims=True)

    @pl.when(i == last)
    def _():
        gn_ref[...] = gn_s[...]
        lines = [gc_s[pl.ds(0, taps + 1), :], gb_ref[...], gk_ref[...]]
        lines = jnp.concatenate(lines + [jnp.zeros((16 - taps - 3, c), F32)], axis=0)
        top = 16 + n + r + p
        la_s[pl.ds(0, 16), :] = lines.astype(BF)
        la_s[pl.ds(16, n), :] = (gd_ref[...] * -jnp.exp(dlog_ref[...])).astype(BF)
        la_s[pl.ds(16 + n, r), :] = gs_s[...].astype(BF)
        la_s[pl.ds(16 + n + r, p), :] = gx_s[...].astype(BF)
        la_s[pl.ds(top, rows_a - top), :] = gin_s[pl.ds(0, rows_a - top), :].astype(BF)
        rest = d - (rows_a - top)
        lb_s[pl.ds(0, rest), :] = gin_s[pl.ds(rows_a - top, rest), :].astype(BF)
        if rows_b > rest:
            lb_s[pl.ds(rest, rows_b - rest), :] = jnp.zeros((rows_b - rest, c), BF)
        for bit, total, keep_ref, send_ref in ((bits_ref[0], la_s, ka_ref, sa_ref), (bits_ref[1], lb_s, kb_ref, sb_ref)):
            rows = keep_ref.shape[0]
            keep_ref[...] = total[pl.ds(pl.multiple_of(bit * rows, 8), rows), :]
            send_ref[...] = total[pl.ds(pl.multiple_of((1 - bit) * rows, 8), rows), :]


def inner(rows_a, rows_b, bits, dproj, ddrive, x, slope, drive, dz, normed, low, rs, w_all, xproj_t, conv_weight, g_bias, g_decay, decay_log, g_skip, proj, dpre):
    l, c = x.shape
    d = normed.shape[1]
    p = dproj.shape[1]
    n = g_decay.shape[0]
    hc = 256
    nc = l // hc
    by = lambda w: pl.BlockSpec((hc, w), lambda i, bits: (nc - 1 - i, 0))
    full = lambda *q: pl.BlockSpec(q, lambda i, bits: (0,) * len(q))
    s = jax.ShapeDtypeStruct
    v = pltpu.VMEM
    early = lambda i: jnp.maximum(nc // 2 - 1 - i, 0)
    late = lambda i: jnp.minimum(nc - 1 - i, nc // 2 - 1)
    kept = pl.BlockSpec((hc, d), lambda i, bits: (jnp.where(bits[2] == 1, early(i), late(i)), 0))
    sent = pl.BlockSpec((hc, d), lambda i, bits: (jnp.where(bits[2] == 1, late(i), early(i)), 0))
    return pl.pallas_call(
        functools.partial(inner_kernel, rows_a, rows_b),
        grid_spec=pltpu.PrefetchScalarGridSpec(
            num_scalar_prefetch=1,
            grid=(nc,),
            in_specs=[by(p), by(c), by(c), by(c), by(c), by(c), by(d), by(d), by(1), full(d, 2 * c), full(p, c), full(*conv_weight.shape),
                      full(1, c), full(n, c), full(n, c), full(1, c), by(p), by(c)],
            out_specs=[full(rows_a // 2, c)] * 2 + [full(rows_b // 2, c)] * 2 + [kept, sent, full(1, d)],
            scratch_shapes=[v((8, c), F32), v((d, c), F32), v((p, c), F32), v((p - 2 * n, c), F32), v((8, c), F32), v((1, d), F32), v((rows_a, c), BF), v((rows_b, c), BF)],
        ),
        out_shape=[s((rows_a // 2, c), BF)] * 2 + [s((rows_b // 2, c), BF)] * 2 + [s((l // 2, d), BF)] * 2 + [s((1, d), F32)],
        compiler_params=pltpu.CompilerParams(vmem_limit_bytes=60 << 20),
        cost_estimate=pl.CostEstimate(flops=6 * l * d * c, transcendentals=l * c, bytes_accessed=10 * l * d),
        name="inner",
    )(bits, dproj, ddrive, x, slope, drive, dz, normed, low, rs, w_all, xproj_t, conv_weight, g_bias, g_decay, decay_log, g_skip, proj, dpre)


def merge_kernel(kinds, bits_ref, *refs):
    take = list(refs)
    ins = [[take.pop(0) for _ in range(2 + EXTRA[kind])] for kind in kinds]
    for j, (kind, (one, two, *more)) in enumerate(zip(kinds, ins)):
        rows = one.shape[0]
        if kind == "join":
            out = take.pop(0)
            out[pl.ds(pl.multiple_of(bits_ref[j] * rows, 8), rows), :] = one[...]
            out[pl.ds(pl.multiple_of((1 - bits_ref[j]) * rows, 8), rows), :] = two[...]
        elif kind == "split":
            half = rows // 2
            for out, at in ((take.pop(0), bits_ref[j]), (take.pop(0), 1 - bits_ref[j])):
                part = pl.ds(pl.multiple_of(at * half, 8), half)
                out[...] = (one[part, :].astype(F32) + two[part, :].astype(F32)).astype(BF)
        else:
            total = one[...].astype(F32) + two[...].astype(F32)
            if kind == "shift":
                total = total + more[0][...].astype(F32)
            if kind == "norm":
                x_ref, rs_ref, gain_ref = more
                x, rs = x_ref[...].astype(F32), rs_ref[...]
                scaled = total * gain_ref[...]
                total = rs * scaled - x * (rs * rs * rs) * jnp.mean(scaled * x, axis=-1, keepdims=True)
            take.pop(0)[...] = total.astype(BF)


EXTRA = dict(join=0, split=0, sum=0, shift=1, norm=3)


def once(*shape):
    return pl.BlockSpec(shape, lambda i: (0,) * len(shape), pipeline_mode=pl.Buffered(1))


def merge(items):
    kinds = tuple(item[0] for item in items)
    bits = jnp.stack([jnp.asarray(item[1], jnp.int32) for item in items])
    arrays = [v for item in items for v in item[2:]]
    shapes = []
    for kind, _, one, *_ in items:
        rows, cols = one.shape
        many = {"join": [2 * rows], "split": [rows // 2] * 2}.get(kind, [rows])
        shapes.append([jax.ShapeDtypeStruct((q, cols), BF) for q in many])
    flat = [q for group in shapes for q in group]
    homes = [len(group) == 2 and j == 0 for group in shapes for j in range(len(group))]
    out = list(pl.pallas_call(
        functools.partial(merge_kernel, kinds),
        grid=(1,),
        in_specs=[SMEM] + [once(*v.shape) for v in arrays],
        out_specs=[once(*v.shape) for v in flat],
        out_shape=[pltpu.HBM(q.shape, q.dtype) if kept else q for q, kept in zip(flat, homes)],
        compiler_params=pltpu.CompilerParams(vmem_limit_bytes=24 << 20),
        name="merge",
    )(bits, *arrays))
    return [[out.pop(0) for _ in group] for group in shapes]


def joined_kernel(bits_ref, one_ref, two_ref, *refs):
    out_ref = refs[-1]
    rows = one_ref.shape[0]
    for at, part in ((bits_ref[0], one_ref), (1 - bits_ref[0], two_ref)):
        where = pl.ds(pl.multiple_of(at * rows, 8), rows)
        value = part[...].astype(F32)
        out_ref[where, :] = value if len(refs) == 1 else value + refs[0][where, :].astype(F32)


def joined(bit, one, two, *add):
    vm = pl.BlockSpec(memory_space=pltpu.VMEM)
    shape = (2 * one.shape[0], one.shape[1])
    return pl.pallas_call(
        joined_kernel,
        in_specs=[SMEM] + [vm] * (2 + len(add)),
        out_specs=vm,
        out_shape=jax.ShapeDtypeStruct(shape, F32),
        compiler_params=pltpu.CompilerParams(vmem_limit_bytes=24 << 20),
        name="joined",
    )(bit.astype(jnp.int32).reshape(1), one, two, *add)


def last_kernel(n, r, p, taps, bits_ref, sa_ref, oa_ref, sb_ref, ob_ref, sz_ref, oz_ref, gin_ref, gc_ref, gcb_ref, gb_ref, gk_ref, gd_ref, gs_ref, gx_ref, all_s, z_s):
    top = 16 + n + r + p
    hc = gin_ref.shape[0]

    @pl.when(pl.program_id(0) == 0)
    def _():
        base = 0
        for j, mine, other, whole_s in ((0, sa_ref, oa_ref, all_s), (1, sb_ref, ob_ref, all_s), (2, sz_ref, oz_ref, z_s)):
            half = mine.shape[0]
            base = 0 if j == 2 else base
            whole_s[pl.ds(pl.multiple_of(base + bits_ref[j] * half, 8), half), :] = mine[...]
            whole_s[pl.ds(pl.multiple_of(base + (1 - bits_ref[j]) * half, 8), half), :] = other[...]
            base += 2 * half
        lines = all_s[pl.ds(0, 16), :].astype(F32)
        gc_ref[...] = lines[:taps]
        gcb_ref[...] = lines[taps : taps + 1]
        gb_ref[...] = lines[taps + 1 : taps + 2]
        gk_ref[...] = lines[taps + 2 : taps + 3]
        gd_ref[...] = all_s[pl.ds(16, n), :].astype(F32)
        gs_ref[...] = all_s[pl.ds(16 + n, r), :].astype(F32)
        gx_ref[...] = all_s[pl.ds(16 + n + r, p), :].astype(F32)

    at = pl.program_id(0) * hc
    gin_ref[:, 0, :] = all_s[pl.ds(pl.multiple_of(top + at, 8), hc), :].astype(F32)
    gin_ref[:, 1, :] = z_s[pl.ds(pl.multiple_of(at, 8), hc), :].astype(F32)


def last(bits, sa, oa, sb, ob, sz, oz, n, r, p, taps):
    half, c = sz.shape
    hc = 256
    s = jax.ShapeDtypeStruct
    small = [s((taps, c), F32), s((1, c), F32), s((1, c), F32), s((1, c), F32), s((n, c), F32), s((r, c), F32), s((p, c), F32)]
    arrays = [sa, oa, sb, ob, sz, oz]
    return pl.pallas_call(
        functools.partial(last_kernel, n, r, p, taps),
        grid=(2 * half // hc,),
        in_specs=[SMEM] + [once(*v.shape) for v in arrays],
        out_specs=[pl.BlockSpec((hc, 2, c), lambda i: (i, 0, 0))] + [whole(*v.shape) for v in small],
        out_shape=[s((2 * half, 2, c), F32)] + small,
        scratch_shapes=[pltpu.VMEM((2 * sa.shape[0] + 2 * sb.shape[0], c), BF), pltpu.VMEM((2 * half, c), BF)],
        compiler_params=pltpu.CompilerParams(vmem_limit_bytes=24 << 20),
        name="last",
    )(bits, *arrays)


def front(order, proj, sw, bias, drive, z, dg, dlog, skip, normed, cot, low, out_weight):
    l, c = drive.shape
    d = low.shape[1]
    p = proj.shape[1]
    n = dlog.shape[0]
    ng = l // 2 // LC
    nc = l // LC
    s = jax.ShapeDtypeStruct
    fwd = lambda i, o: (jnp.clip(i - ng, 0, nc - 1), 0)
    both = lambda i, o: (jnp.where(i < ng, ng - 1 - i, jnp.minimum(i - ng, nc - 1)), 0)
    half = lambda i, o: (jnp.clip(i - ng, 0, ng - 1), 0)
    full = lambda *q: pl.BlockSpec(q, lambda i, o: (0,) * len(q))
    once = lambda *q: pl.BlockSpec(q, lambda i, o: (0,) * len(q), pipeline_mode=pl.Buffered(1))
    B = pl.BlockSpec
    lanes = c // 128
    v = pltpu.VMEM
    return pl.pallas_call(
        functools.partial(front_kernel, ng, nc),
        grid_spec=pltpu.PrefetchScalarGridSpec(
            num_scalar_prefetch=1,
            grid=(ng + nc + 2,),
            in_specs=[B((LC, p), both), full(*sw.shape), full(1, c), B((LC, c), both), B((LC, c), fwd), B((LC, c), fwd), full(n, c), full(1, c),
                      ] + [B(memory_space=pl.ANY)] * 4,
            out_specs=[B((LC, c), fwd), B((LC, c), fwd), B((LC, c), fwd), B((LC, c), fwd), B((LC * n, c), fwd), B((LC * n, c), half), B((LC * n, c), half), B((LC, p), fwd), full(1, c)]
                + [once(d // 2, c)] * 2 + [once(c // 2, d)] * 2 + [once(l // 2, d)] * 2,
            scratch_shapes=[v((lanes, LC, 128), F32)] * 3 + [v((LC, c), F32), v((ng, LC, c), F32), v((n, LC), F32), v((n, LC), F32), v((LC, T * n), BF), v((LC, T * n), BF),
                v((LC // T, T * n, c), BF), v((l // 2 * n, c), BF), v((l // 2 * n, c), BF), v((c // 128, n, 256), F32), v((c // 256, n, 256), BF), v((c // 256, n, 256), F32), v((l, c), BF), v((l, c), BF),
                v((l, d), BF), v((l, d), BF), v((l, d), BF), v((c, d), BF), pltpu.SemaphoreType.DMA((4,))],
        ),
        out_shape=[s((l, c), BF), s((l, c), BF), s((l, c), F32), s((l, c), F32), s((l * n, c), BF), s((l // 2 * n, c), BF), s((l // 2 * n, c), BF), s((l, p), F32), s((1, c), F32)]
            + [s((d // 2, c), BF)] * 2 + [s((c // 2, d), BF)] * 2 + [s((l // 2, d), BF)] * 2,
        compiler_params=pltpu.CompilerParams(vmem_limit_bytes=60 << 20),
        name="front",
    )(order, proj, sw, bias.reshape(1, c), drive, z, dg, dlog, skip.reshape(1, c), normed, cot, low, out_weight)


def back(prefix, proj, sw, drive, step, dy, hprev, ag, wg, pin, dlog, skip, carry, top, low, filled=()):
    l, c = drive.shape
    p = proj.shape[1]
    n = dlog.shape[0]
    ng = l // 2 // LC
    s = jax.ShapeDtypeStruct
    rev = lambda i: (top - i, 0)
    half = lambda i: (jnp.minimum(top - i, ng - 1), 0)
    B = pl.BlockSpec
    v = pltpu.VMEM
    ins = [SMEM, B((LC, p), rev), whole(*sw.shape), B((LC, c), rev), B((LC, c), rev), B((LC, c), rev), B((LC * n, c), rev), B((LC, p), rev), whole(n, c), whole(1, c)]
    extra, more = [], []
    if low < ng:
        extra, more = [ag, wg], [B((LC * n, c), half)] * 2
    if filled:
        extra, more = extra + list(carry) + list(filled), more + [whole(n, c), whole(n, c), whole(1, c)] + [B(memory_space=pl.ANY)] * 3
    first = len(ins) + len(extra) - 3
    return pl.pallas_call(
        functools.partial(back_kernel, ng, top, low, len(extra)),
        grid=(top - low + 1,),
        in_specs=ins + more,
        out_specs=[B((LC, p), rev), B((LC, c), rev), B((LC, c), rev), whole(n, c), whole(n, c), whole(1, c)],
        out_shape=[s((l, p), BF), s((l, c), BF), s((l, c), F32), s((n, c), F32), s((n, c), F32), s((1, c), F32)],
        input_output_aliases={first + j: j for j in range(3)} if filled else {},
        scratch_shapes=[v((c // 128, LC, 128), F32)] * 2 + [v((c // 256, n, 256), F32), v((n, LC), F32), v((LC, T * n), BF), v((LC, T * n), BF), v((LC // T, T * n, c), BF), v((LC // T, T * n, c), BF), v((LC // T, T * n // 2, c), BF), v((p, c), BF)],
        compiler_params=pltpu.CompilerParams(vmem_limit_bytes=60 << 20),
        cost_estimate=pl.CostEstimate(flops=(top - low + 1) * LC * n * c * 4000, transcendentals=0, bytes_accessed=(top - low + 1) * LC * n * c * 4),
        name="back",
    )(prefix, proj, sw, drive, step, dy, hprev, pin, dlog, skip.reshape(1, c), *extra)


def sigmoid(v):
    return 1.0 / (1.0 + jnp.exp(-v))


def exchange(value, name, size, bit):
    return lax.ppermute(value, name, [(j, j ^ (1 << bit)) for j in range(size)])


def bits_of(size):
    count = size.bit_length() - 1
    assert 1 << count == size
    return list(range(count))


class Chain:
    def __init__(self, name, size, order, keep, send, swap=True, middle=("sum", ())):
        order = list(order)
        self.name, self.size, self.keep, self.send, self.middle = name, size, keep, send, middle
        turn = [("swap", order.pop())] if swap else []
        self.steps = [("halve", bit) for bit in order] + turn + [("double", bit) for bit in reversed(order)]
        self.got = None
        self.far = False

    def mine(self, bit):
        return (lax.axis_index(self.name) >> bit) & 1

    def start(self, send):
        self.send = send
        return exchange(send, self.name, self.size, self.steps[0][1])

    def item(self):
        kind, bit = self.steps.pop(0)
        after = self.steps[0]
        if kind == "double":
            got = pltpu.with_memory_space_constraint(self.got, pltpu.HBM) if self.far else self.got
            return ("join", self.mine(bit), self.send, got)
        one = pltpu.with_memory_space_constraint(self.keep, pltpu.HBM) if kind == "halve" else self.send
        if kind == "halve" and after[0] == "halve":
            return ("split", self.mine(after[1]), one, self.got)
        if kind == "swap" or after[0] == "double":
            name, more = self.middle
            return (name, 0, one, self.got, *more)
        return ("sum", 0, one, self.got)

    def ended(self):
        return len(self.steps) == 1 and self.got is not None

    def accept(self, arrays):
        self.send = arrays[-1]
        self.keep = arrays[0]
        self.got = None


def ready(chains):
    live = [c for c in chains if c.got is not None and len(c.steps) > 1 and c not in PENDING]
    if live:
        for c, arrays in zip(live, merge([c.item() for c in live])):
            c.accept(arrays)


PENDING = []


def under(chains, work, *inputs, slow=()):
    waiting = [c for c in PENDING if c.got is not None]
    PENDING[:] = list(slow)
    chains = [c for c in chains if c.steps and c.got is None] + list(slow)
    sends, inputs = lax.optimization_barrier(([c.send for c in chains], inputs))
    got = [c.start(v) for c, v in zip(chains, sends)]
    result = work(*inputs)
    hold = len(chains) - len(slow)
    old = [c.got for c in waiting]
    heads, firsts, old, result = lax.optimization_barrier((sends[:hold], got[:hold], old, result))
    for c, v, w in zip(chains, list(heads) + list(sends[hold:]), list(firsts) + list(got[hold:])):
        c.send, c.got = v, w
    for c, w in zip(waiting, old):
        c.got = w
    return result


def on_device(sizes, tokens, prefix, norm_gain, in_weight, conv_weight, conv_bias, xproj_weight, step_weight, step_bias, decay_log, skip_gain, out_weight, out_cotangent):
    dp, tp = sizes
    seqs, length, width = tokens.shape
    assert seqs == 1
    channels = in_weight.shape[2]
    rank = step_weight.shape[0]
    taps = conv_weight.shape[0]
    n = decay_log.shape[0]
    p = rank + 2 * n
    low = tokens[0]
    cot = out_cotangent[0]
    w_all = lax.optimization_barrier(in_weight.reshape(width, 2 * channels))
    xproj_t = xproj_weight.T
    order = bits_of(dp)
    turned = order[1:] + order[:1]
    t_order = bits_of(tp)
    at = lax.axis_index("tensor")
    at_dp = lax.axis_index("dp")
    spot = 0
    rows = length
    for bit in t_order:
        rows //= 2
        spot = spot + ((at >> bit) & 1) * rows
    part_of = lambda v: lax.dynamic_slice_in_dim(v, spot, rows, 0)
    bit_of = lambda v, bit: (v >> bit) & 1

    normed, xpart, slope, drive, proj, rs = head(low, norm_gain, w_all, conv_weight, conv_bias, xproj_t)
    for bit in t_order[:-1]:
        proj = (proj.astype(F32) + exchange(proj, "tensor", tp, bit).astype(F32)).astype(BF)
    proj, n_in, c_in = lax.optimization_barrier((proj, normed, cot))
    other = exchange(proj, "tensor", tp, t_order[-1])
    zpart, dgated = gates(n_in, w_all, c_in, out_weight)
    other, zpart, dgated = lax.optimization_barrier((other, zpart, dgated))
    proj = (proj.astype(F32) + other.astype(F32)).astype(BF)

    picks = jnp.stack([bit_of(at_dp, order[0]), bit_of(at_dp, turned[0]), bit_of(at, t_order[0]), at, prefix[0]]).astype(jnp.int32)
    gated, dz, step, dy, hprev, ag, wg, pin, g_skip, kz, sz, ko, so, km, sm = front(picks, proj, step_weight, step_bias, drive, zpart, dgated, decay_log, skip_gain, normed, cot, low, out_weight)
    gz = Chain("dp", dp, order, kz, sz)
    go = Chain("dp", dp, turned, ko, so)
    mix = Chain("tensor", tp, t_order, km, sm, swap=False)
    gz.far = go.far = True
    chains = [gz, go, mix]
    nc = length // LC
    carry = ()
    filled = ()
    top = nc - 1
    for low_chunk in PIECES:
        def piece(d, carry, filled, top=top, low_chunk=low_chunk):
            return back(prefix, proj, step_weight, drive, step, d, hprev, ag, wg, pin, decay_log, skip_gain, carry, top, low_chunk, filled)

        *filled, p1, a1, b1 = under(chains, piece, dy, carry, tuple(filled))
        ready(chains)
        carry = (p1, a1, b1)
        top = low_chunk - 1
    dpart, dpre, ddrive_scan = filled
    _, g_decay, g_bias = carry

    for bit in t_order[:-1]:
        dpart = (dpart.astype(F32) + exchange(dpart, "tensor", tp, bit).astype(F32)).astype(BF)
    cross = Chain("tensor", tp, t_order[-1:], dpart, dpart)
    my_x, my_rs = under([gz, go, cross, mix], lambda v, w: (part_of(v), part_of(w)), low, rs)
    ready([gz, go])
    dproj = (cross.send.astype(F32) + cross.got.astype(F32)).astype(BF)
    total = 16 + n + p + rank + width
    total += -total % (16 << (len(order) - 1))
    rows_a = total // 2
    ka, sa, kb, sb, kn, sn, g_norm = under([gz, go], lambda v: inner(rows_a, total - rows_a, picks, v, ddrive_scan, xpart, slope, drive, dz, normed, low, rs, w_all, xproj_t, conv_weight, g_bias, g_decay, decay_log, g_skip, proj, dpre), dproj)
    la = Chain("dp", dp, order, ka, sa)
    lb = Chain("dp", dp, turned, kb, sb)
    dn = Chain("tensor", tp, t_order, kn, sn, swap=False, middle=("norm", (my_x, my_rs, norm_gain.reshape(1, width))))
    turns = [("tensor", tp, bit) for bit in reversed(t_order)] + [("dp", dp, bit) for bit in order]

    def gains(v):
        if turns:
            name, size, bit = turns.pop(0)
            v = v + exchange(v, name, size, bit)
        return v

    def closing(v, one, two, *out):
        joint = merge([("join", mix.mine(mix.steps[0][1]), *out)])[0][0] if mix.ended() else None
        return gains(v), joined(go.mine(go.steps[0][1]), one, two), joint

    block_out = None
    late = [[]]
    g_out = None
    while not la.ended():
        extra = late.pop(0) if late else [c for c in (gz, go) if not c.ended()]
        ready(extra + [la, lb, dn])
        final = len(la.steps) == 1
        slow = [dn] if dn.got is None and len(dn.steps) > 1 and dn.steps[0][1] != t_order[0] else []
        now = [dn] if dn.got is None and not slow and not final else []
        if final and go.ended():
            g_norm, g_out, block_out = under([la, lb] + now + extra, closing, g_norm, go.send, go.got, mix.send, mix.got, slow=slow)
        else:
            g_norm = under([la, lb] + now + extra, gains, g_norm, slow=slow)
    while turns:
        g_norm = gains(g_norm)
    for c in (dn, gz, go):
        while not c.ended():
            ready([c])
            under([c], lambda: ())
    flags = jnp.stack([c.mine(c.steps[0][1]) for c in (la, lb, gz)]).astype(jnp.int32)
    g_in, g_conv, g_convb, g_bias, g_skip, g_decay, g_step, g_xproj = last(flags, la.send, la.got, lb.send, lb.got, gz.send, gz.got, n, rank, p, taps)
    grad_tokens = joined(dn.mine(dn.steps[0][1]), dn.send, dn.got, cot)
    if g_out is None:
        g_out = joined(go.mine(go.steps[0][1]), go.send, go.got)
    if block_out is None:
        while not mix.ended():
            under([mix], lambda: ())
            ready([mix])
        block_out = merge([mix.item()] if len(mix.steps) > 1 else [("join", mix.mine(mix.steps[0][1]), mix.send, mix.got)])[0][0]
    return (block_out[None], grad_tokens[None], g_norm.reshape(-1), g_in, g_conv, g_convb[0], g_xproj.T, g_step, g_bias[0], g_decay, g_skip[0], g_out)


def solution(mesh):
    placed = (
        P("dp", None, None),
        P("dp"),
        P(),
        P(None, None, "tensor"),
        P(None, "tensor"),
        P("tensor"),
        P("tensor", None),
        P(None, "tensor"),
        P("tensor"),
        P(None, "tensor"),
        P("tensor"),
        P("tensor", None),
        P("dp", None, None),
    )
    results = (
        P("dp", None, None),
        P("dp", None, None),
        P(),
        P(None, None, "tensor"),
        P(None, "tensor"),
        P("tensor"),
        P("tensor", None),
        P(None, "tensor"),
        P("tensor"),
        P(None, "tensor"),
        P("tensor"),
        P("tensor", None),
    )
    sizes = (mesh.shape["dp"], mesh.shape["tensor"])
    return jax.shard_map(functools.partial(on_device, sizes), mesh=mesh, in_specs=placed, out_specs=results, check_vma=False)
```
